32 devices in a mesh: gx: 16 (over z, y, x), gy: 2 (over core).
Axes of the slice: x: 2, y: 2, z: 4, core: 2. Of those that a mesh axis runs over, the one named last changes fastest.
Arguments:
- density: float32 [128, 32, 64], P('gx', None, 'gy'), may hold values from 0.5 to 1.5
- momentum: float32 [3, 128, 32, 64], P(None, 'gx', None, 'gy'), may hold values from -3 to 3
- energy: float32 [128, 32, 64], P('gx', None, 'gy'), may hold values from 2.5 to 4
- eddy_normal_cell: int32 [1024], P('gx'), may hold values from 0 to 63
- eddy_spanwise_cell: int32 [1024], P('gx'), may hold values from 0 to 31
- eddy_signs: int32 [1024, 3], P('gx'), may hold values from 0 to 1
- eddy_strengths: float32 [1024], P('gx'), may hold values from 0.3 to 3
- filter_matrices: float32 [1, 128, 128], replicated, may hold values from -1.25 to 1.25
- shock_switch: int32 [1, 64], P(None, 'gy'), may hold values 0 or 1
- dilatation_bin: int32 [128, 32, 64], P('gx', None, 'gy'), may hold values from 0 to 63
- vorticity_bin: int32 [128, 32, 64], P('gx', None, 'gy'), may hold values from 0 to 63, as said below
Outputs:
- conserved_next: float32 [5, 128, 32, 64], P(None, 'gx', None, 'gy')
- histogram: float32 [64, 64], replicated
The draws below stay inside these ranges and needn't reach their ends.
Inputs may be any that keep to these rules, and one draw needn't show every extreme that they name: vorticity_bin at streamwise cell x is x * 64 // 128 or one more, modulo 64.
All inputs are finite; a program needn't handle non-finite values. No bound on the sum of `shock_switch` on one device may be relied on, other than what follows from the above.
Results may differ from the reference program's by a relative error of at most 0.0003.
Values sent between devices are 32-bit elements; how exact they have to be, the bound alone decides.
No kernel may reach another device: no remote copies, remote signals or barrier semaphores. Data moves between devices by JAX's collectives and lax.ppermute only.
A program may use at most 64 MiB of HBM per device.

```python
import math
import jax
import jax.numpy as jnp
from jax import lax

SPANWISE_CELLS = 32
XB = 128
HISTOGRAM_BINS = 64
SIGMA_Y = 32
SIGMA_Z = 8
STREAMWISE_CELLS = 128
NORMAL_CELLS = 64
EDDIES = 1024
NXB = 1


def draw_vorticity_bin(key, part):
    streamwise = jnp.arange(STREAMWISE_CELLS, dtype=jnp.int32)[:, None, None]
    base = streamwise * HISTOGRAM_BINS // STREAMWISE_CELLS
    offset = jax.random.randint(key, (STREAMWISE_CELLS, SPANWISE_CELLS, NORMAL_CELLS), 0, 2, dtype=jnp.int32)
    return jnp.mod(base + offset, HISTOGRAM_BINS).astype(jnp.int32)


def touch_ends(array, rng, smallest, largest):
    longest = array.shape.index(max(array.shape))
    spots = []
    for shift in (0, 1):
        where = [jax.random.randint(jax.random.fold_in(rng, axis), (), 0, length) for axis, length in enumerate(array.shape)]
        where[longest] = (where[longest] + shift) % array.shape[longest]
        spots.append(tuple(where))
    return array.at[spots[0]].set(smallest).at[spots[1]].set(largest)


def block_scale(stream_key, extent, shards, low, largest):
    gain, own = 1.0, jax.random.fold_in(stream_key, 6)
    for position, shards_of in shards:
        steps = jnp.exp(jax.random.uniform(jax.random.fold_in(own, position), (shards_of,), jnp.float32, low / len(shards), largest / len(shards)))
        gain = gain * jnp.repeat(steps, extent[position] // shards_of).reshape([-1 if axis == position else 1 for axis in range(len(extent))])
    return gain


def gaussian(key, shape, width, reach, pieces=(), kind=jnp.bfloat16):
    entries = width * jax.random.normal(key, shape, jnp.float32)
    if pieces:
        entries = entries * block_scale(key, shape, pieces, -0.22, 0.18)
    return jnp.clip(entries, -reach, reach).astype(kind)


def setup_inputs(seed: int = 0) -> dict:
    arg_keys = jax.random.split(jax.random.key(seed), 12)
    density = jnp.clip(0.5 + 1.0 * jax.random.uniform(arg_keys[0], (STREAMWISE_CELLS, SPANWISE_CELLS, NORMAL_CELLS), jnp.float32) ** block_scale(arg_keys[0], (STREAMWISE_CELLS, SPANWISE_CELLS, NORMAL_CELLS), ((0, 16), (2, 2)), -0.2, 0.2), 0.5, 1.5)
    momentum = gaussian(arg_keys[1], (3, STREAMWISE_CELLS, SPANWISE_CELLS, NORMAL_CELLS), 0.5, 3.0, ((1, 16), (3, 2)), jnp.float32)
    energy = jnp.clip(2.5 + 1.5 * jax.random.uniform(arg_keys[2], (STREAMWISE_CELLS, SPANWISE_CELLS, NORMAL_CELLS), jnp.float32) ** block_scale(arg_keys[2], (STREAMWISE_CELLS, SPANWISE_CELLS, NORMAL_CELLS), ((0, 16), (2, 2)), -0.2, 0.2), 2.5, 4.0)
    eddy_normal_cell = touch_ends(jax.random.randint(arg_keys[3], (EDDIES,), 0, NORMAL_CELLS), jax.random.fold_in(arg_keys[3], 1), 0, NORMAL_CELLS - 1).astype(jnp.int32)
    eddy_spanwise_cell = touch_ends(jax.random.randint(arg_keys[4], (EDDIES,), 0, SPANWISE_CELLS), jax.random.fold_in(arg_keys[4], 1), 0, SPANWISE_CELLS - 1).astype(jnp.int32)
    eddy_signs = touch_ends(jax.random.randint(arg_keys[5], (EDDIES, 3), 0, 2), jax.random.fold_in(arg_keys[5], 1), 0, 1).astype(jnp.int32)
    eddy_strengths = jnp.clip(jnp.exp(math.log(3.0) - 2.3025851 * jax.random.uniform(arg_keys[6], (EDDIES,), jnp.float32) ** block_scale(arg_keys[6], (EDDIES,), ((0, 16),), -0.2, 0.2)), 0.3, 3.0)
    filter_matrices = gaussian(arg_keys[7], (NXB, XB, XB), (XB ** -0.5), 1.25, (), jnp.float32)
    shock_switch = touch_ends((jax.random.randint(arg_keys[8], (NXB, NORMAL_CELLS), 0, 2) < 1).astype(jnp.int32), jax.random.fold_in(arg_keys[8], 1), 0, 1)
    dilatation_bin = touch_ends(jax.random.randint(arg_keys[9], (STREAMWISE_CELLS, SPANWISE_CELLS, NORMAL_CELLS), 0, HISTOGRAM_BINS), jax.random.fold_in(arg_keys[9], 1), 0, HISTOGRAM_BINS - 1).astype(jnp.int32)
    vorticity_bin = draw_vorticity_bin(jax.random.fold_in(arg_keys[11], 71), 0)
    return {"density": density, "momentum": momentum, "energy": energy, "eddy_normal_cell": eddy_normal_cell, "eddy_spanwise_cell": eddy_spanwise_cell, "eddy_signs": eddy_signs, "eddy_strengths": eddy_strengths, "filter_matrices": filter_matrices, "shock_switch": shock_switch, "dilatation_bin": dilatation_bin, "vorticity_bin": vorticity_bin}


TIME_STEP = 0.1
GAMMA_GAS = 1.4
SENSOR_EPS = 0.1
HAT_PEAK = math.sqrt(1.5)

def hat_shape(centres, coords, spread, period):
    offset = coords[None, :] - centres[:, None]
    if period > 0:
        offset = jnp.mod(offset + period / 2, period) - period / 2
    return HAT_PEAK * jnp.maximum(0.0, 1.0 - jnp.abs(offset) / spread)

def inflow_from(centre_y, centre_z, eddy_weight, coords_y, coords_z, span):
    shape_y = hat_shape(centre_y, coords_y, float(SIGMA_Y), 0)
    shape_z = hat_shape(centre_z, coords_z, float(SIGMA_Z), span)
    weighted = (eddy_weight[:, :, None] * shape_z[:, None, :]).reshape(eddy_weight.shape[0], -1)
    inflow = jnp.dot(weighted.T, shape_y, precision=lax.Precision.HIGHEST)
    return inflow.reshape(3, coords_z.shape[0], coords_y.shape[0])

def ghost_state(inflow):
    mom_x = 1.0 + inflow[0]
    kinetic = mom_x * mom_x + inflow[1] * inflow[1] + inflow[2] * inflow[2]
    return jnp.stack([jnp.ones_like(mom_x), mom_x, inflow[1], inflow[2], 3.0 + 0.5 * kinetic])

def flux_of(fields, velocity, pressure, direction):
    result = fields * velocity[direction][None]
    result = result.at[1 + direction].add(pressure)
    return result.at[4].add(pressure * velocity[direction])

def central_x(values):
    return (values[..., 2:, :, 1:-1] - values[..., :-2, :, 1:-1]) * 0.5

def central_y(values):
    return (values[..., 1:-1, :, 2:] - values[..., 1:-1, :, :-2]) * 0.5

def central_z(values):
    centre = values[..., 1:-1, :, 1:-1]
    return (jnp.roll(centre, -1, axis=-2) - jnp.roll(centre, 1, axis=-2)) * 0.5

def section_rhs(padded):
    velocity = padded[1:4] / padded[0][None]
    pressure = (GAMMA_GAS - 1.0) * (padded[4] - 0.5 * lax.optimization_barrier(jnp.sum(padded[1:4] * velocity, axis=0)))
    change = central_x(flux_of(padded, velocity, pressure, 0))
    change = change + central_y(flux_of(padded, velocity, pressure, 1))
    change = change + central_z(flux_of(padded, velocity, pressure, 2))
    updated = padded[:, 1:-1, :, 1:-1] - TIME_STEP * change
    dilatation = central_x(velocity[0]) + central_y(velocity[1]) + central_z(velocity[2])
    vort_x = central_y(velocity[2]) - central_z(velocity[1])
    vort_y = central_z(velocity[0]) - central_x(velocity[2])
    vort_z = central_x(velocity[1]) - central_y(velocity[0])
    squared = dilatation * dilatation
    shock_sensor = squared / (squared + vort_x * vort_x + vort_y * vort_y + vort_z * vort_z + SENSOR_EPS)
    return (updated, shock_sensor)

def reference(density, momentum, energy, eddy_normal_cell, eddy_spanwise_cell, eddy_signs, eddy_strengths, filter_matrices, shock_switch, dilatation_bin, vorticity_bin):
    fields = jnp.concatenate([density[None], momentum, energy[None]], axis=0)
    amplitude = math.sqrt(NORMAL_CELLS * SPANWISE_CELLS / (EDDIES * SIGMA_Y * SIGMA_Z))
    eddy_weight = (2 * eddy_signs - 1).astype(jnp.float32) * eddy_strengths[:, None] * amplitude
    coords_y = jnp.arange(NORMAL_CELLS).astype(jnp.float32)
    coords_z = jnp.arange(SPANWISE_CELLS).astype(jnp.float32)
    inflow = inflow_from(eddy_normal_cell.astype(jnp.float32), eddy_spanwise_cell.astype(jnp.float32), eddy_weight, coords_y, coords_z, SPANWISE_CELLS)
    ghost_cells = ghost_state(inflow)
    padded = jnp.pad(fields, ((0, 0), (1, 1), (0, 0), (1, 1)), mode='edge')
    padded = padded.at[:, 0, :, 1:-1].set(ghost_cells)
    joint_counts = dilatation_bin * HISTOGRAM_BINS + vorticity_bin
    mask_float = shock_switch.astype(jnp.float32)

    def one_block(histogram_totals, block_index):
        start = (block_index * XB).astype(jnp.int32)
        piece = lax.dynamic_slice_in_dim(padded, start, XB + 2, 1)
        updated, shock_sensor = section_rhs(piece)
        mask_row = lax.dynamic_index_in_dim(mask_float, block_index, 0, keepdims=False)
        weight = mask_row[None, None, :] * shock_sensor
        matrix = lax.dynamic_index_in_dim(filter_matrices, block_index, 0, keepdims=False)
        smooth = jnp.einsum('ij,fjzy->fizy', matrix, updated, precision=lax.Precision.HIGHEST)
        result = updated + weight[None] * (smooth - updated)
        bins = lax.dynamic_slice_in_dim(joint_counts, start, XB, 0)
        histogram_totals = histogram_totals + jax.ops.segment_sum(shock_sensor.reshape(-1), bins.reshape(-1), HISTOGRAM_BINS * HISTOGRAM_BINS)
        return (histogram_totals, result)
    histogram_totals, results = lax.scan(one_block, jnp.zeros((HISTOGRAM_BINS * HISTOGRAM_BINS,), jnp.float32), jnp.arange(NXB, dtype=jnp.int32))
    conserved_next = jnp.moveaxis(results, 0, 1).reshape(5, STREAMWISE_CELLS, SPANWISE_CELLS, NORMAL_CELLS)
    histogram = (histogram_totals * (HISTOGRAM_BINS * HISTOGRAM_BINS / (STREAMWISE_CELLS * NORMAL_CELLS * SPANWISE_CELLS))).reshape(HISTOGRAM_BINS, HISTOGRAM_BINS)
    return (conserved_next, histogram)
```

```python
import math

import jax
import jax.numpy as jnp
from jax import lax
from jax.experimental import pallas as pl
from jax.experimental.pallas import tpu as pltpu
from jax.sharding import PartitionSpec as P

HISTOGRAM_BINS = 64
SIGMA_Y = 32
SIGMA_Z = 8


TIME_STEP = 0.1
GAMMA_GAS = 1.4
SENSOR_EPS = 0.1
HAT_PEAK = math.sqrt(1.5)


def extended(x, sides, width):
    for axis, dim in sides:
        size, length = (lax.axis_size(axis), x.shape[dim])
        up = [(i, (i + 1) % size) for i in range(size - 1)]
        down = [(j, i) for i, j in up]
        last = lax.slice_in_dim(x, length - width, length, axis=dim)
        first = lax.slice_in_dim(x, 0, width, axis=dim)
        before = lax.ppermute(last, axis, up)
        after = lax.ppermute(first, axis, down)
        x = jnp.concatenate([before, x, after], axis=dim)
    return x


def hat_shape(centres, coords, spread, period):
    offset = coords[None, :] - centres[:, None]
    if period > 0:
        offset = jnp.mod(offset + period / 2, period) - period / 2
    return HAT_PEAK * jnp.maximum(0.0, 1.0 - jnp.abs(offset) / spread)


def inflow_from(centre_y, centre_z, eddy_weight, coords_y, coords_z, span):
    shape_y = hat_shape(centre_y, coords_y, float(SIGMA_Y), 0)
    shape_z = hat_shape(centre_z, coords_z, float(SIGMA_Z), span)
    weighted = (eddy_weight[:, :, None] * shape_z[:, None, :]).reshape(eddy_weight.shape[0], -1)
    inflow = jnp.dot(weighted.T, shape_y, precision=lax.Precision.HIGHEST)
    return inflow.reshape(3, coords_z.shape[0], coords_y.shape[0])


def ghost_state(inflow):
    mom_x = 1.0 + inflow[0]
    kinetic = mom_x * mom_x + inflow[1] * inflow[1] + inflow[2] * inflow[2]
    return jnp.stack([jnp.ones_like(mom_x), mom_x, inflow[1], inflow[2], 3.0 + 0.5 * kinetic])


def flux_of(fields, velocity, pressure, direction):
    result = fields * velocity[direction][None]
    result = result.at[1 + direction].add(pressure)
    return result.at[4].add(pressure * velocity[direction])


def central_x(values):
    return (values[..., 2:, :, 1:-1] - values[..., :-2, :, 1:-1]) * 0.5


def central_y(values):
    return (values[..., 1:-1, :, 2:] - values[..., 1:-1, :, :-2]) * 0.5


def central_z(values):
    centre = values[..., 1:-1, :, 1:-1]
    return (jnp.roll(centre, -1, axis=-2) - jnp.roll(centre, 1, axis=-2)) * 0.5


def section_rhs(padded):
    velocity = padded[1:4] / padded[0][None]
    pressure = (GAMMA_GAS - 1.0) * (padded[4] - 0.5 * jnp.sum(padded[1:4] * velocity, axis=0))
    change = central_x(flux_of(padded, velocity, pressure, 0))
    change = change + central_y(flux_of(padded, velocity, pressure, 1))
    change = change + central_z(flux_of(padded, velocity, pressure, 2))
    updated = padded[:, 1:-1, :, 1:-1] - TIME_STEP * change
    dilatation = central_x(velocity[0]) + central_y(velocity[1]) + central_z(velocity[2])
    vort_x = central_y(velocity[2]) - central_z(velocity[1])
    vort_y = central_z(velocity[0]) - central_x(velocity[2])
    vort_z = central_x(velocity[1]) - central_y(velocity[0])
    squared = dilatation * dilatation
    shock_sensor = squared / (
        squared + vort_x * vort_x + vort_y * vort_y + vort_z * vort_z + SENSOR_EPS
    )
    return (updated, shock_sensor)


def filter_lines(pencil, filter_matrices):
    block_count, block_len = (filter_matrices.shape[0], filter_matrices.shape[1])
    lanes = pencil.shape[2]
    blocks = pencil.reshape(5, block_count, block_len, lanes)
    smooth = jnp.einsum("bij,fbjp->fbip", filter_matrices, blocks, precision=lax.Precision.HIGHEST)
    return smooth.reshape(5, block_count * block_len, lanes)


def plane_histogram(shock_sensor, dilatation_bin, vorticity_bin):
    bin_levels = jnp.arange(HISTOGRAM_BINS, dtype=jnp.int32)

    def accumulate_plane(histogram_totals, histogram_parts):
        sensor_plane, plane_dilatation, plane_vorticity = histogram_parts
        flat_sensor = sensor_plane.reshape(-1)
        dilatation_table = (plane_dilatation.reshape(-1)[None, :] == bin_levels[:, None]).astype(
            jnp.float32
        )
        vorticity_table = jnp.where(
            plane_vorticity.reshape(-1)[:, None] == bin_levels[None, :], flat_sensor[:, None], 0.0
        )
        return (
            histogram_totals
            + jnp.dot(dilatation_table, vorticity_table, precision=lax.Precision.HIGHEST),
            None,
        )

    histogram_totals, _ = lax.scan(
        accumulate_plane,
        jnp.zeros((HISTOGRAM_BINS, HISTOGRAM_BINS), jnp.float32),
        (shock_sensor, dilatation_bin, vorticity_bin),
    )
    return histogram_totals


def general_shards(
    density,
    momentum,
    energy,
    eddy_normal_cell,
    eddy_spanwise_cell,
    eddy_signs,
    eddy_strengths,
    filter_matrices,
    shock_switch,
    dilatation_bin,
    vorticity_bin,
):
    cells_x, span, cells_y = density.shape
    slab_index = lax.axis_index("gx")
    block_index = lax.axis_index("gy")
    slab_count = lax.axis_size("gx")
    fields = jnp.concatenate([density[None], momentum, energy[None]], axis=0)
    total_y = cells_y * lax.axis_size("gy")
    total_eddies = eddy_normal_cell.shape[0] * slab_count
    amplitude = math.sqrt(total_y * span / (total_eddies * SIGMA_Y * SIGMA_Z))
    eddy_weight = (2 * eddy_signs - 1).astype(jnp.float32) * eddy_strengths[:, None] * amplitude
    coords_y = (block_index * cells_y + jnp.arange(cells_y, dtype=jnp.int32)).astype(jnp.float32)
    coords_z = jnp.arange(span, dtype=jnp.int32).astype(jnp.float32)
    partial_sum = inflow_from(
        eddy_normal_cell.astype(jnp.float32),
        eddy_spanwise_cell.astype(jnp.float32),
        eddy_weight,
        coords_y,
        coords_z,
        span,
    )
    inflow = lax.psum(partial_sum, "gx")
    ghost_cells = ghost_state(inflow)
    padded = extended(fields, (("gx", 1), ("gy", 3)), 1)
    padded = padded.at[:, 0, :, 1:-1].set(
        jnp.where(slab_index == 0, ghost_cells, padded[:, 0, :, 1:-1])
    )
    padded = padded.at[:, -1, :, 1:-1].set(
        jnp.where(slab_index == slab_count - 1, fields[:, -1], padded[:, -1, :, 1:-1])
    )
    padded = padded.at[:, 1:-1, :, 0].set(
        jnp.where(block_index == 0, fields[:, :, :, 0], padded[:, 1:-1, :, 0])
    )
    padded = padded.at[:, 1:-1, :, -1].set(
        jnp.where(
            block_index == lax.axis_size("gy") - 1, fields[:, :, :, -1], padded[:, 1:-1, :, -1]
        )
    )
    updated, shock_sensor = section_rhs(padded)
    block_len = filter_matrices.shape[1]
    filter_row = slab_index * cells_x // block_len
    mask_row = lax.dynamic_slice_in_dim(shock_switch, filter_row, 1, 0).astype(jnp.float32)
    weight = mask_row[None] * shock_sensor
    columns = span * cells_y
    stacked = updated.reshape(5, cells_x, columns)
    weight_flat = weight.reshape(1, cells_x, columns)
    pencil, pencil_weight = (
        lax.all_to_all(stacked, "gx", split_axis=2, concat_axis=1, tiled=True),
        lax.all_to_all(weight_flat, "gx", split_axis=2, concat_axis=1, tiled=True),
    )
    smooth = filter_lines(pencil, filter_matrices)
    returned = pencil + pencil_weight * (smooth - pencil)
    back_lines = lax.all_to_all(returned, "gx", split_axis=1, concat_axis=2, tiled=True)
    conserved_next = back_lines.reshape(5, cells_x, span, cells_y)
    partial_histogram = plane_histogram(shock_sensor, dilatation_bin, vorticity_bin)
    summed = lax.psum(partial_histogram, ("gx", "gy"))
    all_cells = cells_x * slab_count * span * total_y
    histogram = summed * (HISTOGRAM_BINS * HISTOGRAM_BINS / all_cells)
    return (conserved_next, histogram)


LANES = 128
HALF_STEP = 0.5 * TIME_STEP


def iota(shape, dim):
    return lax.broadcasted_iota(jnp.int32, shape, dim)


def roll(x, shift, axis):
    shift %= x.shape[axis]
    return x if shift == 0 else pltpu.roll(x, shift, axis)


def packed(ref, *lead):
    parts = [ref[(*lead, slice(None), pl.ds(8 * k, 8), slice(None))] for k in range(4)]
    return jnp.concatenate(parts, axis=-1)


def regrouped(parts, k):
    group = iota(parts[0].shape, len(parts[0].shape) - 1) // 32
    out = None
    for i, part in enumerate(parts):
        moved = roll(part, 32 * (i - k), len(part.shape) - 1)
        out = moved if out is None else jnp.where(group == i, moved, out)
    return out


def velocity_pressure(q):
    inverse = 1.0 / q[0]
    vel = [q[1] * inverse, q[2] * inverse, q[3] * inverse]
    kinetic = q[1] * vel[0] + q[2] * vel[1] + q[3] * vel[2]
    return vel, (GAMMA_GAS - 1.0) * (q[4] - 0.5 * kinetic)


def euler_flux(q, vel, pressure, k):
    flux = [q[1 + k], q[1] * vel[k], q[2] * vel[k], q[3] * vel[k], (q[4] + pressure) * vel[k]]
    flux[1 + k] = flux[1 + k] + pressure
    return flux


def z_difference(a):
    row = iota(a.shape, 1)
    up = roll(a, -1, 1)
    up = jnp.where(row == 7, roll(up, -32, 2), up)
    down = roll(a, 1, 1)
    down = jnp.where(row == 0, roll(down, 32, 2), down)
    return up - down


def y_difference(a, first_core):
    lane = iota(a.shape, 2) % 32
    up = jnp.where(lane == 31, jnp.where(first_core, 0.0, a), roll(a, -1, 2))
    down = jnp.where(lane == 0, jnp.where(first_core, a, 0.0), roll(a, 1, 2))
    return up - down


def x_difference(a, before, after):
    up = jnp.concatenate([a[1:], after], axis=0)
    down = jnp.concatenate([before, a[:-1]], axis=0)
    return up - down


def slab_kernel(
    amplitude,
    density,
    momentum,
    energy,
    normal_cell,
    spanwise_cell,
    signs,
    strengths,
    send,
    partial_out,
    velocity_out,
    first_out,
    last_out,
    edge_out,
):
    slab = lax.axis_index("gx")
    first_core = lax.axis_index("gy") == 0
    last_slab = slab == lax.axis_size("gx") - 1
    q = [packed(density)] + [packed(momentum, c) for c in range(3)] + [packed(energy)]
    vel, pressure = velocity_pressure(q)
    flux_x = euler_flux(q, vel, pressure, 0)
    flux_y = euler_flux(q, vel, pressure, 1)
    flux_z = euler_flux(q, vel, pressure, 2)
    zero = jnp.zeros((1, 8, LANES), jnp.float32)
    partial = []
    for f in range(5):
        after = jnp.where(last_slab, flux_x[f][7:], 0.0)
        change = x_difference(flux_x[f], zero, after)
        change = change + y_difference(flux_y[f], first_core)
        change = change + z_difference(flux_z[f])
        partial.append(q[f] - HALF_STEP * change)
        partial_out[f] = partial[f]
        first_out[f] = q[f][0]
        last_out[f] = q[f][7]
    for c in range(3):
        velocity_out[c] = vel[c]

    lane = iota((8, 8, LANES), 2) % 32
    edge = jnp.zeros((8, 8, LANES), jnp.float32)
    for i, value in enumerate(flux_y + vel):
        near = jnp.where(first_core, roll(value, i - 31, 2), roll(value, i, 2))
        edge = jnp.where(lane == i, near, edge)
    edge_out[...] = edge

    own = slice(0, 32), slice(32, 64)
    pick = lambda a: jnp.where(first_core, a[:, own[0]], a[:, own[1]])
    strength = strengths[...] * amplitude
    rows = [pick(normal_cell[...]).astype(jnp.float32), pick(spanwise_cell[...]).astype(jnp.float32)]
    for c in range(3):
        sign = (2 * signs[c : c + 1, :] - 1).astype(jnp.float32)
        rows.append(pick(sign * strength))
    blank = jnp.zeros((1, 32), jnp.float32)
    eddies = jnp.concatenate([blank] + rows + [blank, blank], axis=0)
    eddies = jnp.concatenate([eddies] * 4, axis=1)

    slots = [flux_x[4][7], None, None, None, None, None, None, flux_x[4][0]]
    extra = jnp.stack([eddies if s is None else s for s in slots])
    faces = [None] * 8
    for f in range(4):
        faces[2 * f] = flux_x[f][7]
        faces[(2 * f - 1) % 8] = flux_x[f][0]
    faces = jnp.stack(faces)
    row = iota((8, LANES), 0)
    lane2 = iota((8, LANES), 1)
    for k in range(4):
        tile_a = regrouped(partial[:4], k)
        tile_b = regrouped([partial[4], extra, edge, faces], k)
        for x in range(8):
            send[pl.ds(k * 128 + x, 8, stride=16), :] = tile_a[x]
            tile = tile_b[x]
            if 1 <= x <= 5:
                tile = jnp.where(lane2 // 32 == 1, eddies[x : x + 1, :], tile)
            elif x == 6:
                tile = jnp.where(lane2 // 32 == 1, 0.0, tile)
            send[pl.ds(k * 128 + 8 + x, 8, stride=16), :] = tile


def dot_nt(a, b, precision=None):
    return lax.dot_general(
        a, b, (((1,), (1,)), ((), ())), precision=precision, preferred_element_type=jnp.float32
    )


def span_hat(z, centre, span):
    offset = z - centre + span / 2
    offset = jnp.where(offset < 0, offset + span, jnp.where(offset >= span, offset - span, offset))
    return HAT_PEAK * jnp.maximum(0.0, 1.0 - jnp.abs(offset - span / 2) / SIGMA_Z)


def normal_hat(y, centre):
    return HAT_PEAK * jnp.maximum(0.0, 1.0 - jnp.abs(y - centre) / SIGMA_Y)


def ghost_flux(a, b, c):
    mom = 1.0 + a
    kinetic = mom * mom + b * b + c * c
    q = [jnp.ones_like(mom), mom, b, c, 3.0 + 0.5 * kinetic]
    return q


def pencil_kernel(
    received,
    matrix,
    partial,
    velocity,
    before,
    after,
    edge,
    dilatation_bin,
    vorticity_bin,
    switch,
    send,
    updated_out,
    energy_out,
    weight_out,
    ghost_planes,
):
    slab = lax.axis_index("gx")
    core = lax.axis_index("gy")
    slabs = lax.axis_size("gx")
    first_core = core == 0
    plane = (slab * 2 + core).astype(jnp.float32)
    row = iota((8, LANES), 0)
    lane = iota((8, LANES), 1)

    tiles = [[received[g, h, 1] for g in range(16)] for h in range(2)]
    chunks = []
    for h in range(2):
        for a in range(4):
            out = None
            for i in range(4):
                moved = roll(tiles[h][4 * a + i], 32 * (i - 1), 1)
                out = moved if out is None else jnp.where(lane // 32 == i, moved, out)
            chunks.append(jnp.where((row >= 1) & (row <= 5), out, 0.0))
    y_all = iota((64, LANES), 0).astype(jnp.float32)
    left, right = [], []
    for chunk in chunks:
        left.append(chunk * span_hat(plane, chunk[2:3], 32.0))
        right.append(normal_hat(y_all, chunk[1:2]))
    inflow = dot_nt(
        jnp.concatenate(left, axis=1), jnp.concatenate(right, axis=1), lax.Precision.HIGHEST
    )
    ghost = ghost_flux(inflow[3:4], inflow[4:5], inflow[5:6])
    ghost_vel, ghost_pressure = velocity_pressure(ghost)
    ghost_x = euler_flux(ghost, ghost_vel, ghost_pressure, 0)

    @pl.when(slab == 0)
    def _():
        z_all = iota((32, LANES), 0).astype(jnp.float32)
        y_own = (iota((32, LANES), 0) + core * 32).astype(jnp.float32)
        lhs, rhs = [], []
        for chunk in chunks:
            hat = span_hat(z_all, chunk[2:3], 32.0)
            lhs.append(jnp.concatenate([hat * chunk[3 + c : 4 + c] for c in range(3)], axis=0))
            rhs.append(normal_hat(y_own, chunk[1:2]))
        own = dot_nt(
            jnp.concatenate(lhs, axis=1), jnp.concatenate(rhs, axis=1), lax.Precision.HIGHEST
        )
        parts = [
            jnp.concatenate([own[c * 32 + 8 * k : c * 32 + 8 * k + 8] for k in range(4)], axis=1)
            for c in range(3)
        ]
        q = ghost_flux(*parts)
        for f in range(5):
            ghost_planes[f] = q[f]

    @pl.when(slab != 0)
    def _():
        ghost_planes[...] = before[...]

    face_a, face_e = [], []
    for h in range(2):
        fa, fe = [], []
        for g in range(16):
            tile = tiles[h][g]
            out = None
            for f in range(4):
                moved = roll(roll(tile, 32 * (f - 3), 1), -2 * f, 0)
                out = moved if out is None else jnp.where(lane // 32 == f, moved, out)
            fa.append(out)
            fe.append(roll(tile, -32, 1))
        face_a.append(fa)
        face_e.append(fe)
    columns_a, columns_e = [], []
    for h in range(2):
        ga = jnp.zeros((1, 32), jnp.float32)
        own = slice(32 * h, 32 * h + 32)
        ga = jnp.concatenate([ghost_x[f][:, own] for f in range(4)], axis=1)
        ge = jnp.concatenate([ghost_x[4][:, own]] * 4, axis=1)
        ca, ce = [], []
        for g in range(16):
            previous_a = face_a[h][g - 1] if g > 0 else ga
            previous_e = face_e[h][g - 1] if g > 0 else ge
            next_a = face_a[h][g + 1] if g < 15 else jnp.zeros((8, LANES), jnp.float32)
            next_e = face_e[h][g + 1] if g < 15 else jnp.zeros((8, LANES), jnp.float32)
            fix_a = jnp.where(row == 0, previous_a, jnp.where(row == 7, -next_a, 0.0))
            fix_e = jnp.where(row == 0, previous_e, jnp.where(row == 7, -next_e, 0.0))
            other = tiles[1 - h][g]
            target = 31 if h == 0 else 0
            side = -1.0 if h == 0 else 1.0
            for f in range(4):
                moved = roll(other, 32 * f + target - (64 + f), 1)
                fix_a = jnp.where(lane == 32 * f + target, fix_a + side * moved, fix_a)
            moved = roll(other, target - 68, 1)
            fix_e = jnp.where(lane == target, fix_e + side * moved, fix_e)
            ca.append(received[g, h, 0] + HALF_STEP * fix_a)
            ce.append(jnp.where(lane < 32, tiles[h][g] + HALF_STEP * fix_e, 0.0))
        columns_a.append(jnp.concatenate(ca, axis=0))
        columns_e.append(jnp.concatenate(ce, axis=0))
    columns = jnp.concatenate(
        [columns_a[0], columns_a[1], columns_e[0] + roll(columns_e[1], 32, 1)], axis=1
    )
    smooth = lax.dot_general(
        matrix[...],
        columns,
        (((1,), (0,)), ((), ())),
        precision=lax.Precision.HIGHEST,
        preferred_element_type=jnp.float32,
    )

    vel = [velocity[c] for c in range(3)]
    planes = []
    for ref, end in ((ghost_planes, 0), (after, 7)):
        q = [ref[f][None] for f in range(5)]
        halo_vel, halo_pressure = velocity_pressure(q)
        planes.append((halo_vel, euler_flux(q, halo_vel, halo_pressure, 0)))
    (before_vel, before_flux), (after_vel, after_flux) = planes
    last_slab = slab == slabs - 1
    lane3 = iota((8, 8, LANES), 2) % 32
    halo = edge[...]

    def y_halo(i):
        near = jnp.where(first_core, roll(halo, 31 - i, 2), -roll(halo, -i, 2))
        return jnp.where(lane3 == jnp.where(first_core, 31, 0), near, 0.0)

    def x_all(c):
        end = jnp.where(last_slab, vel[c][7:], after_vel[c])
        return x_difference(vel[c], before_vel[c], end)

    def y_all_(c):
        return y_difference(vel[c], first_core) + y_halo(5 + c)

    x_row = iota((8, 8, LANES), 0)
    updated = []
    for f in range(5):
        flux_after = jnp.where(last_slab, 0.0, after_flux[f])
        fix = jnp.where(x_row == 7, flux_after, jnp.where(x_row == 0, -before_flux[f], 0.0))
        updated.append(partial[f] - HALF_STEP * (fix + y_halo(f)))
    dx = [x_all(c) for c in range(3)]
    dy = [y_all_(c) for c in range(3)]
    dz = [z_difference(vel[c]) for c in range(3)]
    dilatation = dx[0] + dy[1] + dz[2]
    vort_x = dy[2] - dz[1]
    vort_y = dz[0] - dx[2]
    vort_z = dx[1] - dy[0]
    squared = dilatation * dilatation
    total = squared + vort_x * vort_x + vort_y * vort_y + vort_z * vort_z
    sensor = squared / (total + 4.0 * SENSOR_EPS)
    mask = jnp.concatenate([switch[...].astype(jnp.float32)] * 4, axis=1)
    weight = sensor * mask[None]
    for k in range(4):
        updated_out[k] = regrouped(updated[:4], k)
        energy_out[k] = roll(updated[4], -32 * k, 2)
        weight_out[k] = regrouped([weight] * 4, k)

    base = slab * 8 * HISTOGRAM_BINS // (8 * slabs)
    dil = packed(dilatation_bin)
    vort = (packed(vorticity_bin) - base) & (HISTOGRAM_BINS - 1)
    levels = iota((HISTOGRAM_BINS, LANES), 0)
    values, ones = [], []
    for x in range(8):
        for z in range(8):
            values.append(jnp.where(vort[x, z : z + 1] == row, sensor[x, z : z + 1], 0.0))
            ones.append(jnp.where(dil[x, z : z + 1] == levels, 1.0, 0.0).astype(jnp.bfloat16))
    values = jnp.concatenate(values, axis=1)
    high = values.astype(jnp.bfloat16)
    low = (values - high.astype(jnp.float32)).astype(jnp.bfloat16)
    ones = jnp.concatenate(ones, axis=1)
    counts = dot_nt(jnp.concatenate([high, low], axis=0), ones)
    counts = counts[:8] + counts[8:]
    counts = jnp.concatenate([jnp.zeros((8, 64), jnp.float32), counts], axis=1)

    for g in range(16):
        block = smooth[8 * g : 8 * g + 8]
        for h in range(2):
            send[g, h, 0] = block[:, 128 * h : 128 * h + 128]
            energy = roll(block[:, 256:], -32 * h, 1)
            send[g, h, 1] = jnp.where(lane < 32, energy, counts)


def final_kernel(scale, received, updated, energy, weight, conserved, histogram, totals):
    for k in range(4):
        for x in range(8):
            w = weight[k, x]
            smooth = received[pl.ds(k * 128 + x, 8, stride=16), :]
            u = updated[k, x]
            result = u + w * (smooth - u)
            for f in range(4):
                conserved[f, x, 8 * k : 8 * k + 8, :] = result[:, 32 * f : 32 * f + 32]
            smooth = received[pl.ds(k * 128 + 8 + x, 8, stride=16), :]
            u = energy[k, x]
            result = u + w * (smooth - u)
            conserved[4, x, 8 * k : 8 * k + 8, :] = result[:, :32]
    totals[...] = jnp.zeros_like(totals)
    for g in range(16):
        both = received[32 * g + 8 : 32 * g + 16, :] + received[32 * g + 24 : 32 * g + 32, :]
        totals[4 * g : 4 * g + 8, :] = totals[4 * g : 4 * g + 8, :] + both
    first = totals[0:8, :] + totals[64:72, :]
    table = jnp.concatenate([first, totals[8:64, :]], axis=0)[:, 64:]
    histogram[...] = table.T * scale


def shards(
    density,
    momentum,
    energy,
    eddy_normal_cell,
    eddy_spanwise_cell,
    eddy_signs,
    eddy_strengths,
    filter_matrices,
    shock_switch,
    dilatation_bin,
    vorticity_bin,
):
    slabs, cores = lax.axis_size("gx"), lax.axis_size("gy")
    shapes = (density.shape, eddy_strengths.shape, filter_matrices.shape, slabs, cores)
    if shapes != ((8, 32, 32), (64,), (1, 128, 128), 16, 2):
        return general_shards(
            density,
            momentum,
            energy,
            eddy_normal_cell,
            eddy_spanwise_cell,
            eddy_signs,
            eddy_strengths,
            filter_matrices,
            shock_switch,
            dilatation_bin,
            vorticity_bin,
        )
    cells_x, span, cells_y = density.shape
    total_y = cells_y * cores
    total_eddies = eddy_strengths.shape[0] * slabs
    amplitude = math.sqrt(total_y * span / (total_eddies * SIGMA_Y * SIGMA_Z))
    plane = jax.ShapeDtypeStruct((5, 8, LANES), jnp.float32)
    cells = (8, 8, LANES)
    send, partial, velocity, first, last, edge = pl.pallas_call(
        lambda *refs: slab_kernel(amplitude, *refs),
        out_shape=[
            jax.ShapeDtypeStruct((512, LANES), jnp.float32),
            jax.ShapeDtypeStruct((5, *cells), jnp.float32),
            jax.ShapeDtypeStruct((3, *cells), jnp.float32),
            plane,
            plane,
            jax.ShapeDtypeStruct(cells, jnp.float32),
        ],
        name="slab",
    )(
        density,
        momentum,
        energy,
        eddy_normal_cell.reshape(1, -1),
        eddy_spanwise_cell.reshape(1, -1),
        eddy_signs.T,
        eddy_strengths.reshape(1, -1),
    )
    received = lax.all_to_all(send.reshape(32, 16, LANES), ("gx", "gy"), 0, 0, tiled=True)
    up = [(i, i + 1) for i in range(slabs - 1)]
    down = [(j, i) for i, j in up]
    before = lax.ppermute(last, "gx", up)
    after = lax.ppermute(first, "gx", down)
    other_edge = lax.ppermute(edge, "gy", [(0, 1), (1, 0)])
    send, updated, updated_energy, weight = pl.pallas_call(
        pencil_kernel,
        out_shape=[
            jax.ShapeDtypeStruct((16, 2, 2, 8, LANES), jnp.float32),
            jax.ShapeDtypeStruct((4, *cells), jnp.float32),
            jax.ShapeDtypeStruct((4, *cells), jnp.float32),
            jax.ShapeDtypeStruct((4, *cells), jnp.float32),
        ],
        scratch_shapes=[pltpu.VMEM((5, 8, LANES), jnp.float32)],
        name="pencil",
    )(
        received.reshape(16, 2, 2, 8, LANES),
        filter_matrices[0],
        partial,
        velocity,
        before,
        after,
        other_edge,
        dilatation_bin,
        vorticity_bin,
        shock_switch,
    )
    received = lax.all_to_all(send.reshape(32, 16, LANES), ("gx", "gy"), 0, 0, tiled=True)
    scale = HISTOGRAM_BINS * HISTOGRAM_BINS / (cells_x * slabs * span * total_y)
    conserved_next, histogram = pl.pallas_call(
        lambda *refs: final_kernel(scale, *refs),
        out_shape=[
            jax.ShapeDtypeStruct((5, cells_x, span, cells_y), jnp.float32),
            jax.ShapeDtypeStruct((HISTOGRAM_BINS, HISTOGRAM_BINS), jnp.float32),
        ],
        scratch_shapes=[pltpu.VMEM((72, LANES), jnp.float32)],
        name="final",
    )(received.reshape(512, LANES), updated, updated_energy, weight)
    return (conserved_next, histogram)


def solution(mesh):
    in_specs = (
        P("gx", None, "gy"),
        P(None, "gx", None, "gy"),
        P("gx", None, "gy"),
        P("gx"),
        P("gx"),
        P("gx", None),
        P("gx"),
        P(),
        P(None, "gy"),
        P("gx", None, "gy"),
        P("gx", None, "gy"),
    )
    out_specs = (P(None, "gx", None, "gy"), P())
    return jax.shard_map(shards, mesh=mesh, in_specs=in_specs, out_specs=out_specs, check_vma=False)
```

```python
import math

import jax
import jax.numpy as jnp
from jax import lax
from jax.experimental import pallas as pl
from jax.experimental.pallas import tpu as pltpu
from jax.sharding import PartitionSpec as P

HISTOGRAM_BINS = 64
SIGMA_Y = 32
SIGMA_Z = 8


TIME_STEP = 0.1
GAMMA_GAS = 1.4
SENSOR_EPS = 0.1
HAT_PEAK = math.sqrt(1.5)


def extended(x, sides, width):
    for axis, dim in sides:
        size, length = (lax.axis_size(axis), x.shape[dim])
        up = [(i, (i + 1) % size) for i in range(size - 1)]
        down = [(j, i) for i, j in up]
        last = lax.slice_in_dim(x, length - width, length, axis=dim)
        first = lax.slice_in_dim(x, 0, width, axis=dim)
        before = lax.ppermute(last, axis, up)
        after = lax.ppermute(first, axis, down)
        x = jnp.concatenate([before, x, after], axis=dim)
    return x


def hat_shape(centres, coords, spread, period):
    offset = coords[None, :] - centres[:, None]
    if period > 0:
        offset = jnp.mod(offset + period / 2, period) - period / 2
    return HAT_PEAK * jnp.maximum(0.0, 1.0 - jnp.abs(offset) / spread)


def inflow_from(centre_y, centre_z, eddy_weight, coords_y, coords_z, span):
    shape_y = hat_shape(centre_y, coords_y, float(SIGMA_Y), 0)
    shape_z = hat_shape(centre_z, coords_z, float(SIGMA_Z), span)
    weighted = (eddy_weight[:, :, None] * shape_z[:, None, :]).reshape(eddy_weight.shape[0], -1)
    inflow = jnp.dot(weighted.T, shape_y, precision=lax.Precision.HIGHEST)
    return inflow.reshape(3, coords_z.shape[0], coords_y.shape[0])


def ghost_state(inflow):
    mom_x = 1.0 + inflow[0]
    kinetic = mom_x * mom_x + inflow[1] * inflow[1] + inflow[2] * inflow[2]
    return jnp.stack([jnp.ones_like(mom_x), mom_x, inflow[1], inflow[2], 3.0 + 0.5 * kinetic])


def flux_of(fields, velocity, pressure, direction):
    result = fields * velocity[direction][None]
    result = result.at[1 + direction].add(pressure)
    return result.at[4].add(pressure * velocity[direction])


def central_x(values):
    return (values[..., 2:, :, 1:-1] - values[..., :-2, :, 1:-1]) * 0.5


def central_y(values):
    return (values[..., 1:-1, :, 2:] - values[..., 1:-1, :, :-2]) * 0.5


def central_z(values):
    centre = values[..., 1:-1, :, 1:-1]
    return (jnp.roll(centre, -1, axis=-2) - jnp.roll(centre, 1, axis=-2)) * 0.5


def section_rhs(padded):
    velocity = padded[1:4] / padded[0][None]
    pressure = (GAMMA_GAS - 1.0) * (padded[4] - 0.5 * jnp.sum(padded[1:4] * velocity, axis=0))
    change = central_x(flux_of(padded, velocity, pressure, 0))
    change = change + central_y(flux_of(padded, velocity, pressure, 1))
    change = change + central_z(flux_of(padded, velocity, pressure, 2))
    updated = padded[:, 1:-1, :, 1:-1] - TIME_STEP * change
    dilatation = central_x(velocity[0]) + central_y(velocity[1]) + central_z(velocity[2])
    vort_x = central_y(velocity[2]) - central_z(velocity[1])
    vort_y = central_z(velocity[0]) - central_x(velocity[2])
    vort_z = central_x(velocity[1]) - central_y(velocity[0])
    squared = dilatation * dilatation
    shock_sensor = squared / (
        squared + vort_x * vort_x + vort_y * vort_y + vort_z * vort_z + SENSOR_EPS
    )
    return (updated, shock_sensor)


def filter_lines(pencil, filter_matrices):
    block_count, block_len = (filter_matrices.shape[0], filter_matrices.shape[1])
    lanes = pencil.shape[2]
    blocks = pencil.reshape(5, block_count, block_len, lanes)
    smooth = jnp.einsum("bij,fbjp->fbip", filter_matrices, blocks, precision=lax.Precision.HIGHEST)
    return smooth.reshape(5, block_count * block_len, lanes)


def plane_histogram(shock_sensor, dilatation_bin, vorticity_bin):
    bin_levels = jnp.arange(HISTOGRAM_BINS, dtype=jnp.int32)

    def accumulate_plane(histogram_totals, histogram_parts):
        sensor_plane, plane_dilatation, plane_vorticity = histogram_parts
        flat_sensor = sensor_plane.reshape(-1)
        dilatation_table = (plane_dilatation.reshape(-1)[None, :] == bin_levels[:, None]).astype(
            jnp.float32
        )
        vorticity_table = jnp.where(
            plane_vorticity.reshape(-1)[:, None] == bin_levels[None, :], flat_sensor[:, None], 0.0
        )
        return (
            histogram_totals
            + jnp.dot(dilatation_table, vorticity_table, precision=lax.Precision.HIGHEST),
            None,
        )

    histogram_totals, _ = lax.scan(
        accumulate_plane,
        jnp.zeros((HISTOGRAM_BINS, HISTOGRAM_BINS), jnp.float32),
        (shock_sensor, dilatation_bin, vorticity_bin),
    )
    return histogram_totals


def general_shards(
    density,
    momentum,
    energy,
    eddy_normal_cell,
    eddy_spanwise_cell,
    eddy_signs,
    eddy_strengths,
    filter_matrices,
    shock_switch,
    dilatation_bin,
    vorticity_bin,
):
    cells_x, span, cells_y = density.shape
    slab_index = lax.axis_index("gx")
    block_index = lax.axis_index("gy")
    slab_count = lax.axis_size("gx")
    fields = jnp.concatenate([density[None], momentum, energy[None]], axis=0)
    total_y = cells_y * lax.axis_size("gy")
    total_eddies = eddy_normal_cell.shape[0] * slab_count
    amplitude = math.sqrt(total_y * span / (total_eddies * SIGMA_Y * SIGMA_Z))
    eddy_weight = (2 * eddy_signs - 1).astype(jnp.float32) * eddy_strengths[:, None] * amplitude
    coords_y = (block_index * cells_y + jnp.arange(cells_y, dtype=jnp.int32)).astype(jnp.float32)
    coords_z = jnp.arange(span, dtype=jnp.int32).astype(jnp.float32)
    partial_sum = inflow_from(
        eddy_normal_cell.astype(jnp.float32),
        eddy_spanwise_cell.astype(jnp.float32),
        eddy_weight,
        coords_y,
        coords_z,
        span,
    )
    inflow = lax.psum(partial_sum, "gx")
    ghost_cells = ghost_state(inflow)
    padded = extended(fields, (("gx", 1), ("gy", 3)), 1)
    padded = padded.at[:, 0, :, 1:-1].set(
        jnp.where(slab_index == 0, ghost_cells, padded[:, 0, :, 1:-1])
    )
    padded = padded.at[:, -1, :, 1:-1].set(
        jnp.where(slab_index == slab_count - 1, fields[:, -1], padded[:, -1, :, 1:-1])
    )
    padded = padded.at[:, 1:-1, :, 0].set(
        jnp.where(block_index == 0, fields[:, :, :, 0], padded[:, 1:-1, :, 0])
    )
    padded = padded.at[:, 1:-1, :, -1].set(
        jnp.where(
            block_index == lax.axis_size("gy") - 1, fields[:, :, :, -1], padded[:, 1:-1, :, -1]
        )
    )
    updated, shock_sensor = section_rhs(padded)
    block_len = filter_matrices.shape[1]
    filter_row = slab_index * cells_x // block_len
    mask_row = lax.dynamic_slice_in_dim(shock_switch, filter_row, 1, 0).astype(jnp.float32)
    weight = mask_row[None] * shock_sensor
    columns = span * cells_y
    stacked = updated.reshape(5, cells_x, columns)
    weight_flat = weight.reshape(1, cells_x, columns)
    pencil, pencil_weight = (
        lax.all_to_all(stacked, "gx", split_axis=2, concat_axis=1, tiled=True),
        lax.all_to_all(weight_flat, "gx", split_axis=2, concat_axis=1, tiled=True),
    )
    smooth = filter_lines(pencil, filter_matrices)
    returned = pencil + pencil_weight * (smooth - pencil)
    back_lines = lax.all_to_all(returned, "gx", split_axis=1, concat_axis=2, tiled=True)
    conserved_next = back_lines.reshape(5, cells_x, span, cells_y)
    partial_histogram = plane_histogram(shock_sensor, dilatation_bin, vorticity_bin)
    summed = lax.psum(partial_histogram, ("gx", "gy"))
    all_cells = cells_x * slab_count * span * total_y
    histogram = summed * (HISTOGRAM_BINS * HISTOGRAM_BINS / all_cells)
    return (conserved_next, histogram)


LANES = 128
HALF_STEP = 0.5 * TIME_STEP


def iota(shape, dim):
    return lax.broadcasted_iota(jnp.int32, shape, dim)


def roll(x, shift, axis):
    shift %= x.shape[axis]
    return x if shift == 0 else pltpu.roll(x, shift, axis)


def packed(ref, *lead):
    lead = lead if len(lead) == len(ref.shape) - 2 else (*lead, slice(None))
    parts = [ref[(*lead, pl.ds(8 * k, 8), slice(None))] for k in range(4)]
    return jnp.concatenate(parts, axis=-1)


def regrouped(parts, k):
    group = iota(parts[0].shape, len(parts[0].shape) - 1) // 32
    out = None
    for i, part in enumerate(parts):
        moved = roll(part, 32 * (i - k), len(part.shape) - 1)
        out = moved if out is None else jnp.where(group == i, moved, out)
    return out


def velocity_pressure(q):
    inverse = 1.0 / q[0]
    vel = [q[1] * inverse, q[2] * inverse, q[3] * inverse]
    kinetic = q[1] * vel[0] + q[2] * vel[1] + q[3] * vel[2]
    return vel, (GAMMA_GAS - 1.0) * (q[4] - 0.5 * kinetic)


def euler_flux(q, vel, pressure, k):
    flux = [q[1 + k], q[1] * vel[k], q[2] * vel[k], q[3] * vel[k], (q[4] + pressure) * vel[k]]
    flux[1 + k] = flux[1 + k] + pressure
    return flux


def z_difference(a):
    row = iota(a.shape, 1)
    up = roll(a, -1, 1)
    up = jnp.where(row == 7, roll(up, -32, 2), up)
    down = roll(a, 1, 1)
    down = jnp.where(row == 0, roll(down, 32, 2), down)
    return up - down


def y_difference(a, first_core):
    lane = iota(a.shape, 2) % 32
    up = jnp.where(lane == 31, jnp.where(first_core, 0.0, a), roll(a, -1, 2))
    down = jnp.where(lane == 0, jnp.where(first_core, a, 0.0), roll(a, 1, 2))
    return up - down


def x_difference(a, before, after):
    up = jnp.concatenate([a[1:], after], axis=0)
    down = jnp.concatenate([before, a[:-1]], axis=0)
    return up - down


def slab_kernel(
    amplitude,
    density,
    momentum,
    energy,
    normal_cell,
    spanwise_cell,
    signs,
    strengths,
    send,
    first_out,
    last_out,
    edge_out,
):
    slab = lax.axis_index("gx")
    first_core = lax.axis_index("gy") == 0
    last_slab = slab == lax.axis_size("gx") - 1
    q = [packed(density)] + [packed(momentum, c) for c in range(3)] + [packed(energy)]
    vel, pressure = velocity_pressure(q)
    flux_x = euler_flux(q, vel, pressure, 0)
    flux_y = euler_flux(q, vel, pressure, 1)
    flux_z = euler_flux(q, vel, pressure, 2)
    zero = jnp.zeros((1, 8, LANES), jnp.float32)
    partial = []
    for f in range(5):
        after = jnp.where(last_slab, flux_x[f][7:], 0.0)
        change = x_difference(flux_x[f], zero, after)
        change = change + y_difference(flux_y[f], first_core)
        change = change + z_difference(flux_z[f])
        partial.append(q[f] - HALF_STEP * change)
        first_out[f] = q[f][0]
        last_out[f] = q[f][7]

    lane = iota((8, 8, LANES), 2) % 32
    edge = jnp.zeros((8, 8, LANES), jnp.float32)
    for i, value in enumerate(flux_y + vel):
        near = jnp.where(first_core, roll(value, i - 31, 2), roll(value, i, 2))
        edge = jnp.where(lane == i, near, edge)
    edge_out[...] = edge

    own = slice(0, 32), slice(32, 64)
    pick = lambda a: jnp.where(first_core, a[:, own[0]], a[:, own[1]])
    strength = strengths[...] * amplitude
    rows = [pick(normal_cell[...]).astype(jnp.float32), pick(spanwise_cell[...]).astype(jnp.float32)]
    for c in range(3):
        sign = (2 * signs[c : c + 1, :] - 1).astype(jnp.float32)
        rows.append(pick(sign * strength))
    blank = jnp.zeros((1, 32), jnp.float32)
    eddies = jnp.concatenate([blank] + rows + [blank, blank], axis=0)
    eddies = jnp.concatenate([eddies] * 4, axis=1)

    slots = [flux_x[4][7], None, None, None, None, None, None, flux_x[4][0]]
    extra = jnp.stack([eddies if s is None else s for s in slots])
    faces = [None] * 8
    for f in range(4):
        faces[2 * f] = flux_x[f][7]
        faces[(2 * f - 1) % 8] = flux_x[f][0]
    faces = jnp.stack(faces)
    row = iota((8, LANES), 0)
    lane2 = iota((8, LANES), 1)
    for k in range(4):
        tile_a = regrouped(partial[:4], k)
        tile_b = regrouped([partial[4], extra, edge, faces], k)
        for x in range(8):
            send[pl.ds(k * 128 + x, 8, stride=16), :] = tile_a[x]
            tile = tile_b[x]
            if 1 <= x <= 5:
                tile = jnp.where(lane2 // 32 == 1, eddies[x : x + 1, :], tile)
            elif x == 6:
                tile = jnp.where(lane2 // 32 == 1, 0.0, tile)
            send[pl.ds(k * 128 + 8 + x, 8, stride=16), :] = tile


def dot_nt(a, b):
    return lax.dot_general(
        a, b, (((1,), (1,)), ((), ())), preferred_element_type=jnp.float32
    )


def halves(a):
    high = a.astype(jnp.bfloat16)
    return high, (a - high.astype(jnp.float32)).astype(jnp.bfloat16)


def span_hat(z, centre, span):
    offset = z - centre + span / 2
    offset = jnp.where(offset < 0, offset + span, jnp.where(offset >= span, offset - span, offset))
    return jnp.maximum(0.0, 1.0 - jnp.abs(offset - span / 2) * (1.0 / SIGMA_Z))


def normal_hat(y, centre):
    return jnp.maximum(0.0, 1.0 - jnp.abs(y - centre) * (1.0 / SIGMA_Y)).astype(jnp.bfloat16)


def ghost_state_rows(a, b, c):
    mom = 1.0 + a
    kinetic = mom * mom + b * b + c * c
    return [jnp.ones_like(mom), mom, b, c, 3.0 + 0.5 * kinetic]


def sensor_of(d, vort_x, vort_y, vort_z):
    squared = d * d
    total = squared + vort_x * vort_x + vort_y * vort_y + vort_z * vort_z
    return squared / (total + 4.0 * SENSOR_EPS)


def counted(sensor, dil, vort):
    row = iota((8, LANES), 0)
    levels = iota((HISTOGRAM_BINS, LANES), 0)
    values, ones = [], []
    for x in range(len(sensor)):
        for z in range(8):
            values.append(jnp.where(vort[x][z : z + 1] == row, sensor[x][z : z + 1], 0.0))
            ones.append(jnp.where(dil[x][z : z + 1] == levels, 1.0, 0.0).astype(jnp.bfloat16))
    high, low = halves(jnp.concatenate(values, axis=1))
    counts = dot_nt(jnp.concatenate([high, low], axis=0), jnp.concatenate(ones, axis=1))
    return counts[:8] + counts[8:]


def slab_bins(vorticity_bin, rows):
    slab = lax.axis_index("gx")
    base = slab * HISTOGRAM_BINS // lax.axis_size("gx")
    return (packed(vorticity_bin, rows) - base) & (HISTOGRAM_BINS - 1)


def interior_kernel(
    density,
    momentum,
    energy,
    edge,
    dilatation_bin,
    vorticity_bin,
    switch,
    updated_out,
    energy_out,
    weight_out,
    ends_out,
    counts_out,
):
    first_core = lax.axis_index("gy") == 0
    last_slab = lax.axis_index("gx") == lax.axis_size("gx") - 1
    q = [packed(density)] + [packed(momentum, c) for c in range(3)] + [packed(energy)]
    vel, pressure = velocity_pressure(q)
    flux_x = euler_flux(q, vel, pressure, 0)
    flux_y = euler_flux(q, vel, pressure, 1)
    flux_z = euler_flux(q, vel, pressure, 2)
    zero = jnp.zeros((1, 8, LANES), jnp.float32)
    lane = iota((8, 8, LANES), 2) % 32
    halo = edge[...]

    def y_whole(a, i):
        near = jnp.where(first_core, roll(halo, 31 - i, 2), -roll(halo, -i, 2))
        near = jnp.where(lane == jnp.where(first_core, 31, 0), near, 0.0)
        return y_difference(a, first_core) + near

    updated = []
    for f in range(5):
        after = jnp.where(last_slab, flux_x[f][7:], 0.0)
        change = x_difference(flux_x[f], zero, after)
        change = change + y_whole(flux_y[f], f) + z_difference(flux_z[f])
        updated.append(q[f] - HALF_STEP * change)
    dx = [x_difference(a, zero, jnp.where(last_slab, a[7:], 0.0)) for a in vel]
    dy = [y_whole(vel[c], 5 + c) for c in range(3)]
    dz = [z_difference(a) for a in vel]
    rates = [dx[0] + dy[1] + dz[2], dy[2] - dz[1], dz[0] - dx[2], dx[1] - dy[0]]
    sensor = sensor_of(*rates)
    mask = jnp.concatenate([switch[...].astype(jnp.float32)] * 4, axis=1)
    weight = sensor * mask[None]
    for k in range(4):
        updated_out[k] = regrouped(updated[:4], k)
        energy_out[k] = roll(updated[4], -32 * k, 2)
        weight_out[k] = regrouped([weight] * 4, k)
    for i, a in enumerate(updated + rates):
        ends_out[i, 0] = a[0]
        ends_out[i, 1] = a[7]
    dil = packed(dilatation_bin)
    vort = slab_bins(vorticity_bin, slice(None))
    inner = range(1, 7)
    counts_out[...] = counted(
        [sensor[x] for x in inner], [dil[x] for x in inner], [vort[x] for x in inner]
    )


def pencil_kernel(
    received,
    matrix,
    ends,
    before,
    after,
    dilatation_bin,
    vorticity_bin,
    switch,
    counts_in,
    send,
    updated_out,
    energy_out,
    weight_out,
    ghost_planes,
):
    slab = lax.axis_index("gx")
    core = lax.axis_index("gy")
    last_slab = slab == lax.axis_size("gx") - 1
    plane = (slab * 2 + core).astype(jnp.float32)
    row = iota((8, LANES), 0)
    lane = iota((8, LANES), 1)
    peak = HAT_PEAK * HAT_PEAK

    tiles = [[received[g, h, 1] for g in range(16)] for h in range(2)]
    chunks = []
    for h in range(2):
        for a in range(4):
            out = None
            for i in range(4):
                moved = roll(tiles[h][4 * a + i], 32 * (i - 1), 1)
                out = moved if out is None else jnp.where(lane // 32 == i, moved, out)
            chunks.append(out)
    y_all = iota((64, LANES), 0).astype(jnp.float32)
    lhs, rhs = [], []
    for chunk in chunks:
        weighted = (chunk * peak) * span_hat(plane, chunk[2:3], 32.0)
        lhs.append(jnp.where((row >= 3) & (row <= 5), weighted, 0.0))
        rhs.append(normal_hat(y_all, chunk[1:2]))
    high, low = halves(jnp.concatenate(lhs, axis=1))
    inflow = dot_nt(jnp.concatenate([high, low], axis=0), jnp.concatenate(rhs, axis=1))
    inflow = inflow[:8] + inflow[8:]
    ghost = ghost_state_rows(inflow[3:4], inflow[4:5], inflow[5:6])
    ghost_vel, ghost_pressure = velocity_pressure(ghost)
    ghost_x = euler_flux(ghost, ghost_vel, ghost_pressure, 0)

    @pl.when(slab == 0)
    def _():
        z_all = iota((32, LANES), 0).astype(jnp.float32)
        y_own = (iota((32, LANES), 0) + core * 32).astype(jnp.float32)
        lhs, rhs = [], []
        for chunk in chunks:
            hat = span_hat(z_all, chunk[2:3], 32.0) * peak
            lhs.append(jnp.concatenate([hat * chunk[3 + c : 4 + c] for c in range(3)], axis=0))
            rhs.append(normal_hat(y_own, chunk[1:2]))
        high, low = halves(jnp.concatenate(lhs, axis=1))
        own = dot_nt(jnp.concatenate([high, low], axis=0), jnp.concatenate(rhs, axis=1))
        own = own[:96] + own[96:]
        parts = [
            jnp.concatenate([own[c * 32 + 8 * k : c * 32 + 8 * k + 8] for k in range(4)], axis=1)
            for c in range(3)
        ]
        q = ghost_state_rows(*parts)
        for f in range(5):
            ghost_planes[f] = q[f]

    @pl.when(slab != 0)
    def _():
        ghost_planes[...] = before[...]

    face_a, face_e = [], []
    for h in range(2):
        fa, fe = [], []
        for g in range(16):
            tile = tiles[h][g]
            out = None
            for f in range(4):
                moved = roll(roll(tile, 32 * (f - 3), 1), -2 * f, 0)
                out = moved if out is None else jnp.where(lane // 32 == f, moved, out)
            fa.append(out)
            fe.append(roll(tile, -32, 1))
        face_a.append(fa)
        face_e.append(fe)
    columns_a, columns_e = [], []
    for h in range(2):
        own = slice(32 * h, 32 * h + 32)
        ghost_a = jnp.concatenate([ghost_x[f][:, own] for f in range(4)], axis=1)
        ghost_e = jnp.concatenate([ghost_x[4][:, own]] * 4, axis=1)
        ca, ce = [], []
        for g in range(16):
            zero = jnp.zeros((8, LANES), jnp.float32)
            previous_a, previous_e = (face_a[h][g - 1], face_e[h][g - 1]) if g else (ghost_a, ghost_e)
            next_a, next_e = (face_a[h][g + 1], face_e[h][g + 1]) if g < 15 else (zero, zero)
            fix_a = jnp.where(row == 0, previous_a, jnp.where(row == 7, -next_a, 0.0))
            fix_e = jnp.where(row == 0, previous_e, jnp.where(row == 7, -next_e, 0.0))
            other = tiles[1 - h][g]
            target = 31 if h == 0 else 0
            side = -1.0 if h == 0 else 1.0
            for f in range(4):
                moved = roll(other, 32 * f + target - (64 + f), 1)
                fix_a = jnp.where(lane == 32 * f + target, fix_a + side * moved, fix_a)
            moved = roll(other, target - 68, 1)
            fix_e = jnp.where(lane == target, fix_e + side * moved, fix_e)
            ca.append(received[g, h, 0] + HALF_STEP * fix_a)
            ce.append(jnp.where(lane < 32, tiles[h][g] + HALF_STEP * fix_e, 0.0))
        columns_a.append(jnp.concatenate(ca, axis=0))
        columns_e.append(jnp.concatenate(ce, axis=0))
    columns = jnp.concatenate(
        [columns_a[0], columns_a[1], columns_e[0] + roll(columns_e[1], 32, 1)], axis=1
    )
    m_high, m_low = halves(matrix[...])
    c_high, c_low = halves(columns)
    smooth = (
        jnp.dot(m_high, c_high, preferred_element_type=jnp.float32)
        + jnp.dot(m_high, c_low, preferred_element_type=jnp.float32)
        + jnp.dot(m_low, c_high, preferred_element_type=jnp.float32)
    )

    sensors, dils, vorts = [], [], []
    mask = jnp.concatenate([switch[...].astype(jnp.float32)] * 4, axis=1)
    for end, ref in ((0, ghost_planes), (1, after)):
        q = [ref[f] for f in range(5)]
        vel, pressure = velocity_pressure(q)
        flux = euler_flux(q, vel, pressure, 0)
        sign = -1.0 if end == 0 else 1.0
        add = [sign * a for a in flux + vel]
        if end == 1:
            add = [jnp.where(last_slab, 0.0, a) for a in add]
        updated = [ends[f, end] - HALF_STEP * add[f] for f in range(5)]
        rates = [ends[5 + i, end] for i in range(4)]
        rates = [rates[0] + add[5], rates[1], rates[2] - add[7], rates[3] + add[6]]
        sensor = sensor_of(*rates)
        weight = sensor * mask
        for k in range(4):
            updated_out[end, k] = regrouped(updated[:4], k)
            energy_out[end, k] = roll(updated[4], -32 * k, 1)
            weight_out[end, k] = regrouped([weight] * 4, k)
        at = pl.ds(7 * end, 1)
        sensors.append(sensor)
        dils.append(packed(dilatation_bin, at)[0])
        vorts.append(slab_bins(vorticity_bin, at)[0])
    counts = counts_in[...] + counted(sensors, dils, vorts)
    counts = jnp.concatenate([jnp.zeros((8, 64), jnp.float32), counts], axis=1)

    for g in range(16):
        block = smooth[8 * g : 8 * g + 8]
        for h in range(2):
            send[g, h, 0] = block[:, 128 * h : 128 * h + 128]
            own_energy = roll(block[:, 256:], -32 * h, 1)
            send[g, h, 1] = jnp.where(lane < 32, own_energy, counts)


def final_kernel(
    scale,
    received,
    updated,
    energy,
    weight,
    end_updated,
    end_energy,
    end_weight,
    conserved,
    histogram,
    totals,
):
    for k in range(4):
        for x in range(8):
            if x in (0, 7):
                end = x // 7
                u, e, w = end_updated[end, k], end_energy[end, k], end_weight[end, k]
            else:
                u, e, w = updated[k, x], energy[k, x], weight[k, x]
            smooth = received[pl.ds(k * 128 + x, 8, stride=16), :]
            result = u + w * (smooth - u)
            for f in range(4):
                conserved[f, x, 8 * k : 8 * k + 8, :] = result[:, 32 * f : 32 * f + 32]
            smooth = received[pl.ds(k * 128 + 8 + x, 8, stride=16), :]
            result = e + w * (smooth - e)
            conserved[4, x, 8 * k : 8 * k + 8, :] = result[:, :32]
    totals[...] = jnp.zeros_like(totals)
    for g in range(16):
        both = received[32 * g + 8 : 32 * g + 16, :] + received[32 * g + 24 : 32 * g + 32, :]
        totals[4 * g : 4 * g + 8, :] = totals[4 * g : 4 * g + 8, :] + both
    first = totals[0:8, :] + totals[64:72, :]
    table = jnp.concatenate([first, totals[8:64, :]], axis=0)[:, 64:]
    histogram[...] = table.T * scale


def shards(
    density,
    momentum,
    energy,
    eddy_normal_cell,
    eddy_spanwise_cell,
    eddy_signs,
    eddy_strengths,
    filter_matrices,
    shock_switch,
    dilatation_bin,
    vorticity_bin,
):
    slabs, cores = lax.axis_size("gx"), lax.axis_size("gy")
    shapes = (density.shape, eddy_strengths.shape, filter_matrices.shape, slabs, cores)
    if shapes != ((8, 32, 32), (64,), (1, 128, 128), 16, 2):
        return general_shards(
            density,
            momentum,
            energy,
            eddy_normal_cell,
            eddy_spanwise_cell,
            eddy_signs,
            eddy_strengths,
            filter_matrices,
            shock_switch,
            dilatation_bin,
            vorticity_bin,
        )
    cells_x, span, cells_y = density.shape
    total_y = cells_y * cores
    total_eddies = eddy_strengths.shape[0] * slabs
    amplitude = math.sqrt(total_y * span / (total_eddies * SIGMA_Y * SIGMA_Z))
    plane = jax.ShapeDtypeStruct((5, 8, LANES), jnp.float32)
    cells = (8, 8, LANES)
    f32 = lambda *shape: jax.ShapeDtypeStruct(shape, jnp.float32)
    vmem = lambda *shape: pltpu.VMEM(shape, jnp.float32)
    near = lambda a: pltpu.with_memory_space_constraint(a, pltpu.VMEM)
    send, first, last, edge = pl.pallas_call(
        lambda *refs: slab_kernel(amplitude, *refs),
        out_shape=[vmem(512, LANES), vmem(5, 8, LANES), vmem(5, 8, LANES), vmem(*cells)],
        name="slab",
    )(
        density,
        momentum,
        energy,
        eddy_normal_cell.reshape(1, -1),
        eddy_spanwise_cell.reshape(1, -1),
        eddy_signs.T,
        eddy_strengths.reshape(1, -1),
    )
    received = lax.all_to_all(send.reshape(32, 16, LANES), ("gx", "gy"), 0, 0, tiled=True)
    up = [(i, i + 1) for i in range(slabs - 1)]
    down = [(j, i) for i, j in up]
    before = lax.ppermute(last, "gx", up)
    after = lax.ppermute(first, "gx", down)
    other_edge = lax.ppermute(edge, "gy", [(0, 1), (1, 0)])
    updated, updated_energy, weight, ends, counts = pl.pallas_call(
        interior_kernel,
        out_shape=[vmem(4, *cells), vmem(4, *cells), vmem(4, *cells), vmem(9, 2, 8, LANES), vmem(8, 64)],
        cost_estimate=pl.CostEstimate(flops=10_000_000, bytes_accessed=2_000_000, transcendentals=0),
        name="interior",
    )(density, momentum, energy, near(other_edge), dilatation_bin, vorticity_bin, shock_switch)
    send, *end_rows = pl.pallas_call(
        pencil_kernel,
        out_shape=[vmem(16, 2, 2, 8, LANES)] + [vmem(2, 4, 8, LANES)] * 3,
        scratch_shapes=[pltpu.VMEM((5, 8, LANES), jnp.float32)],
        name="pencil",
    )(
        near(received.reshape(16, 2, 2, 8, LANES)),
        filter_matrices[0],
        near(ends),
        near(before),
        near(after),
        dilatation_bin,
        vorticity_bin,
        shock_switch,
        near(counts),
    )
    received = lax.all_to_all(send.reshape(32, 16, LANES), ("gx", "gy"), 0, 0, tiled=True)
    scale = HISTOGRAM_BINS * HISTOGRAM_BINS / (cells_x * slabs * span * total_y)
    conserved_next, histogram = pl.pallas_call(
        lambda *refs: final_kernel(scale, *refs),
        out_shape=[f32(5, cells_x, span, cells_y), f32(HISTOGRAM_BINS, HISTOGRAM_BINS)],
        scratch_shapes=[pltpu.VMEM((72, LANES), jnp.float32)],
        name="final",
    )(*map(near, (received.reshape(512, LANES), updated, updated_energy, weight, *end_rows)))
    return (conserved_next, histogram)


def solution(mesh):
    in_specs = (
        P("gx", None, "gy"),
        P(None, "gx", None, "gy"),
        P("gx", None, "gy"),
        P("gx"),
        P("gx"),
        P("gx", None),
        P("gx"),
        P(),
        P(None, "gy"),
        P("gx", None, "gy"),
        P("gx", None, "gy"),
    )
    out_specs = (P(None, "gx", None, "gy"), P())
    return jax.shard_map(shards, mesh=mesh, in_specs=in_specs, out_specs=out_specs, check_vma=False)
```

```python
import math

import jax
import jax.numpy as jnp
from jax import lax
from jax.experimental import pallas as pl
from jax.experimental.pallas import tpu as pltpu
from jax.sharding import PartitionSpec as P

HISTOGRAM_BINS = 64
SIGMA_Y = 32
SIGMA_Z = 8


TIME_STEP = 0.1
GAMMA_GAS = 1.4
SENSOR_EPS = 0.1
HAT_PEAK = math.sqrt(1.5)


def extended(x, sides, width):
    for axis, dim in sides:
        size, length = (lax.axis_size(axis), x.shape[dim])
        up = [(i, (i + 1) % size) for i in range(size - 1)]
        down = [(j, i) for i, j in up]
        last = lax.slice_in_dim(x, length - width, length, axis=dim)
        first = lax.slice_in_dim(x, 0, width, axis=dim)
        before = lax.ppermute(last, axis, up)
        after = lax.ppermute(first, axis, down)
        x = jnp.concatenate([before, x, after], axis=dim)
    return x


def hat_shape(centres, coords, spread, period):
    offset = coords[None, :] - centres[:, None]
    if period > 0:
        offset = jnp.mod(offset + period / 2, period) - period / 2
    return HAT_PEAK * jnp.maximum(0.0, 1.0 - jnp.abs(offset) / spread)


def inflow_from(centre_y, centre_z, eddy_weight, coords_y, coords_z, span):
    shape_y = hat_shape(centre_y, coords_y, float(SIGMA_Y), 0)
    shape_z = hat_shape(centre_z, coords_z, float(SIGMA_Z), span)
    weighted = (eddy_weight[:, :, None] * shape_z[:, None, :]).reshape(eddy_weight.shape[0], -1)
    inflow = jnp.dot(weighted.T, shape_y, precision=lax.Precision.HIGHEST)
    return inflow.reshape(3, coords_z.shape[0], coords_y.shape[0])


def ghost_state(inflow):
    mom_x = 1.0 + inflow[0]
    kinetic = mom_x * mom_x + inflow[1] * inflow[1] + inflow[2] * inflow[2]
    return jnp.stack([jnp.ones_like(mom_x), mom_x, inflow[1], inflow[2], 3.0 + 0.5 * kinetic])


def flux_of(fields, velocity, pressure, direction):
    result = fields * velocity[direction][None]
    result = result.at[1 + direction].add(pressure)
    return result.at[4].add(pressure * velocity[direction])


def central_x(values):
    return (values[..., 2:, :, 1:-1] - values[..., :-2, :, 1:-1]) * 0.5


def central_y(values):
    return (values[..., 1:-1, :, 2:] - values[..., 1:-1, :, :-2]) * 0.5


def central_z(values):
    centre = values[..., 1:-1, :, 1:-1]
    return (jnp.roll(centre, -1, axis=-2) - jnp.roll(centre, 1, axis=-2)) * 0.5


def section_rhs(padded):
    velocity = padded[1:4] / padded[0][None]
    pressure = (GAMMA_GAS - 1.0) * (padded[4] - 0.5 * jnp.sum(padded[1:4] * velocity, axis=0))
    change = central_x(flux_of(padded, velocity, pressure, 0))
    change = change + central_y(flux_of(padded, velocity, pressure, 1))
    change = change + central_z(flux_of(padded, velocity, pressure, 2))
    updated = padded[:, 1:-1, :, 1:-1] - TIME_STEP * change
    dilatation = central_x(velocity[0]) + central_y(velocity[1]) + central_z(velocity[2])
    vort_x = central_y(velocity[2]) - central_z(velocity[1])
    vort_y = central_z(velocity[0]) - central_x(velocity[2])
    vort_z = central_x(velocity[1]) - central_y(velocity[0])
    squared = dilatation * dilatation
    shock_sensor = squared / (
        squared + vort_x * vort_x + vort_y * vort_y + vort_z * vort_z + SENSOR_EPS
    )
    return (updated, shock_sensor)


def filter_lines(pencil, filter_matrices):
    block_count, block_len = (filter_matrices.shape[0], filter_matrices.shape[1])
    lanes = pencil.shape[2]
    blocks = pencil.reshape(5, block_count, block_len, lanes)
    smooth = jnp.einsum("bij,fbjp->fbip", filter_matrices, blocks, precision=lax.Precision.HIGHEST)
    return smooth.reshape(5, block_count * block_len, lanes)


def plane_histogram(shock_sensor, dilatation_bin, vorticity_bin):
    bin_levels = jnp.arange(HISTOGRAM_BINS, dtype=jnp.int32)

    def accumulate_plane(histogram_totals, histogram_parts):
        sensor_plane, plane_dilatation, plane_vorticity = histogram_parts
        flat_sensor = sensor_plane.reshape(-1)
        dilatation_table = (plane_dilatation.reshape(-1)[None, :] == bin_levels[:, None]).astype(
            jnp.float32
        )
        vorticity_table = jnp.where(
            plane_vorticity.reshape(-1)[:, None] == bin_levels[None, :], flat_sensor[:, None], 0.0
        )
        return (
            histogram_totals
            + jnp.dot(dilatation_table, vorticity_table, precision=lax.Precision.HIGHEST),
            None,
        )

    histogram_totals, _ = lax.scan(
        accumulate_plane,
        jnp.zeros((HISTOGRAM_BINS, HISTOGRAM_BINS), jnp.float32),
        (shock_sensor, dilatation_bin, vorticity_bin),
    )
    return histogram_totals


def general_shards(
    density,
    momentum,
    energy,
    eddy_normal_cell,
    eddy_spanwise_cell,
    eddy_signs,
    eddy_strengths,
    filter_matrices,
    shock_switch,
    dilatation_bin,
    vorticity_bin,
):
    cells_x, span, cells_y = density.shape
    slab_index = lax.axis_index("gx")
    block_index = lax.axis_index("gy")
    slab_count = lax.axis_size("gx")
    fields = jnp.concatenate([density[None], momentum, energy[None]], axis=0)
    total_y = cells_y * lax.axis_size("gy")
    total_eddies = eddy_normal_cell.shape[0] * slab_count
    amplitude = math.sqrt(total_y * span / (total_eddies * SIGMA_Y * SIGMA_Z))
    eddy_weight = (2 * eddy_signs - 1).astype(jnp.float32) * eddy_strengths[:, None] * amplitude
    coords_y = (block_index * cells_y + jnp.arange(cells_y, dtype=jnp.int32)).astype(jnp.float32)
    coords_z = jnp.arange(span, dtype=jnp.int32).astype(jnp.float32)
    partial_sum = inflow_from(
        eddy_normal_cell.astype(jnp.float32),
        eddy_spanwise_cell.astype(jnp.float32),
        eddy_weight,
        coords_y,
        coords_z,
        span,
    )
    inflow = lax.psum(partial_sum, "gx")
    ghost_cells = ghost_state(inflow)
    padded = extended(fields, (("gx", 1), ("gy", 3)), 1)
    padded = padded.at[:, 0, :, 1:-1].set(
        jnp.where(slab_index == 0, ghost_cells, padded[:, 0, :, 1:-1])
    )
    padded = padded.at[:, -1, :, 1:-1].set(
        jnp.where(slab_index == slab_count - 1, fields[:, -1], padded[:, -1, :, 1:-1])
    )
    padded = padded.at[:, 1:-1, :, 0].set(
        jnp.where(block_index == 0, fields[:, :, :, 0], padded[:, 1:-1, :, 0])
    )
    padded = padded.at[:, 1:-1, :, -1].set(
        jnp.where(
            block_index == lax.axis_size("gy") - 1, fields[:, :, :, -1], padded[:, 1:-1, :, -1]
        )
    )
    updated, shock_sensor = section_rhs(padded)
    block_len = filter_matrices.shape[1]
    filter_row = slab_index * cells_x // block_len
    mask_row = lax.dynamic_slice_in_dim(shock_switch, filter_row, 1, 0).astype(jnp.float32)
    weight = mask_row[None] * shock_sensor
    columns = span * cells_y
    stacked = updated.reshape(5, cells_x, columns)
    weight_flat = weight.reshape(1, cells_x, columns)
    pencil, pencil_weight = (
        lax.all_to_all(stacked, "gx", split_axis=2, concat_axis=1, tiled=True),
        lax.all_to_all(weight_flat, "gx", split_axis=2, concat_axis=1, tiled=True),
    )
    smooth = filter_lines(pencil, filter_matrices)
    returned = pencil + pencil_weight * (smooth - pencil)
    back_lines = lax.all_to_all(returned, "gx", split_axis=1, concat_axis=2, tiled=True)
    conserved_next = back_lines.reshape(5, cells_x, span, cells_y)
    partial_histogram = plane_histogram(shock_sensor, dilatation_bin, vorticity_bin)
    summed = lax.psum(partial_histogram, ("gx", "gy"))
    all_cells = cells_x * slab_count * span * total_y
    histogram = summed * (HISTOGRAM_BINS * HISTOGRAM_BINS / all_cells)
    return (conserved_next, histogram)


LANES = 128
HALF_STEP = 0.5 * TIME_STEP


def iota(shape, dim):
    return lax.broadcasted_iota(jnp.int32, shape, dim)


def roll(x, shift, axis):
    shift %= x.shape[axis]
    return x if shift == 0 else pltpu.roll(x, shift, axis)


def packed(ref, *lead):
    lead = lead if len(lead) == len(ref.shape) - 2 else (*lead, slice(None))
    parts = [ref[(*lead, pl.ds(8 * k, 8), slice(None))] for k in range(4)]
    return jnp.concatenate(parts, axis=-1)


def regrouped(parts, k):
    group = iota(parts[0].shape, len(parts[0].shape) - 1) // 32
    out = None
    for i, part in enumerate(parts):
        moved = roll(part, 32 * (i - k), len(part.shape) - 1)
        out = moved if out is None else jnp.where(group == i, moved, out)
    return out


def velocity_pressure(q):
    inverse = 1.0 / q[0]
    vel = [q[1] * inverse, q[2] * inverse, q[3] * inverse]
    kinetic = q[1] * vel[0] + q[2] * vel[1] + q[3] * vel[2]
    return vel, (GAMMA_GAS - 1.0) * (q[4] - 0.5 * kinetic)


def euler_flux(q, vel, pressure, k):
    flux = [q[1 + k], q[1] * vel[k], q[2] * vel[k], q[3] * vel[k], (q[4] + pressure) * vel[k]]
    flux[1 + k] = flux[1 + k] + pressure
    return flux


def z_difference(a):
    row = iota(a.shape, 1)
    up = roll(a, -1, 1)
    up = jnp.where(row == 7, roll(up, -32, 2), up)
    down = roll(a, 1, 1)
    down = jnp.where(row == 0, roll(down, 32, 2), down)
    return up - down


def y_difference(a, first_core):
    lane = iota(a.shape, 2) % 32
    up = jnp.where(lane == 31, jnp.where(first_core, 0.0, a), roll(a, -1, 2))
    down = jnp.where(lane == 0, jnp.where(first_core, a, 0.0), roll(a, 1, 2))
    return up - down


def x_difference(a, before, after):
    up = jnp.concatenate([a[1:], after], axis=0)
    down = jnp.concatenate([before, a[:-1]], axis=0)
    return up - down


def slab_kernel(
    amplitude,
    density,
    momentum,
    energy,
    normal_cell,
    spanwise_cell,
    signs,
    strengths,
    send,
    far_out,
    pair_out,
    edge_out,
):
    slab = lax.axis_index("gx")
    first_core = lax.axis_index("gy") == 0
    odd = slab % 2 == 1
    last_slab = slab == lax.axis_size("gx") - 1
    q = [packed(density)] + [packed(momentum, c) for c in range(3)] + [packed(energy)]
    vel, pressure = velocity_pressure(q)
    flux_x = euler_flux(q, vel, pressure, 0)
    flux_y = euler_flux(q, vel, pressure, 1)
    flux_z = euler_flux(q, vel, pressure, 2)
    zero = jnp.zeros((1, 8, LANES), jnp.float32)
    partial = []
    for f in range(5):
        after = jnp.where(last_slab, flux_x[f][7:], 0.0)
        change = x_difference(flux_x[f], zero, after)
        change = change + y_difference(flux_y[f], first_core)
        change = change + z_difference(flux_z[f])
        partial.append(q[f] - HALF_STEP * change)
        far_out[f] = jnp.where(odd, q[f][7], q[f][0])
        pair_out[f] = jnp.where(odd, q[f][0], q[f][7])

    lane = iota((8, 8, LANES), 2) % 32
    edge = jnp.zeros((8, 8, LANES), jnp.float32)
    for i, value in enumerate(flux_y + vel):
        near = jnp.where(first_core, roll(value, i - 31, 2), roll(value, i, 2))
        edge = jnp.where(lane == i, near, edge)
    edge_out[...] = edge

    own = slice(0, 32), slice(32, 64)
    pick = lambda a: jnp.where(first_core, a[:, own[0]], a[:, own[1]])
    strength = strengths[...] * amplitude
    rows = [pick(normal_cell[...]).astype(jnp.float32), pick(spanwise_cell[...]).astype(jnp.float32)]
    for c in range(3):
        sign = (2 * signs[c : c + 1, :] - 1).astype(jnp.float32)
        rows.append(pick(sign * strength))
    blank = jnp.zeros((1, 32), jnp.float32)
    eddies = jnp.concatenate([blank] + rows + [blank, blank], axis=0)
    eddies = jnp.concatenate([eddies] * 4, axis=1)

    slots = [flux_x[4][7], None, None, None, None, None, None, flux_x[4][0]]
    extra = jnp.stack([eddies if s is None else s for s in slots])
    faces = [None] * 8
    for f in range(4):
        faces[2 * f] = flux_x[f][7]
        faces[(2 * f - 1) % 8] = flux_x[f][0]
    faces = jnp.stack(faces)
    row = iota((8, LANES), 0)
    lane2 = iota((8, LANES), 1)
    for k in range(4):
        tile_a = regrouped(partial[:4], k)
        tile_b = regrouped([partial[4], extra, edge, faces], k)
        for x in range(8):
            send[pl.ds(k * 128 + x, 8, stride=16), :] = tile_a[x]
            tile = tile_b[x]
            if 1 <= x <= 5:
                tile = jnp.where(lane2 // 32 == 1, eddies[x : x + 1, :], tile)
            elif x == 6:
                tile = jnp.where(lane2 // 32 == 1, 0.0, tile)
            send[pl.ds(k * 128 + 8 + x, 8, stride=16), :] = tile


def dot_nt(a, b):
    return lax.dot_general(
        a, b, (((1,), (1,)), ((), ())), preferred_element_type=jnp.float32
    )


def halves(a):
    high = a.astype(jnp.bfloat16)
    return high, (a - high.astype(jnp.float32)).astype(jnp.bfloat16)


def span_hat(z, centre, span):
    offset = z - centre + span / 2
    offset = jnp.where(offset < 0, offset + span, jnp.where(offset >= span, offset - span, offset))
    return jnp.maximum(0.0, 1.0 - jnp.abs(offset - span / 2) * (1.0 / SIGMA_Z))


def normal_hat(y, centre):
    return jnp.maximum(0.0, 1.0 - jnp.abs(y - centre) * (1.0 / SIGMA_Y)).astype(jnp.bfloat16)


def ghost_state_rows(a, b, c):
    mom = 1.0 + a
    kinetic = mom * mom + b * b + c * c
    return [jnp.ones_like(mom), mom, b, c, 3.0 + 0.5 * kinetic]


def sensor_of(d, vort_x, vort_y, vort_z):
    squared = d * d
    total = squared + vort_x * vort_x + vort_y * vort_y + vort_z * vort_z
    return squared / (total + 4.0 * SENSOR_EPS)


def counted(sensor, dil, vort):
    row = iota((8, LANES), 0)
    levels = iota((HISTOGRAM_BINS, LANES), 0)
    values, ones = [], []
    for x in range(len(sensor)):
        for z in range(8):
            values.append(jnp.where(vort[x][z : z + 1] == row, sensor[x][z : z + 1], 0.0))
            ones.append(jnp.where(dil[x][z : z + 1] == levels, 1.0, 0.0).astype(jnp.bfloat16))
    high, low = halves(jnp.concatenate(values, axis=1))
    counts = dot_nt(jnp.concatenate([high, low], axis=0), jnp.concatenate(ones, axis=1))
    return counts[:8] + counts[8:]


def slab_bins(bins):
    base = lax.axis_index("gx") * HISTOGRAM_BINS // lax.axis_size("gx")
    return (bins - base) & (HISTOGRAM_BINS - 1)


def interior_kernel(
    density,
    momentum,
    energy,
    edge,
    dilatation_bin,
    vorticity_bin,
    switch,
    matrix,
    updated_out,
    energy_out,
    weight_out,
    ends_out,
    counts_out,
    bins_out,
    matrix_out,
    mask_out,
):
    first_core = lax.axis_index("gy") == 0
    last_slab = lax.axis_index("gx") == lax.axis_size("gx") - 1
    q = [packed(density)] + [packed(momentum, c) for c in range(3)] + [packed(energy)]
    vel, pressure = velocity_pressure(q)
    flux_x = euler_flux(q, vel, pressure, 0)
    flux_y = euler_flux(q, vel, pressure, 1)
    flux_z = euler_flux(q, vel, pressure, 2)
    zero = jnp.zeros((1, 8, LANES), jnp.float32)
    lane = iota((8, 8, LANES), 2) % 32
    halo = edge[...]

    def y_whole(a, i):
        near = jnp.where(first_core, roll(halo, 31 - i, 2), -roll(halo, -i, 2))
        near = jnp.where(lane == jnp.where(first_core, 31, 0), near, 0.0)
        return y_difference(a, first_core) + near

    updated = []
    for f in range(5):
        after = jnp.where(last_slab, flux_x[f][7:], 0.0)
        change = x_difference(flux_x[f], zero, after)
        change = change + y_whole(flux_y[f], f) + z_difference(flux_z[f])
        updated.append(q[f] - HALF_STEP * change)
    dx = [x_difference(a, zero, jnp.where(last_slab, a[7:], 0.0)) for a in vel]
    dy = [y_whole(vel[c], 5 + c) for c in range(3)]
    dz = [z_difference(a) for a in vel]
    rates = [dx[0] + dy[1] + dz[2], dy[2] - dz[1], dz[0] - dx[2], dx[1] - dy[0]]
    sensor = sensor_of(*rates)
    mask = jnp.concatenate([switch[...].astype(jnp.float32)] * 4, axis=1)
    weight = sensor * mask[None]
    for k in range(4):
        updated_out[k] = regrouped(updated[:4], k)
        energy_out[k] = roll(updated[4], -32 * k, 2)
        weight_out[k] = regrouped([weight] * 4, k)
    for i, a in enumerate(updated + rates):
        ends_out[i, 0] = a[0]
        ends_out[i, 1] = a[7]
    dil = packed(dilatation_bin)
    vort = slab_bins(packed(vorticity_bin))
    inner = range(1, 7)
    counts_out[...] = counted(
        [sensor[x] for x in inner], [dil[x] for x in inner], [vort[x] for x in inner]
    )
    for end in range(2):
        bins_out[0, end] = dil[7 * end]
        bins_out[1, end] = vort[7 * end]
    matrix_out[0], matrix_out[1] = halves(matrix[...])
    mask_out[...] = jnp.broadcast_to(mask, (8, LANES))


def pencil_kernel(
    received,
    matrix,
    ends,
    counts_in,
    bins,
    mask,
    far,
    pair,
    send,
    updated_out,
    energy_out,
    weight_out,
    before,
):
    slab = lax.axis_index("gx")
    core = lax.axis_index("gy")
    last_slab = slab == lax.axis_size("gx") - 1
    odd = slab % 2 == 1
    plane = (slab * 2 + core).astype(jnp.float32)
    row = iota((8, LANES), 0)
    lane = iota((8, LANES), 1)
    peak = HAT_PEAK * HAT_PEAK

    chunk_tile = lambda g, h, t: received[pl.ds(32 * g + 16 * h + 8 * t, 8), :]
    tiles = [[chunk_tile(g, h, 1) for g in range(16)] for h in range(2)]
    chunks = []
    for h in range(2):
        for a in range(4):
            out = None
            for i in range(4):
                moved = roll(tiles[h][4 * a + i], 32 * (i - 1), 1)
                out = moved if out is None else jnp.where(lane // 32 == i, moved, out)
            chunks.append(out)
    y_all = iota((64, LANES), 0).astype(jnp.float32)
    lhs, rhs = [], []
    for chunk in chunks:
        weighted = (chunk * peak) * span_hat(plane, chunk[2:3], 32.0)
        lhs.append(jnp.where((row >= 3) & (row <= 5), weighted, 0.0))
        rhs.append(normal_hat(y_all, chunk[1:2]))
    high, low = halves(jnp.concatenate(lhs, axis=1))
    inflow = dot_nt(jnp.concatenate([high, low], axis=0), jnp.concatenate(rhs, axis=1))
    inflow = inflow[:8] + inflow[8:]
    ghost = ghost_state_rows(inflow[3:4], inflow[4:5], inflow[5:6])
    ghost_vel, ghost_pressure = velocity_pressure(ghost)
    ghost_x = euler_flux(ghost, ghost_vel, ghost_pressure, 0)

    @pl.when(slab == 0)
    def _():
        z_all = iota((32, LANES), 0).astype(jnp.float32)
        y_own = (iota((32, LANES), 0) + core * 32).astype(jnp.float32)
        lhs, rhs = [], []
        for chunk in chunks:
            hat = span_hat(z_all, chunk[2:3], 32.0) * peak
            lhs.append(jnp.concatenate([hat * chunk[3 + c : 4 + c] for c in range(3)], axis=0))
            rhs.append(normal_hat(y_own, chunk[1:2]))
        high, low = halves(jnp.concatenate(lhs, axis=1))
        own = dot_nt(jnp.concatenate([high, low], axis=0), jnp.concatenate(rhs, axis=1))
        own = own[:96] + own[96:]
        parts = [
            jnp.concatenate([own[c * 32 + 8 * k : c * 32 + 8 * k + 8] for k in range(4)], axis=1)
            for c in range(3)
        ]
        q = ghost_state_rows(*parts)
        for f in range(5):
            before[f] = q[f]

    @pl.when(slab != 0)
    def _():
        before[...] = jnp.where(odd, pair[...], far[...])

    chunk_row = lambda r: received[pl.ds(8 + r, 32, stride=16), :]
    group = iota((32, LANES), 1) // 32
    faces = []
    for slots in ((0, 2, 4, 6), (7, 1, 3, 5)):
        side = None
        for f, r in enumerate(slots):
            moved = roll(chunk_row(r), 32 * (f - 3), 1)
            side = moved if side is None else jnp.where(group == f, moved, side)
        faces.append((side, roll(chunk_row(slots[0]), -32, 1)))
    last_faces, first_faces = faces
    columns_a, columns_e = [], []
    for h in range(2):
        own = slice(32 * h, 32 * h + 32)
        ghost_a = jnp.concatenate([ghost_x[f][:, own] for f in range(4)], axis=1)
        ghost_e = jnp.concatenate([ghost_x[4][:, own]] * 4, axis=1)
        ca, ce = [], []
        for g in range(16):
            zero = jnp.zeros((1, LANES), jnp.float32)
            i, j = 2 * g + h - 2, 2 * g + h + 2
            previous_a, previous_e = ghost_a, ghost_e
            if g > 0:
                previous_a, previous_e = last_faces[0][i : i + 1], last_faces[1][i : i + 1]
            next_a, next_e = zero, zero
            if g < 15:
                next_a, next_e = first_faces[0][j : j + 1], first_faces[1][j : j + 1]
            fix_a = jnp.where(row == 0, previous_a, jnp.where(row == 7, -next_a, 0.0))
            fix_e = jnp.where(row == 0, previous_e, jnp.where(row == 7, -next_e, 0.0))
            other = tiles[1 - h][g]
            target = 31 if h == 0 else 0
            side = -1.0 if h == 0 else 1.0
            for f in range(4):
                moved = roll(other, 32 * f + target - (64 + f), 1)
                fix_a = jnp.where(lane == 32 * f + target, fix_a + side * moved, fix_a)
            moved = roll(other, target - 68, 1)
            fix_e = jnp.where(lane == target, fix_e + side * moved, fix_e)
            ca.append(chunk_tile(g, h, 0) + HALF_STEP * fix_a)
            ce.append(jnp.where(lane < 32, tiles[h][g] + HALF_STEP * fix_e, 0.0))
        columns_a.append(jnp.concatenate(ca, axis=0))
        columns_e.append(jnp.concatenate(ce, axis=0))
    columns = jnp.concatenate(
        [columns_a[0], columns_a[1], columns_e[0] + roll(columns_e[1], 32, 1)], axis=1
    )
    m_high, m_low = matrix[0], matrix[1]
    c_high, c_low = halves(columns)
    smooth = (
        jnp.dot(m_high, c_high, preferred_element_type=jnp.float32)
        + jnp.dot(m_high, c_low, preferred_element_type=jnp.float32)
        + jnp.dot(m_low, c_high, preferred_element_type=jnp.float32)
    )

    sensors, dils, vorts = [], [], []
    for end in range(2):
        q = [jnp.where(odd, far[f], pair[f]) if end else before[f] for f in range(5)]
        vel, pressure = velocity_pressure(q)
        flux = euler_flux(q, vel, pressure, 0)
        sign = -1.0 if end == 0 else 1.0
        add = [sign * a for a in flux + vel]
        if end == 1:
            add = [jnp.where(last_slab, 0.0, a) for a in add]
        updated = [ends[f, end] - HALF_STEP * add[f] for f in range(5)]
        rates = [ends[5 + i, end] for i in range(4)]
        rates = [rates[0] + add[5], rates[1], rates[2] - add[7], rates[3] + add[6]]
        sensor = sensor_of(*rates)
        weight = sensor * mask[...]
        for k in range(4):
            updated_out[end, k] = regrouped(updated[:4], k)
            energy_out[end, k] = roll(updated[4], -32 * k, 1)
            weight_out[end, k] = regrouped([weight] * 4, k)
        sensors.append(sensor)
        dils.append(bins[0, end])
        vorts.append(bins[1, end])
    counts = counts_in[...] + counted(sensors, dils, vorts)
    counts = jnp.concatenate([jnp.zeros((8, 64), jnp.float32), counts], axis=1)

    for g in range(16):
        block = smooth[8 * g : 8 * g + 8]
        for h in range(2):
            send[g, h, 0] = block[:, 128 * h : 128 * h + 128]
            own_energy = roll(block[:, 256:], -32 * h, 1)
            send[g, h, 1] = jnp.where(lane < 32, own_energy, counts)


def final_kernel(
    scale,
    received,
    updated,
    energy,
    weight,
    end_updated,
    end_energy,
    end_weight,
    conserved,
    histogram,
    totals,
):
    for k in range(4):
        for x in range(8):
            if x in (0, 7):
                end = x // 7
                u, e, w = end_updated[end, k], end_energy[end, k], end_weight[end, k]
            else:
                u, e, w = updated[k, x], energy[k, x], weight[k, x]
            smooth = received[pl.ds(k * 128 + x, 8, stride=16), :]
            result = u + w * (smooth - u)
            for f in range(4):
                conserved[f, x, 8 * k : 8 * k + 8, :] = result[:, 32 * f : 32 * f + 32]
            smooth = received[pl.ds(k * 128 + 8 + x, 8, stride=16), :]
            result = e + w * (smooth - e)
            conserved[4, x, 8 * k : 8 * k + 8, :] = result[:, :32]
    totals[...] = jnp.zeros_like(totals)
    for g in range(16):
        both = received[32 * g + 8 : 32 * g + 16, :] + received[32 * g + 24 : 32 * g + 32, :]
        totals[4 * g : 4 * g + 8, :] = totals[4 * g : 4 * g + 8, :] + both
    first = totals[0:8, :] + totals[64:72, :]
    table = jnp.concatenate([first, totals[8:64, :]], axis=0)[:, 64:]
    histogram[...] = table.T * scale


def shards(
    density,
    momentum,
    energy,
    eddy_normal_cell,
    eddy_spanwise_cell,
    eddy_signs,
    eddy_strengths,
    filter_matrices,
    shock_switch,
    dilatation_bin,
    vorticity_bin,
):
    slabs, cores = lax.axis_size("gx"), lax.axis_size("gy")
    shapes = (density.shape, eddy_strengths.shape, filter_matrices.shape, slabs, cores)
    if shapes != ((8, 32, 32), (64,), (1, 128, 128), 16, 2):
        return general_shards(
            density,
            momentum,
            energy,
            eddy_normal_cell,
            eddy_spanwise_cell,
            eddy_signs,
            eddy_strengths,
            filter_matrices,
            shock_switch,
            dilatation_bin,
            vorticity_bin,
        )
    cells_x, span, cells_y = density.shape
    total_y = cells_y * cores
    total_eddies = eddy_strengths.shape[0] * slabs
    amplitude = math.sqrt(total_y * span / (total_eddies * SIGMA_Y * SIGMA_Z))
    plane = jax.ShapeDtypeStruct((5, 8, LANES), jnp.float32)
    cells = (8, 8, LANES)
    f32 = lambda *shape: jax.ShapeDtypeStruct(shape, jnp.float32)
    vmem = lambda *shape: pltpu.VMEM(shape, jnp.float32)
    near = lambda a: pltpu.with_memory_space_constraint(a, pltpu.VMEM)
    send, far, pair, edge = pl.pallas_call(
        lambda *refs: slab_kernel(amplitude, *refs),
        out_shape=[vmem(512, LANES), vmem(5, 8, LANES), vmem(5, 8, LANES), vmem(*cells)],
        name="slab",
    )(
        density,
        momentum,
        energy,
        eddy_normal_cell.reshape(1, -1),
        eddy_spanwise_cell.reshape(1, -1),
        eddy_signs.T,
        eddy_strengths.reshape(1, -1),
    )
    received = lax.all_to_all(send.reshape(32, 16, LANES), ("gx", "gy"), 0, 0, tiled=True)
    both = lambda first: [p for i in range(first, slabs - 1, 2) for p in ((i, i + 1), (i + 1, i))]
    far = lax.ppermute(far, "gx", both(1))
    pair = lax.ppermute(pair, "gx", both(0))
    other_edge = lax.ppermute(edge, "gy", [(0, 1), (1, 0)])
    updated, updated_energy, weight, ends, counts, bins, matrix, mask = pl.pallas_call(
        interior_kernel,
        out_shape=[
            vmem(4, *cells),
            vmem(4, *cells),
            vmem(4, *cells),
            vmem(9, 2, 8, LANES),
            vmem(8, 64),
            pltpu.VMEM((2, 2, 8, LANES), jnp.int32),
            pltpu.VMEM((2, *filter_matrices.shape[1:]), jnp.bfloat16),
            vmem(8, LANES),
        ],
        cost_estimate=pl.CostEstimate(flops=10_000_000, bytes_accessed=2_000_000, transcendentals=0),
        name="interior",
    )(
        density,
        momentum,
        energy,
        near(other_edge),
        dilatation_bin,
        vorticity_bin,
        shock_switch,
        filter_matrices[0],
    )
    send, *end_rows = pl.pallas_call(
        pencil_kernel,
        out_shape=[vmem(16, 2, 2, 8, LANES)] + [vmem(2, 4, 8, LANES)] * 3,
        scratch_shapes=[pltpu.VMEM((5, 8, LANES), jnp.float32)],
        name="pencil",
    )(
        near(received.reshape(512, LANES)),
        *map(near, (matrix, ends, counts, bins, mask, far, pair)),
    )
    received = lax.all_to_all(send.reshape(32, 16, LANES), ("gx", "gy"), 0, 0, tiled=True)
    scale = HISTOGRAM_BINS * HISTOGRAM_BINS / (cells_x * slabs * span * total_y)
    conserved_next, histogram = pl.pallas_call(
        lambda *refs: final_kernel(scale, *refs),
        out_shape=[f32(5, cells_x, span, cells_y), f32(HISTOGRAM_BINS, HISTOGRAM_BINS)],
        scratch_shapes=[pltpu.VMEM((72, LANES), jnp.float32)],
        name="final",
    )(*map(near, (received.reshape(512, LANES), updated, updated_energy, weight, *end_rows)))
    return (conserved_next, histogram)


def solution(mesh):
    in_specs = (
        P("gx", None, "gy"),
        P(None, "gx", None, "gy"),
        P("gx", None, "gy"),
        P("gx"),
        P("gx"),
        P("gx", None),
        P("gx"),
        P(),
        P(None, "gy"),
        P("gx", None, "gy"),
        P("gx", None, "gy"),
    )
    out_specs = (P(None, "gx", None, "gy"), P())
    return jax.shard_map(shards, mesh=mesh, in_specs=in_specs, out_specs=out_specs, check_vma=False)
```

```python
import math

import jax
import jax.numpy as jnp
from jax import lax
from jax.experimental import pallas as pl
from jax.experimental.pallas import tpu as pltpu
from jax.sharding import PartitionSpec as P

HISTOGRAM_BINS = 64
SIGMA_Y = 32
SIGMA_Z = 8


TIME_STEP = 0.1
GAMMA_GAS = 1.4
SENSOR_EPS = 0.1
HAT_PEAK = math.sqrt(1.5)


def extended(x, sides, width):
    for axis, dim in sides:
        size, length = (lax.axis_size(axis), x.shape[dim])
        up = [(i, (i + 1) % size) for i in range(size - 1)]
        down = [(j, i) for i, j in up]
        last = lax.slice_in_dim(x, length - width, length, axis=dim)
        first = lax.slice_in_dim(x, 0, width, axis=dim)
        before = lax.ppermute(last, axis, up)
        after = lax.ppermute(first, axis, down)
        x = jnp.concatenate([before, x, after], axis=dim)
    return x


def hat_shape(centres, coords, spread, period):
    offset = coords[None, :] - centres[:, None]
    if period > 0:
        offset = jnp.mod(offset + period / 2, period) - period / 2
    return HAT_PEAK * jnp.maximum(0.0, 1.0 - jnp.abs(offset) / spread)


def inflow_from(centre_y, centre_z, eddy_weight, coords_y, coords_z, span):
    shape_y = hat_shape(centre_y, coords_y, float(SIGMA_Y), 0)
    shape_z = hat_shape(centre_z, coords_z, float(SIGMA_Z), span)
    weighted = (eddy_weight[:, :, None] * shape_z[:, None, :]).reshape(eddy_weight.shape[0], -1)
    inflow = jnp.dot(weighted.T, shape_y, precision=lax.Precision.HIGHEST)
    return inflow.reshape(3, coords_z.shape[0], coords_y.shape[0])


def ghost_state(inflow):
    mom_x = 1.0 + inflow[0]
    kinetic = mom_x * mom_x + inflow[1] * inflow[1] + inflow[2] * inflow[2]
    return jnp.stack([jnp.ones_like(mom_x), mom_x, inflow[1], inflow[2], 3.0 + 0.5 * kinetic])


def flux_of(fields, velocity, pressure, direction):
    result = fields * velocity[direction][None]
    result = result.at[1 + direction].add(pressure)
    return result.at[4].add(pressure * velocity[direction])


def central_x(values):
    return (values[..., 2:, :, 1:-1] - values[..., :-2, :, 1:-1]) * 0.5


def central_y(values):
    return (values[..., 1:-1, :, 2:] - values[..., 1:-1, :, :-2]) * 0.5


def central_z(values):
    centre = values[..., 1:-1, :, 1:-1]
    return (jnp.roll(centre, -1, axis=-2) - jnp.roll(centre, 1, axis=-2)) * 0.5


def section_rhs(padded):
    velocity = padded[1:4] / padded[0][None]
    pressure = (GAMMA_GAS - 1.0) * (padded[4] - 0.5 * jnp.sum(padded[1:4] * velocity, axis=0))
    change = central_x(flux_of(padded, velocity, pressure, 0))
    change = change + central_y(flux_of(padded, velocity, pressure, 1))
    change = change + central_z(flux_of(padded, velocity, pressure, 2))
    updated = padded[:, 1:-1, :, 1:-1] - TIME_STEP * change
    dilatation = central_x(velocity[0]) + central_y(velocity[1]) + central_z(velocity[2])
    vort_x = central_y(velocity[2]) - central_z(velocity[1])
    vort_y = central_z(velocity[0]) - central_x(velocity[2])
    vort_z = central_x(velocity[1]) - central_y(velocity[0])
    squared = dilatation * dilatation
    shock_sensor = squared / (
        squared + vort_x * vort_x + vort_y * vort_y + vort_z * vort_z + SENSOR_EPS
    )
    return (updated, shock_sensor)


def filter_lines(pencil, filter_matrices):
    block_count, block_len = (filter_matrices.shape[0], filter_matrices.shape[1])
    lanes = pencil.shape[2]
    blocks = pencil.reshape(5, block_count, block_len, lanes)
    smooth = jnp.einsum("bij,fbjp->fbip", filter_matrices, blocks, precision=lax.Precision.HIGHEST)
    return smooth.reshape(5, block_count * block_len, lanes)


def plane_histogram(shock_sensor, dilatation_bin, vorticity_bin):
    bin_levels = jnp.arange(HISTOGRAM_BINS, dtype=jnp.int32)

    def accumulate_plane(histogram_totals, histogram_parts):
        sensor_plane, plane_dilatation, plane_vorticity = histogram_parts
        flat_sensor = sensor_plane.reshape(-1)
        dilatation_table = (plane_dilatation.reshape(-1)[None, :] == bin_levels[:, None]).astype(
            jnp.float32
        )
        vorticity_table = jnp.where(
            plane_vorticity.reshape(-1)[:, None] == bin_levels[None, :], flat_sensor[:, None], 0.0
        )
        return (
            histogram_totals
            + jnp.dot(dilatation_table, vorticity_table, precision=lax.Precision.HIGHEST),
            None,
        )

    histogram_totals, _ = lax.scan(
        accumulate_plane,
        jnp.zeros((HISTOGRAM_BINS, HISTOGRAM_BINS), jnp.float32),
        (shock_sensor, dilatation_bin, vorticity_bin),
    )
    return histogram_totals


def general_shards(
    density,
    momentum,
    energy,
    eddy_normal_cell,
    eddy_spanwise_cell,
    eddy_signs,
    eddy_strengths,
    filter_matrices,
    shock_switch,
    dilatation_bin,
    vorticity_bin,
):
    cells_x, span, cells_y = density.shape
    slab_index = lax.axis_index("gx")
    block_index = lax.axis_index("gy")
    slab_count = lax.axis_size("gx")
    fields = jnp.concatenate([density[None], momentum, energy[None]], axis=0)
    total_y = cells_y * lax.axis_size("gy")
    total_eddies = eddy_normal_cell.shape[0] * slab_count
    amplitude = math.sqrt(total_y * span / (total_eddies * SIGMA_Y * SIGMA_Z))
    eddy_weight = (2 * eddy_signs - 1).astype(jnp.float32) * eddy_strengths[:, None] * amplitude
    coords_y = (block_index * cells_y + jnp.arange(cells_y, dtype=jnp.int32)).astype(jnp.float32)
    coords_z = jnp.arange(span, dtype=jnp.int32).astype(jnp.float32)
    partial_sum = inflow_from(
        eddy_normal_cell.astype(jnp.float32),
        eddy_spanwise_cell.astype(jnp.float32),
        eddy_weight,
        coords_y,
        coords_z,
        span,
    )
    inflow = lax.psum(partial_sum, "gx")
    ghost_cells = ghost_state(inflow)
    padded = extended(fields, (("gx", 1), ("gy", 3)), 1)
    padded = padded.at[:, 0, :, 1:-1].set(
        jnp.where(slab_index == 0, ghost_cells, padded[:, 0, :, 1:-1])
    )
    padded = padded.at[:, -1, :, 1:-1].set(
        jnp.where(slab_index == slab_count - 1, fields[:, -1], padded[:, -1, :, 1:-1])
    )
    padded = padded.at[:, 1:-1, :, 0].set(
        jnp.where(block_index == 0, fields[:, :, :, 0], padded[:, 1:-1, :, 0])
    )
    padded = padded.at[:, 1:-1, :, -1].set(
        jnp.where(
            block_index == lax.axis_size("gy") - 1, fields[:, :, :, -1], padded[:, 1:-1, :, -1]
        )
    )
    updated, shock_sensor = section_rhs(padded)
    block_len = filter_matrices.shape[1]
    filter_row = slab_index * cells_x // block_len
    mask_row = lax.dynamic_slice_in_dim(shock_switch, filter_row, 1, 0).astype(jnp.float32)
    weight = mask_row[None] * shock_sensor
    columns = span * cells_y
    stacked = updated.reshape(5, cells_x, columns)
    weight_flat = weight.reshape(1, cells_x, columns)
    pencil, pencil_weight = (
        lax.all_to_all(stacked, "gx", split_axis=2, concat_axis=1, tiled=True),
        lax.all_to_all(weight_flat, "gx", split_axis=2, concat_axis=1, tiled=True),
    )
    smooth = filter_lines(pencil, filter_matrices)
    returned = pencil + pencil_weight * (smooth - pencil)
    back_lines = lax.all_to_all(returned, "gx", split_axis=1, concat_axis=2, tiled=True)
    conserved_next = back_lines.reshape(5, cells_x, span, cells_y)
    partial_histogram = plane_histogram(shock_sensor, dilatation_bin, vorticity_bin)
    summed = lax.psum(partial_histogram, ("gx", "gy"))
    all_cells = cells_x * slab_count * span * total_y
    histogram = summed * (HISTOGRAM_BINS * HISTOGRAM_BINS / all_cells)
    return (conserved_next, histogram)


LANES = 128
SENT = 15
BACK = 13
HALF_STEP = 0.5 * TIME_STEP


def iota(shape, dim):
    return lax.broadcasted_iota(jnp.int32, shape, dim)


def roll(x, shift, axis):
    shift %= x.shape[axis]
    return x if shift == 0 else pltpu.roll(x, shift, axis)


def packed(ref, *lead):
    lead = lead if len(lead) == len(ref.shape) - 2 else (*lead, slice(None))
    parts = [ref[(*lead, pl.ds(8 * k, 8), slice(None))] for k in range(4)]
    return jnp.concatenate(parts, axis=-1)


def regrouped(parts, k):
    group = iota(parts[0].shape, len(parts[0].shape) - 1) // 32
    out = None
    for i, part in enumerate(parts):
        moved = roll(part, 32 * (i - k), len(part.shape) - 1)
        out = moved if out is None else jnp.where(group == i, moved, out)
    return out


def velocity_pressure(q):
    inverse = 1.0 / q[0]
    vel = [q[1] * inverse, q[2] * inverse, q[3] * inverse]
    kinetic = q[1] * vel[0] + q[2] * vel[1] + q[3] * vel[2]
    return vel, (GAMMA_GAS - 1.0) * (q[4] - 0.5 * kinetic)


def euler_flux(q, vel, pressure, k):
    flux = [q[1 + k], q[1] * vel[k], q[2] * vel[k], q[3] * vel[k], (q[4] + pressure) * vel[k]]
    flux[1 + k] = flux[1 + k] + pressure
    return flux


def z_difference(a):
    row = iota(a.shape, 1)
    up = roll(a, -1, 1)
    up = jnp.where(row == 7, roll(up, -32, 2), up)
    down = roll(a, 1, 1)
    down = jnp.where(row == 0, roll(down, 32, 2), down)
    return up - down


def y_difference(a, first_core):
    lane = iota(a.shape, 2) % 32
    up = jnp.where(lane == 31, jnp.where(first_core, 0.0, a), roll(a, -1, 2))
    down = jnp.where(lane == 0, jnp.where(first_core, a, 0.0), roll(a, 1, 2))
    return up - down


def x_difference(a, before, after):
    up = jnp.concatenate([a[1:], after], axis=0)
    down = jnp.concatenate([before, a[:-1]], axis=0)
    return up - down


def slab_kernel(
    amplitude,
    density,
    momentum,
    energy,
    normal_cell,
    spanwise_cell,
    signs,
    strengths,
    send,
    far_out,
    pair_out,
    edge_out,
):
    slab = lax.axis_index("gx")
    first_core = lax.axis_index("gy") == 0
    odd = slab % 2 == 1
    last_slab = slab == lax.axis_size("gx") - 1
    q = [packed(density)] + [packed(momentum, c) for c in range(3)] + [packed(energy)]
    vel, pressure = velocity_pressure(q)
    flux_x = euler_flux(q, vel, pressure, 0)
    flux_y = euler_flux(q, vel, pressure, 1)
    flux_z = euler_flux(q, vel, pressure, 2)
    zero = jnp.zeros((1, 8, LANES), jnp.float32)
    partial = []
    for f in range(5):
        after = jnp.where(last_slab, flux_x[f][7:], 0.0)
        change = x_difference(flux_x[f], zero, after)
        change = change + y_difference(flux_y[f], first_core)
        change = change + z_difference(flux_z[f])
        partial.append(q[f] - HALF_STEP * change)
        far_out[f] = jnp.where(odd, q[f][7], q[f][0])
        pair_out[f] = jnp.where(odd, q[f][0], q[f][7])

    lane2 = iota((8, LANES), 1)
    shift = jnp.where(first_core, LANES - 31, 0)
    sides = []
    for i, value in enumerate(flux_y + vel):
        side = jnp.zeros((8, LANES), jnp.float32)
        for x in range(8):
            side = jnp.where(lane2 % 32 == x, pltpu.roll(value[x], shift + x, 1), side)
        edge_out[i] = side
        sides.append(side)
    energy_side = roll(sides[4], 8, 1)
    sides = [jnp.where(lane2 % 32 < 8, sides[0], energy_side)] + sides[1:4]

    pick = lambda a: jnp.where(first_core, a[:, :32], a[:, 32:])
    strength = strengths[...] * amplitude
    eddies = [pick(normal_cell[...]).astype(jnp.float32), pick(spanwise_cell[...]).astype(jnp.float32)]
    for c in range(3):
        sign = (2 * signs[c : c + 1, :] - 1).astype(jnp.float32)
        eddies.append(pick(sign * strength))
    eddy_row = jnp.broadcast_to(jnp.concatenate(eddies[:4], axis=1), (8, LANES))
    eddy_rest = jnp.broadcast_to(jnp.concatenate([eddies[4]] * 4, axis=1), (8, LANES))
    for k in range(4):
        cells = regrouped(partial[:4], k)
        rows = [cells[x] for x in range(8)]
        rows += [regrouped([partial[4][4 * a + b] for b in range(4)], k) for a in range(2)]
        rows += [regrouped([flux_x[f][x] for f in range(4)], k) for x in (7, 0)]
        rows += [regrouped(sides, k), eddy_row]
        ends = [jnp.zeros_like(eddy_rest), flux_x[4][7], flux_x[4][0], jnp.zeros_like(eddy_rest)]
        rows.append(jnp.where(lane2 < 32, eddy_rest, regrouped(ends, k)))
        for r, value in enumerate(rows):
            send[pl.ds(8 * SENT * k + r, 8, stride=SENT), :] = value


def dot_nt(a, b):
    return lax.dot_general(
        a, b, (((1,), (1,)), ((), ())), preferred_element_type=jnp.float32
    )


def halves(a):
    high = a.astype(jnp.bfloat16)
    return high, (a - high.astype(jnp.float32)).astype(jnp.bfloat16)


def span_hat(z, centre, span):
    offset = z - centre + span / 2
    offset = jnp.where(offset < 0, offset + span, jnp.where(offset >= span, offset - span, offset))
    return jnp.maximum(0.0, 1.0 - jnp.abs(offset - span / 2) * (1.0 / SIGMA_Z))


def normal_hat(y, centre):
    return jnp.maximum(0.0, 1.0 - jnp.abs(y - centre) * (1.0 / SIGMA_Y)).astype(jnp.bfloat16)


def ghost_state_rows(a, b, c):
    mom = 1.0 + a
    kinetic = mom * mom + b * b + c * c
    return [jnp.ones_like(mom), mom, b, c, 3.0 + 0.5 * kinetic]


def sensor_of(d, vort_x, vort_y, vort_z):
    squared = d * d
    total = squared + vort_x * vort_x + vort_y * vort_y + vort_z * vort_z
    return squared / (total + 4.0 * SENSOR_EPS)


def counted(sensor, dil, vort):
    row = iota((8, LANES), 0)
    levels = iota((HISTOGRAM_BINS, LANES), 0)
    values, ones = [], []
    for x in range(len(sensor)):
        for z in range(8):
            values.append(jnp.where(vort[x][z : z + 1] == row, sensor[x][z : z + 1], 0.0))
            ones.append(jnp.where(dil[x][z : z + 1] == levels, 1.0, 0.0).astype(jnp.bfloat16))
    high, low = halves(jnp.concatenate(values, axis=1))
    counts = dot_nt(jnp.concatenate([high, low], axis=0), jnp.concatenate(ones, axis=1))
    return counts[:8] + counts[8:]


def slab_bins(bins):
    base = lax.axis_index("gx") * HISTOGRAM_BINS // lax.axis_size("gx")
    return (bins - base) & (HISTOGRAM_BINS - 1)


def interior_kernel(
    density,
    momentum,
    energy,
    edge,
    dilatation_bin,
    vorticity_bin,
    switch,
    matrix,
    updated_out,
    energy_out,
    weight_out,
    ends_out,
    counts_out,
    bins_out,
    matrix_out,
    mask_out,
):
    first_core = lax.axis_index("gy") == 0
    last_slab = lax.axis_index("gx") == lax.axis_size("gx") - 1
    q = [packed(density)] + [packed(momentum, c) for c in range(3)] + [packed(energy)]
    vel, pressure = velocity_pressure(q)
    flux_x = euler_flux(q, vel, pressure, 0)
    flux_y = euler_flux(q, vel, pressure, 1)
    flux_z = euler_flux(q, vel, pressure, 2)
    zero = jnp.zeros((1, 8, LANES), jnp.float32)
    lane = iota((8, 8, LANES), 2) % 32
    halo = edge[...]

    shift = jnp.where(first_core, 31, LANES)
    sign = jnp.where(first_core, 1.0, -1.0)

    def y_whole(a, i):
        near = jnp.stack([pltpu.roll(halo[i], shift - x, 1) for x in range(8)]) * sign
        near = jnp.where(lane == jnp.where(first_core, 31, 0), near, 0.0)
        return y_difference(a, first_core) + near

    updated = []
    for f in range(5):
        after = jnp.where(last_slab, flux_x[f][7:], 0.0)
        change = x_difference(flux_x[f], zero, after)
        change = change + y_whole(flux_y[f], f) + z_difference(flux_z[f])
        updated.append(q[f] - HALF_STEP * change)
    dx = [x_difference(a, zero, jnp.where(last_slab, a[7:], 0.0)) for a in vel]
    dy = [y_whole(vel[c], 5 + c) for c in range(3)]
    dz = [z_difference(a) for a in vel]
    rates = [dx[0] + dy[1] + dz[2], dy[2] - dz[1], dz[0] - dx[2], dx[1] - dy[0]]
    sensor = sensor_of(*rates)
    mask = jnp.concatenate([switch[...].astype(jnp.float32)] * 4, axis=1)
    weight = sensor * mask[None]
    for k in range(4):
        updated_out[k] = regrouped(updated[:4], k)
        weight_out[k] = regrouped([weight] * 4, k)
        for a in range(2):
            four = range(4 * a, 4 * a + 4)
            energy_out[0, k, a] = regrouped([updated[4][x] for x in four], k)
            energy_out[1, k, a] = regrouped([weight[x] for x in four], k)
    for i, a in enumerate(updated + rates):
        ends_out[i, 0] = a[0]
        ends_out[i, 1] = a[7]
    dil = packed(dilatation_bin)
    vort = slab_bins(packed(vorticity_bin))
    inner = range(1, 7)
    counts_out[...] = counted(
        [sensor[x] for x in inner], [dil[x] for x in inner], [vort[x] for x in inner]
    )
    for end in range(2):
        bins_out[0, end] = dil[7 * end]
        bins_out[1, end] = vort[7 * end]
    rows = jnp.concatenate([matrix[pl.ds(r, 16, stride=8), :] for r in range(8)], axis=0)
    source, target = iota((LANES, LANES), 0), iota((LANES, LANES), 1)
    order = jnp.where(source == 8 * (target % 16) + target // 16, 1.0, 0.0).astype(jnp.bfloat16)
    for i, part in enumerate(halves(rows)):
        ordered = jnp.dot(part, order, preferred_element_type=jnp.float32)
        matrix_out[i] = ordered.astype(jnp.bfloat16)
    mask_out[...] = jnp.broadcast_to(mask, (8, LANES))


def pencil_kernel(
    received,
    matrix,
    ends,
    counts_in,
    bins,
    mask,
    far,
    pair,
    send,
    updated_out,
    energy_out,
    weight_out,
    before,
):
    slab = lax.axis_index("gx")
    core = lax.axis_index("gy")
    last_slab = slab == lax.axis_size("gx") - 1
    odd = slab % 2 == 1
    plane = (slab * 2 + core).astype(jnp.float32)
    row = iota((8, LANES), 0)
    lane = iota((8, LANES), 1)
    peak = HAT_PEAK * HAT_PEAK

    def side_by_side(r, group):
        out = None
        for j in range(4):
            moved = received[pl.ds(SENT * j + r, 8, stride=4 * SENT), :]
            moved = roll(moved, 32 * (j - group), 1)
            out = moved if out is None else jnp.where(lane // 32 == j, moved, out)
        return out

    centre_y, centre_z = side_by_side(13, 0), side_by_side(13, 1)
    strength = [side_by_side(13, 2), side_by_side(13, 3), side_by_side(14, 0)]
    strength = [a * peak for a in strength]
    hat = span_hat(plane, centre_z, 32.0)
    y_all = iota((64, LANES), 0).astype(jnp.float32)
    lhs, rhs = [], []
    for c in range(8):
        weighted = jnp.where(row == 1, strength[1][c : c + 1], strength[2][c : c + 1])
        weighted = jnp.where(row == 0, strength[0][c : c + 1], weighted)
        lhs.append(jnp.where(row < 3, weighted * hat[c : c + 1], 0.0))
        rhs.append(normal_hat(y_all, centre_y[c : c + 1]))
    high, low = halves(jnp.concatenate(lhs, axis=1))
    inflow = dot_nt(jnp.concatenate([high, low], axis=0), jnp.concatenate(rhs, axis=1))
    inflow = inflow[:8] + inflow[8:]
    ghost = ghost_state_rows(inflow[0:1], inflow[1:2], inflow[2:3])
    ghost_vel, ghost_pressure = velocity_pressure(ghost)
    ghost_x = euler_flux(ghost, ghost_vel, ghost_pressure, 0)

    @pl.when(slab == 0)
    def _():
        z_all = iota((32, LANES), 0).astype(jnp.float32)
        y_own = (iota((32, LANES), 0) + core * 32).astype(jnp.float32)
        lhs, rhs = [], []
        for c in range(8):
            hat = span_hat(z_all, centre_z[c : c + 1], 32.0)
            lhs.append(jnp.concatenate([hat * a[c : c + 1] for a in strength], axis=0))
            rhs.append(normal_hat(y_own, centre_y[c : c + 1]))
        high, low = halves(jnp.concatenate(lhs, axis=1))
        own = dot_nt(jnp.concatenate([high, low], axis=0), jnp.concatenate(rhs, axis=1))
        own = own[:96] + own[96:]
        parts = [
            jnp.concatenate([own[c * 32 + 8 * k : c * 32 + 8 * k + 8] for k in range(4)], axis=1)
            for c in range(3)
        ]
        q = ghost_state_rows(*parts)
        for f in range(5):
            before[f] = q[f]

    @pl.when(slab != 0)
    def _():
        before[...] = jnp.where(odd, pair[...], far[...])

    row16 = iota((16, LANES), 0)
    lane16 = iota((16, LANES), 1)
    chunk_row = lambda r, h: received[pl.ds(SENT * h + r, 16, stride=2 * SENT), :]
    columns, energy_columns = [], []
    for h in range(2):
        own = slice(32 * h, 32 * h + 32)
        target = 31 if h == 0 else 0
        side = -HALF_STEP if h == 0 else HALF_STEP
        across = side * chunk_row(12, 1 - h)
        ghost_a = jnp.concatenate([ghost_x[f][:, own] for f in range(4)], axis=1)
        ghost_e = jnp.concatenate([ghost_x[4][:, own]] * 4, axis=1)
        both_ends = chunk_row(14, h)
        last_a, first_a = chunk_row(10, h), chunk_row(11, h)
        last_e, first_e = roll(both_ends, -32, 1), roll(both_ends, -64, 1)
        before_a = jnp.where(row16 == 0, ghost_a, roll(last_a, 1, 0))
        before_e = jnp.where(row16 == 0, ghost_e, roll(last_e, 1, 0))
        after_a = jnp.where(row16 == 15, 0.0, roll(first_a, -1, 0))
        after_e = jnp.where(row16 == 15, 0.0, roll(first_e, -1, 0))
        for r in range(8):
            a = chunk_row(r, h)
            e = roll(chunk_row(8 + r // 4, h), -32 * (r % 4), 1)
            if r == 0:
                a, e = a + HALF_STEP * before_a, e + HALF_STEP * before_e
            if r == 7:
                a, e = a - HALF_STEP * after_a, e - HALF_STEP * after_e
            a = jnp.where(lane16 % 32 == target, a + roll(across, target - r, 1), a)
            e = jnp.where(lane16 == target, e + roll(across, target - r - 8, 1), e)
            columns.append(a)
            energy_columns.append(roll(e, 32 * h, 1))
    joined = [jnp.where(lane16 < 32, energy_columns[r], energy_columns[8 + r]) for r in range(8)]
    columns = jnp.concatenate(
        [jnp.concatenate(part, axis=0) for part in (columns[:8], columns[8:], joined)], axis=1
    )
    m_high, m_low = matrix[0], matrix[1]
    c_high, c_low = halves(columns)
    smooth = (
        jnp.dot(m_high, c_high, preferred_element_type=jnp.float32)
        + jnp.dot(m_high, c_low, preferred_element_type=jnp.float32)
        + jnp.dot(m_low, c_high, preferred_element_type=jnp.float32)
    )

    sensors, dils, vorts = [], [], []
    for end in range(2):
        q = [jnp.where(odd, far[f], pair[f]) if end else before[f] for f in range(5)]
        vel, pressure = velocity_pressure(q)
        flux = euler_flux(q, vel, pressure, 0)
        sign = -1.0 if end == 0 else 1.0
        add = [sign * a for a in flux + vel]
        if end == 1:
            add = [jnp.where(last_slab, 0.0, a) for a in add]
        updated = [ends[f, end] - HALF_STEP * add[f] for f in range(5)]
        rates = [ends[5 + i, end] for i in range(4)]
        rates = [rates[0] + add[5], rates[1], rates[2] - add[7], rates[3] + add[6]]
        sensor = sensor_of(*rates)
        weight = sensor * mask[...]
        for k in range(4):
            updated_out[end, k] = regrouped(updated[:4], k)
            energy_out[end, k] = roll(updated[4], 32 * (3 * end - k), 1)
            weight_out[end, k] = regrouped([weight] * 4, k)
        sensors.append(sensor)
        dils.append(bins[0, end])
        vorts.append(bins[1, end])
    counts = counts_in[...] + counted(sensors, dils, vorts)

    for h in range(2):
        back_row = lambda r: (pl.ds(BACK * h + r, 16, stride=2 * BACK), slice(None))
        for r in range(8):
            send[back_row(r)] = smooth[16 * r : 16 * r + 16, 128 * h : 128 * h + 128]
        for a in range(2):
            out = None
            for b in range(4):
                r = 4 * a + b
                moved = roll(smooth[16 * r : 16 * r + 16, 256:], 32 * (b - h), 1)
                out = moved if out is None else jnp.where(lane16 // 32 == b, moved, out)
            send[back_row(8 + a)] = out
        for i in range(3):
            pair_of_bins = jnp.concatenate([counts[2 * i : 2 * i + 1], counts[2 * i + 1 : 2 * i + 2]], axis=1)
            send[back_row(10 + i)] = jnp.broadcast_to(pair_of_bins, (16, LANES))


def final_kernel(
    scale,
    received,
    updated,
    energy,
    weight,
    end_updated,
    end_energy,
    end_weight,
    conserved,
    histogram,
    totals,
):
    group = iota((8, LANES), 1) // 32
    for k in range(4):
        planes = pl.ds(8 * k, 8)
        chunk_row = lambda r: received[pl.ds(8 * BACK * k + r, 8, stride=BACK), :]
        for x in range(8):
            if x in (0, 7):
                u, w = end_updated[x // 7, k], end_weight[x // 7, k]
            else:
                u, w = updated[k, x], weight[k, x]
            result = u + w * (chunk_row(x) - u)
            for f in range(4):
                conserved[f, x, planes, :] = result[:, 32 * f : 32 * f + 32]
        for a in range(2):
            ours = group == 3 * a
            u = jnp.where(ours, end_energy[a, k], energy[0, k, a])
            w = jnp.where(ours, end_weight[a, k], energy[1, k, a])
            result = u + w * (chunk_row(8 + a) - u)
            for b in range(4):
                conserved[4, 4 * a + b, planes, :] = result[:, 32 * b : 32 * b + 32]

    bins = []
    for i in range(3):
        both = [received[pl.ds(BACK * h + 10 + i, 16, stride=2 * BACK), :] for h in range(2)]
        bins.append(both[0] + both[1])
    first = bins[0] + roll(bins[2], 1, 0)
    for c, part in enumerate((first, roll(bins[0], 64, 1), bins[1], roll(bins[1], 64, 1))):
        totals[pl.ds(c, 16, stride=4), :] = part
    histogram[...] = totals[:, :64].T * scale


def shards(
    density,
    momentum,
    energy,
    eddy_normal_cell,
    eddy_spanwise_cell,
    eddy_signs,
    eddy_strengths,
    filter_matrices,
    shock_switch,
    dilatation_bin,
    vorticity_bin,
):
    slabs, cores = lax.axis_size("gx"), lax.axis_size("gy")
    shapes = (density.shape, eddy_strengths.shape, filter_matrices.shape, slabs, cores)
    if shapes != ((8, 32, 32), (64,), (1, 128, 128), 16, 2):
        return general_shards(
            density,
            momentum,
            energy,
            eddy_normal_cell,
            eddy_spanwise_cell,
            eddy_signs,
            eddy_strengths,
            filter_matrices,
            shock_switch,
            dilatation_bin,
            vorticity_bin,
        )
    cells_x, span, cells_y = density.shape
    total_y = cells_y * cores
    total_eddies = eddy_strengths.shape[0] * slabs
    amplitude = math.sqrt(total_y * span / (total_eddies * SIGMA_Y * SIGMA_Z))
    plane = jax.ShapeDtypeStruct((5, 8, LANES), jnp.float32)
    cells = (8, 8, LANES)
    f32 = lambda *shape: jax.ShapeDtypeStruct(shape, jnp.float32)
    vmem = lambda *shape: pltpu.VMEM(shape, jnp.float32)
    near = lambda a: pltpu.with_memory_space_constraint(a, pltpu.VMEM)
    send, far, pair, edge = pl.pallas_call(
        lambda *refs: slab_kernel(amplitude, *refs),
        out_shape=[vmem(32 * SENT, LANES), vmem(5, 8, LANES), vmem(5, 8, LANES), vmem(*cells)],
        name="slab",
    )(
        density,
        momentum,
        energy,
        eddy_normal_cell.reshape(1, -1),
        eddy_spanwise_cell.reshape(1, -1),
        eddy_signs.T,
        eddy_strengths.reshape(1, -1),
    )
    received = lax.all_to_all(send.reshape(32, SENT, 1, LANES), ("gx", "gy"), 0, 0, tiled=True)
    both = lambda first: [p for i in range(first, slabs - 1, 2) for p in ((i, i + 1), (i + 1, i))]
    far = lax.ppermute(far, "gx", both(1))
    pair = lax.ppermute(pair, "gx", both(0))
    other_edge = lax.ppermute(edge, "gy", [(0, 1), (1, 0)])
    updated, updated_energy, weight, ends, counts, bins, matrix, mask = pl.pallas_call(
        interior_kernel,
        out_shape=[
            vmem(4, *cells),
            vmem(2, 4, 2, 8, LANES),
            vmem(4, *cells),
            vmem(9, 2, 8, LANES),
            vmem(8, 64),
            pltpu.VMEM((2, 2, 8, LANES), jnp.int32),
            pltpu.VMEM((2, *filter_matrices.shape[1:]), jnp.bfloat16),
            vmem(8, LANES),
        ],
        cost_estimate=pl.CostEstimate(flops=10_000_000, bytes_accessed=2_000_000, transcendentals=0),
        name="interior",
    )(
        density,
        momentum,
        energy,
        near(other_edge),
        dilatation_bin,
        vorticity_bin,
        shock_switch,
        filter_matrices[0],
    )
    send, *end_rows = pl.pallas_call(
        pencil_kernel,
        out_shape=[vmem(32 * BACK, LANES)] + [vmem(2, 4, 8, LANES)] * 3,
        scratch_shapes=[pltpu.VMEM((5, 8, LANES), jnp.float32)],
        name="pencil",
    )(
        near(received.reshape(32 * SENT, LANES)),
        *map(near, (matrix, ends, counts, bins, mask, far, pair)),
    )
    received = lax.all_to_all(send.reshape(32, BACK, 1, LANES), ("gx", "gy"), 0, 0, tiled=True)
    scale = HISTOGRAM_BINS * HISTOGRAM_BINS / (cells_x * slabs * span * total_y)
    conserved_next, histogram = pl.pallas_call(
        lambda *refs: final_kernel(scale, *refs),
        out_shape=[f32(5, cells_x, span, cells_y), f32(HISTOGRAM_BINS, HISTOGRAM_BINS)],
        scratch_shapes=[vmem(HISTOGRAM_BINS, LANES)],
        name="final",
    )(
        near(received.reshape(32 * BACK, LANES)),
        *map(near, (updated, updated_energy, weight, *end_rows)),
    )
    return (conserved_next, histogram)


def solution(mesh):
    in_specs = (
        P("gx", None, "gy"),
        P(None, "gx", None, "gy"),
        P("gx", None, "gy"),
        P("gx"),
        P("gx"),
        P("gx", None),
        P("gx"),
        P(),
        P(None, "gy"),
        P("gx", None, "gy"),
        P("gx", None, "gy"),
    )
    out_specs = (P(None, "gx", None, "gy"), P())
    return jax.shard_map(shards, mesh=mesh, in_specs=in_specs, out_specs=out_specs, check_vma=False)
```

```python
import math

import jax
import jax.numpy as jnp
from jax import lax
from jax.experimental import pallas as pl
from jax.experimental.pallas import tpu as pltpu
from jax.sharding import PartitionSpec as P

HISTOGRAM_BINS = 64
SIGMA_Y = 32
SIGMA_Z = 8


TIME_STEP = 0.1
GAMMA_GAS = 1.4
SENSOR_EPS = 0.1
HAT_PEAK = math.sqrt(1.5)


def extended(x, sides, width):
    for axis, dim in sides:
        size, length = (lax.axis_size(axis), x.shape[dim])
        up = [(i, (i + 1) % size) for i in range(size - 1)]
        down = [(j, i) for i, j in up]
        last = lax.slice_in_dim(x, length - width, length, axis=dim)
        first = lax.slice_in_dim(x, 0, width, axis=dim)
        before = lax.ppermute(last, axis, up)
        after = lax.ppermute(first, axis, down)
        x = jnp.concatenate([before, x, after], axis=dim)
    return x


def hat_shape(centres, coords, spread, period):
    offset = coords[None, :] - centres[:, None]
    if period > 0:
        offset = jnp.mod(offset + period / 2, period) - period / 2
    return HAT_PEAK * jnp.maximum(0.0, 1.0 - jnp.abs(offset) / spread)


def inflow_from(centre_y, centre_z, eddy_weight, coords_y, coords_z, span):
    shape_y = hat_shape(centre_y, coords_y, float(SIGMA_Y), 0)
    shape_z = hat_shape(centre_z, coords_z, float(SIGMA_Z), span)
    weighted = (eddy_weight[:, :, None] * shape_z[:, None, :]).reshape(eddy_weight.shape[0], -1)
    inflow = jnp.dot(weighted.T, shape_y, precision=lax.Precision.HIGHEST)
    return inflow.reshape(3, coords_z.shape[0], coords_y.shape[0])


def ghost_state(inflow):
    mom_x = 1.0 + inflow[0]
    kinetic = mom_x * mom_x + inflow[1] * inflow[1] + inflow[2] * inflow[2]
    return jnp.stack([jnp.ones_like(mom_x), mom_x, inflow[1], inflow[2], 3.0 + 0.5 * kinetic])


def flux_of(fields, velocity, pressure, direction):
    result = fields * velocity[direction][None]
    result = result.at[1 + direction].add(pressure)
    return result.at[4].add(pressure * velocity[direction])


def central_x(values):
    return (values[..., 2:, :, 1:-1] - values[..., :-2, :, 1:-1]) * 0.5


def central_y(values):
    return (values[..., 1:-1, :, 2:] - values[..., 1:-1, :, :-2]) * 0.5


def central_z(values):
    centre = values[..., 1:-1, :, 1:-1]
    return (jnp.roll(centre, -1, axis=-2) - jnp.roll(centre, 1, axis=-2)) * 0.5


def section_rhs(padded):
    velocity = padded[1:4] / padded[0][None]
    pressure = (GAMMA_GAS - 1.0) * (padded[4] - 0.5 * jnp.sum(padded[1:4] * velocity, axis=0))
    change = central_x(flux_of(padded, velocity, pressure, 0))
    change = change + central_y(flux_of(padded, velocity, pressure, 1))
    change = change + central_z(flux_of(padded, velocity, pressure, 2))
    updated = padded[:, 1:-1, :, 1:-1] - TIME_STEP * change
    dilatation = central_x(velocity[0]) + central_y(velocity[1]) + central_z(velocity[2])
    vort_x = central_y(velocity[2]) - central_z(velocity[1])
    vort_y = central_z(velocity[0]) - central_x(velocity[2])
    vort_z = central_x(velocity[1]) - central_y(velocity[0])
    squared = dilatation * dilatation
    shock_sensor = squared / (
        squared + vort_x * vort_x + vort_y * vort_y + vort_z * vort_z + SENSOR_EPS
    )
    return (updated, shock_sensor)


def filter_lines(pencil, filter_matrices):
    block_count, block_len = (filter_matrices.shape[0], filter_matrices.shape[1])
    lanes = pencil.shape[2]
    blocks = pencil.reshape(5, block_count, block_len, lanes)
    smooth = jnp.einsum("bij,fbjp->fbip", filter_matrices, blocks, precision=lax.Precision.HIGHEST)
    return smooth.reshape(5, block_count * block_len, lanes)


def plane_histogram(shock_sensor, dilatation_bin, vorticity_bin):
    bin_levels = jnp.arange(HISTOGRAM_BINS, dtype=jnp.int32)

    def accumulate_plane(histogram_totals, histogram_parts):
        sensor_plane, plane_dilatation, plane_vorticity = histogram_parts
        flat_sensor = sensor_plane.reshape(-1)
        dilatation_table = (plane_dilatation.reshape(-1)[None, :] == bin_levels[:, None]).astype(
            jnp.float32
        )
        vorticity_table = jnp.where(
            plane_vorticity.reshape(-1)[:, None] == bin_levels[None, :], flat_sensor[:, None], 0.0
        )
        return (
            histogram_totals
            + jnp.dot(dilatation_table, vorticity_table, precision=lax.Precision.HIGHEST),
            None,
        )

    histogram_totals, _ = lax.scan(
        accumulate_plane,
        jnp.zeros((HISTOGRAM_BINS, HISTOGRAM_BINS), jnp.float32),
        (shock_sensor, dilatation_bin, vorticity_bin),
    )
    return histogram_totals


def general_shards(
    density,
    momentum,
    energy,
    eddy_normal_cell,
    eddy_spanwise_cell,
    eddy_signs,
    eddy_strengths,
    filter_matrices,
    shock_switch,
    dilatation_bin,
    vorticity_bin,
):
    cells_x, span, cells_y = density.shape
    slab_index = lax.axis_index("gx")
    block_index = lax.axis_index("gy")
    slab_count = lax.axis_size("gx")
    fields = jnp.concatenate([density[None], momentum, energy[None]], axis=0)
    total_y = cells_y * lax.axis_size("gy")
    total_eddies = eddy_normal_cell.shape[0] * slab_count
    amplitude = math.sqrt(total_y * span / (total_eddies * SIGMA_Y * SIGMA_Z))
    eddy_weight = (2 * eddy_signs - 1).astype(jnp.float32) * eddy_strengths[:, None] * amplitude
    coords_y = (block_index * cells_y + jnp.arange(cells_y, dtype=jnp.int32)).astype(jnp.float32)
    coords_z = jnp.arange(span, dtype=jnp.int32).astype(jnp.float32)
    partial_sum = inflow_from(
        eddy_normal_cell.astype(jnp.float32),
        eddy_spanwise_cell.astype(jnp.float32),
        eddy_weight,
        coords_y,
        coords_z,
        span,
    )
    inflow = lax.psum(partial_sum, "gx")
    ghost_cells = ghost_state(inflow)
    padded = extended(fields, (("gx", 1), ("gy", 3)), 1)
    padded = padded.at[:, 0, :, 1:-1].set(
        jnp.where(slab_index == 0, ghost_cells, padded[:, 0, :, 1:-1])
    )
    padded = padded.at[:, -1, :, 1:-1].set(
        jnp.where(slab_index == slab_count - 1, fields[:, -1], padded[:, -1, :, 1:-1])
    )
    padded = padded.at[:, 1:-1, :, 0].set(
        jnp.where(block_index == 0, fields[:, :, :, 0], padded[:, 1:-1, :, 0])
    )
    padded = padded.at[:, 1:-1, :, -1].set(
        jnp.where(
            block_index == lax.axis_size("gy") - 1, fields[:, :, :, -1], padded[:, 1:-1, :, -1]
        )
    )
    updated, shock_sensor = section_rhs(padded)
    block_len = filter_matrices.shape[1]
    filter_row = slab_index * cells_x // block_len
    mask_row = lax.dynamic_slice_in_dim(shock_switch, filter_row, 1, 0).astype(jnp.float32)
    weight = mask_row[None] * shock_sensor
    columns = span * cells_y
    stacked = updated.reshape(5, cells_x, columns)
    weight_flat = weight.reshape(1, cells_x, columns)
    pencil, pencil_weight = (
        lax.all_to_all(stacked, "gx", split_axis=2, concat_axis=1, tiled=True),
        lax.all_to_all(weight_flat, "gx", split_axis=2, concat_axis=1, tiled=True),
    )
    smooth = filter_lines(pencil, filter_matrices)
    returned = pencil + pencil_weight * (smooth - pencil)
    back_lines = lax.all_to_all(returned, "gx", split_axis=1, concat_axis=2, tiled=True)
    conserved_next = back_lines.reshape(5, cells_x, span, cells_y)
    partial_histogram = plane_histogram(shock_sensor, dilatation_bin, vorticity_bin)
    summed = lax.psum(partial_histogram, ("gx", "gy"))
    all_cells = cells_x * slab_count * span * total_y
    histogram = summed * (HISTOGRAM_BINS * HISTOGRAM_BINS / all_cells)
    return (conserved_next, histogram)


LANES = 128
SENT = 15
BACK = 13
HALF_STEP = 0.5 * TIME_STEP


def iota(shape, dim):
    return lax.broadcasted_iota(jnp.int32, shape, dim)


def roll(x, shift, axis):
    shift %= x.shape[axis]
    return x if shift == 0 else pltpu.roll(x, shift, axis)


def packed(ref, *lead):
    lead = lead if len(lead) == len(ref.shape) - 2 else (*lead, slice(None))
    parts = [ref[(*lead, pl.ds(8 * k, 8), slice(None))] for k in range(4)]
    return jnp.concatenate(parts, axis=-1)


def regrouped(parts):
    axis = len(parts[0].shape) - 1
    group = iota(parts[0].shape, axis) // 32
    turned = [roll(part, 32 * i, axis) for i, part in enumerate(parts)]
    out = []
    for k in range(4):
        mixed = turned[0]
        for i in range(1, 4):
            mixed = jnp.where(group == (k + i) % 4, turned[i], mixed)
        out.append(roll(mixed, -32 * k, axis))
    return out


def repeated(part):
    return regrouped([part] * 4)


def velocity_pressure(q):
    inverse = 1.0 / q[0]
    vel = [q[1] * inverse, q[2] * inverse, q[3] * inverse]
    kinetic = q[1] * vel[0] + q[2] * vel[1] + q[3] * vel[2]
    return vel, (GAMMA_GAS - 1.0) * (q[4] - 0.5 * kinetic)


def euler_flux(q, vel, pressure, k):
    flux = [q[1 + k], q[1] * vel[k], q[2] * vel[k], q[3] * vel[k], (q[4] + pressure) * vel[k]]
    flux[1 + k] = flux[1 + k] + pressure
    return flux


def z_difference(a):
    row = iota(a.shape, 1)
    up = roll(a, -1, 1)
    up = jnp.where(row == 7, roll(up, -32, 2), up)
    down = roll(a, 1, 1)
    down = jnp.where(row == 0, roll(down, 32, 2), down)
    return up - down


def y_difference(a, first_core):
    lane = iota(a.shape, 2) % 32
    up = jnp.where(lane == 31, jnp.where(first_core, 0.0, a), roll(a, -1, 2))
    down = jnp.where(lane == 0, jnp.where(first_core, a, 0.0), roll(a, 1, 2))
    return up - down


def x_difference(a, before, after):
    up = jnp.concatenate([a[1:], after], axis=0)
    down = jnp.concatenate([before, a[:-1]], axis=0)
    return up - down


def slab_kernel(
    amplitude,
    density,
    momentum,
    energy,
    normal_cell,
    spanwise_cell,
    signs,
    strengths,
    send,
    far_out,
    pair_out,
    edge_out,
):
    slab = lax.axis_index("gx")
    first_core = lax.axis_index("gy") == 0
    odd = slab % 2 == 1
    last_slab = slab == lax.axis_size("gx") - 1
    q = [packed(density)] + [packed(momentum, c) for c in range(3)] + [packed(energy)]
    vel, pressure = velocity_pressure(q)
    flux_x = euler_flux(q, vel, pressure, 0)
    flux_y = euler_flux(q, vel, pressure, 1)
    flux_z = euler_flux(q, vel, pressure, 2)
    zero = jnp.zeros((1, 8, LANES), jnp.float32)
    partial = []
    for f in range(5):
        after = jnp.where(last_slab, flux_x[f][7:], 0.0)
        change = x_difference(flux_x[f], zero, after)
        change = change + y_difference(flux_y[f], first_core)
        change = change + z_difference(flux_z[f])
        partial.append(q[f] - HALF_STEP * change)
        far_out[f] = jnp.where(odd, q[f][7], q[f][0])
        pair_out[f] = jnp.where(odd, q[f][0], q[f][7])

    lane2 = iota((8, LANES), 1)
    shift = jnp.where(first_core, LANES - 31, 0)
    sides = []
    for i, value in enumerate(flux_y + vel):
        side = jnp.zeros((8, LANES), jnp.float32)
        for x in range(8):
            side = jnp.where(lane2 % 32 == x, pltpu.roll(value[x], shift + x, 1), side)
        edge_out[i] = side
        sides.append(side)
    energy_side = roll(sides[4], 8, 1)
    sides = [jnp.where(lane2 % 32 < 8, sides[0], energy_side)] + sides[1:4]

    pick = lambda a: jnp.where(first_core, a[:, :32], a[:, 32:])
    strength = strengths[...] * amplitude
    eddies = [pick(normal_cell[...]).astype(jnp.float32), pick(spanwise_cell[...]).astype(jnp.float32)]
    for c in range(3):
        sign = (2 * signs[c : c + 1, :] - 1).astype(jnp.float32)
        eddies.append(pick(sign * strength))
    eddy_row = jnp.broadcast_to(jnp.concatenate(eddies[:4], axis=1), (8, LANES))
    eddy_rest = jnp.broadcast_to(jnp.concatenate([eddies[4]] * 4, axis=1), (8, LANES))
    cells = regrouped(partial[:4])
    energies = [regrouped([partial[4][4 * a + b] for b in range(4)]) for a in range(2)]
    faces = [regrouped([flux_x[f][x] for f in range(4)]) for x in (7, 0)]
    blank = jnp.zeros_like(eddy_rest)
    sides, ends = regrouped(sides), regrouped([blank, flux_x[4][7], flux_x[4][0], blank])
    for k in range(4):
        rows = [cells[k][x] for x in range(8)] + [e[k] for e in energies] + [a[k] for a in faces]
        rows += [sides[k], eddy_row, jnp.where(lane2 < 32, eddy_rest, ends[k])]
        for r, value in enumerate(rows):
            send[pl.ds(8 * SENT * k + r, 8, stride=SENT), :] = value


def dot_nt(a, b):
    return lax.dot_general(
        a, b, (((1,), (1,)), ((), ())), preferred_element_type=jnp.float32
    )


def halves(a):
    high = a.astype(jnp.bfloat16)
    return high, (a - high.astype(jnp.float32)).astype(jnp.bfloat16)


def span_hat(z, centre, span):
    offset = z - centre + span / 2
    offset = jnp.where(offset < 0, offset + span, jnp.where(offset >= span, offset - span, offset))
    return jnp.maximum(0.0, 1.0 - jnp.abs(offset - span / 2) * (1.0 / SIGMA_Z))


def normal_hat(y, centre):
    return jnp.maximum(0.0, 1.0 - jnp.abs(y - centre) * (1.0 / SIGMA_Y)).astype(jnp.bfloat16)


def ghost_state_rows(a, b, c):
    mom = 1.0 + a
    kinetic = mom * mom + b * b + c * c
    return [jnp.ones_like(mom), mom, b, c, 3.0 + 0.5 * kinetic]


def sensor_of(d, vort_x, vort_y, vort_z):
    squared = d * d
    total = squared + vort_x * vort_x + vort_y * vort_y + vort_z * vort_z
    return squared / (total + 4.0 * SENSOR_EPS)


def counted(sensor, dil, vort):
    row = iota((8, LANES), 0)
    levels = iota((HISTOGRAM_BINS, LANES), 0)
    values, ones = [], []
    for x in range(len(sensor)):
        for z in range(8):
            values.append(jnp.where(vort[x][z : z + 1] == row, sensor[x][z : z + 1], 0.0))
            ones.append(jnp.where(dil[x][z : z + 1] == levels, 1.0, 0.0).astype(jnp.bfloat16))
    high, low = halves(jnp.concatenate(values, axis=1))
    counts = dot_nt(jnp.concatenate([high, low], axis=0), jnp.concatenate(ones, axis=1))
    return counts[:8] + counts[8:]


def slab_bins(bins):
    base = lax.axis_index("gx") * HISTOGRAM_BINS // lax.axis_size("gx")
    return (bins - base) & (HISTOGRAM_BINS - 1)


def interior_kernel(
    density,
    momentum,
    energy,
    edge,
    dilatation_bin,
    vorticity_bin,
    switch,
    matrix,
    updated_out,
    energy_out,
    weight_out,
    ends_out,
    counts_out,
    bins_out,
    matrix_out,
    mask_out,
):
    first_core = lax.axis_index("gy") == 0
    last_slab = lax.axis_index("gx") == lax.axis_size("gx") - 1
    q = [packed(density)] + [packed(momentum, c) for c in range(3)] + [packed(energy)]
    vel, pressure = velocity_pressure(q)
    flux_x = euler_flux(q, vel, pressure, 0)
    flux_y = euler_flux(q, vel, pressure, 1)
    flux_z = euler_flux(q, vel, pressure, 2)
    zero = jnp.zeros((1, 8, LANES), jnp.float32)
    lane = iota((8, 8, LANES), 2) % 32
    halo = edge[...]

    shift = jnp.where(first_core, 31, LANES)
    sign = jnp.where(first_core, 1.0, -1.0)

    def y_whole(a, i):
        near = jnp.stack([pltpu.roll(halo[i], shift - x, 1) for x in range(8)]) * sign
        near = jnp.where(lane == jnp.where(first_core, 31, 0), near, 0.0)
        return y_difference(a, first_core) + near

    updated = []
    for f in range(5):
        after = jnp.where(last_slab, flux_x[f][7:], 0.0)
        change = x_difference(flux_x[f], zero, after)
        change = change + y_whole(flux_y[f], f) + z_difference(flux_z[f])
        updated.append(q[f] - HALF_STEP * change)
    dx = [x_difference(a, zero, jnp.where(last_slab, a[7:], 0.0)) for a in vel]
    dy = [y_whole(vel[c], 5 + c) for c in range(3)]
    dz = [z_difference(a) for a in vel]
    rates = [dx[0] + dy[1] + dz[2], dy[2] - dz[1], dz[0] - dx[2], dx[1] - dy[0]]
    sensor = sensor_of(*rates)
    mask = jnp.concatenate([switch[...].astype(jnp.float32)] * 4, axis=1)
    weight = sensor * mask[None]
    cells, weights = regrouped(updated[:4]), repeated(weight)
    for k in range(4):
        updated_out[k] = cells[k]
        weight_out[k] = weights[k]
    for a in range(2):
        energies = regrouped([updated[4][x] for x in range(4 * a, 4 * a + 4)])
        weights = regrouped([weight[x] for x in range(4 * a, 4 * a + 4)])
        for k in range(4):
            energy_out[0, k, a] = energies[k]
            energy_out[1, k, a] = weights[k]
    for i, a in enumerate(updated + rates):
        ends_out[i, 0] = a[0]
        ends_out[i, 1] = a[7]
    dil = packed(dilatation_bin)
    vort = slab_bins(packed(vorticity_bin))
    inner = range(1, 7)
    counts_out[...] = counted(
        [sensor[x] for x in inner], [dil[x] for x in inner], [vort[x] for x in inner]
    )
    for end in range(2):
        bins_out[0, end] = dil[7 * end]
        bins_out[1, end] = vort[7 * end]
    rows = jnp.concatenate([matrix[pl.ds(r, 16, stride=8), :] for r in range(8)], axis=0)
    source, target = iota((LANES, LANES), 0), iota((LANES, LANES), 1)
    order = jnp.where(source == 8 * (target % 16) + target // 16, 1.0, 0.0).astype(jnp.bfloat16)
    for i, part in enumerate(halves(rows)):
        ordered = jnp.dot(part, order, preferred_element_type=jnp.float32)
        matrix_out[i] = ordered.astype(jnp.bfloat16)
    mask_out[...] = jnp.broadcast_to(mask, (8, LANES))


def pencil_kernel(
    received,
    matrix,
    ends,
    counts_in,
    bins,
    mask,
    far,
    pair,
    send,
    updated_out,
    energy_out,
    weight_out,
    before,
):
    slab = lax.axis_index("gx")
    core = lax.axis_index("gy")
    last_slab = slab == lax.axis_size("gx") - 1
    odd = slab % 2 == 1
    plane = (slab * 2 + core).astype(jnp.float32)
    row = iota((8, LANES), 0)
    lane = iota((8, LANES), 1)
    peak = HAT_PEAK * HAT_PEAK

    def side_by_side(r, group):
        out = None
        for j in range(4):
            moved = received[pl.ds(SENT * j + r, 8, stride=4 * SENT), :]
            moved = roll(moved, 32 * (j - group), 1)
            out = moved if out is None else jnp.where(lane // 32 == j, moved, out)
        return out

    centre_y, centre_z = side_by_side(13, 0), side_by_side(13, 1)
    strength = [side_by_side(13, 2), side_by_side(13, 3), side_by_side(14, 0)]
    strength = [a * peak for a in strength]
    @pl.when(slab == 0)
    def _():
        z_all = iota((32, LANES), 0).astype(jnp.float32)
        y_own = (iota((32, LANES), 0) + core * 32).astype(jnp.float32)
        lhs, rhs = [], []
        for c in range(8):
            hat = span_hat(z_all, centre_z[c : c + 1], 32.0)
            lhs.append(jnp.concatenate([hat * a[c : c + 1] for a in strength], axis=0))
            rhs.append(normal_hat(y_own, centre_y[c : c + 1]))
        high, low = halves(jnp.concatenate(lhs, axis=1))
        own = dot_nt(jnp.concatenate([high, low], axis=0), jnp.concatenate(rhs, axis=1))
        own = own[:96] + own[96:]
        parts = [
            jnp.concatenate([own[c * 32 + 8 * k : c * 32 + 8 * k + 8] for k in range(4)], axis=1)
            for c in range(3)
        ]
        q = ghost_state_rows(*parts)
        for f in range(5):
            before[f] = q[f]

    @pl.when(slab != 0)
    def _():
        before[...] = jnp.where(odd, pair[...], far[...])

    hat = span_hat(plane, centre_z, 32.0)
    y_all = iota((64, LANES), 0).astype(jnp.float32)
    lhs, rhs = [], []
    for c in range(8):
        weighted = jnp.where(row == 1, strength[1][c : c + 1], strength[2][c : c + 1])
        weighted = jnp.where(row == 0, strength[0][c : c + 1], weighted)
        lhs.append(jnp.where(row < 3, weighted * hat[c : c + 1], 0.0))
        rhs.append(normal_hat(y_all, centre_y[c : c + 1]))
    high, low = halves(jnp.concatenate(lhs, axis=1))
    inflow = dot_nt(jnp.concatenate([high, low], axis=0), jnp.concatenate(rhs, axis=1))
    inflow = inflow[:8] + inflow[8:]
    ghost = ghost_state_rows(inflow[0:1], inflow[1:2], inflow[2:3])
    ghost_vel, ghost_pressure = velocity_pressure(ghost)
    ghost_x = euler_flux(ghost, ghost_vel, ghost_pressure, 0)

    row16 = iota((16, LANES), 0)
    lane16 = iota((16, LANES), 1)
    chunk_row = lambda r, h: received[pl.ds(SENT * h + r, 16, stride=2 * SENT), :]
    columns, energy_columns = [], []
    for h in range(2):
        target = 31 if h == 0 else 0
        side = -HALF_STEP if h == 0 else HALF_STEP
        across = side * chunk_row(12, 1 - h)
        both_ends = chunk_row(14, h)
        last_a, first_a = chunk_row(10, h), chunk_row(11, h)
        last_e, first_e = roll(both_ends, -32, 1), roll(both_ends, -64, 1)
        before_a = jnp.where(row16 == 0, 0.0, roll(last_a, 1, 0))
        before_e = jnp.where(row16 == 0, 0.0, roll(last_e, 1, 0))
        after_a = jnp.where(row16 == 15, 0.0, roll(first_a, -1, 0))
        after_e = jnp.where(row16 == 15, 0.0, roll(first_e, -1, 0))
        for r in range(8):
            a = chunk_row(r, h)
            e = roll(chunk_row(8 + r // 4, h), -32 * (r % 4), 1)
            if r == 0:
                a, e = a + HALF_STEP * before_a, e + HALF_STEP * before_e
            if r == 7:
                a, e = a - HALF_STEP * after_a, e - HALF_STEP * after_e
            a = jnp.where(lane16 % 32 == target, a + roll(across, target - r, 1), a)
            e = jnp.where(lane16 == target, e + roll(across, target - r - 8, 1), e)
            columns.append(a)
            energy_columns.append(roll(e, 32 * h, 1))
    joined = [jnp.where(lane16 < 32, energy_columns[r], energy_columns[8 + r]) for r in range(8)]
    columns = jnp.concatenate(
        [jnp.concatenate(part, axis=0) for part in (columns[:8], columns[8:], joined)], axis=1
    )
    m_high, m_low = matrix[0], matrix[1]
    c_high, c_low = halves(columns)
    smooth = (
        jnp.dot(m_high, c_high, preferred_element_type=jnp.float32)
        + jnp.dot(m_high, c_low, preferred_element_type=jnp.float32)
        + jnp.dot(m_low, c_high, preferred_element_type=jnp.float32)
    )

    first_column = (m_high[:, :1].astype(jnp.float32) + m_low[:, :1].astype(jnp.float32)) * HALF_STEP
    inflow_flux = [ghost_x[f][:, 32 * h : 32 * h + 32] for h in range(2) for f in range(4)]
    inflow_flux += [ghost_x[4], jnp.zeros((1, 64), jnp.float32)]
    smooth = smooth + first_column * jnp.concatenate(inflow_flux, axis=1)

    sensors, dils, vorts = [], [], []
    for end in range(2):
        q = [jnp.where(odd, far[f], pair[f]) if end else before[f] for f in range(5)]
        vel, pressure = velocity_pressure(q)
        flux = euler_flux(q, vel, pressure, 0)
        sign = -1.0 if end == 0 else 1.0
        add = [sign * a for a in flux + vel]
        if end == 1:
            add = [jnp.where(last_slab, 0.0, a) for a in add]
        updated = [ends[f, end] - HALF_STEP * add[f] for f in range(5)]
        rates = [ends[5 + i, end] for i in range(4)]
        rates = [rates[0] + add[5], rates[1], rates[2] - add[7], rates[3] + add[6]]
        sensor = sensor_of(*rates)
        weight = sensor * mask[...]
        cells, weights = regrouped(updated[:4]), repeated(weight)
        for k in range(4):
            updated_out[end, k] = cells[k]
            energy_out[end, k] = roll(updated[4], 32 * (3 * end - k), 1)
            weight_out[end, k] = weights[k]
        sensors.append(sensor)
        dils.append(bins[0, end])
        vorts.append(bins[1, end])
    counts = counts_in[...] + counted(sensors, dils, vorts)

    for h in range(2):
        back_row = lambda r: (pl.ds(BACK * h + r, 16, stride=2 * BACK), slice(None))
        for r in range(8):
            send[back_row(r)] = smooth[16 * r : 16 * r + 16, 128 * h : 128 * h + 128]
        for a in range(2):
            out = None
            for b in range(4):
                r = 4 * a + b
                moved = roll(smooth[16 * r : 16 * r + 16, 256:], 32 * (b - h), 1)
                out = moved if out is None else jnp.where(lane16 // 32 == b, moved, out)
            send[back_row(8 + a)] = out
        for i in range(3):
            pair_of_bins = jnp.concatenate([counts[2 * i : 2 * i + 1], counts[2 * i + 1 : 2 * i + 2]], axis=1)
            send[back_row(10 + i)] = jnp.broadcast_to(pair_of_bins, (16, LANES))


def final_kernel(
    scale,
    received,
    updated,
    energy,
    weight,
    end_updated,
    end_energy,
    end_weight,
    conserved,
    histogram,
    totals,
):
    group = iota((8, LANES), 1) // 32
    for k in range(4):
        planes = pl.ds(8 * k, 8)
        chunk_row = lambda r: received[pl.ds(8 * BACK * k + r, 8, stride=BACK), :]
        for x in range(8):
            if x in (0, 7):
                u, w = end_updated[x // 7, k], end_weight[x // 7, k]
            else:
                u, w = updated[k, x], weight[k, x]
            result = u + w * (chunk_row(x) - u)
            for f in range(4):
                conserved[f, x, planes, :] = result[:, 32 * f : 32 * f + 32]
        for a in range(2):
            ours = group == 3 * a
            u = jnp.where(ours, end_energy[a, k], energy[0, k, a])
            w = jnp.where(ours, end_weight[a, k], energy[1, k, a])
            result = u + w * (chunk_row(8 + a) - u)
            for b in range(4):
                conserved[4, 4 * a + b, planes, :] = result[:, 32 * b : 32 * b + 32]

    bins = []
    for i in range(3):
        both = [received[pl.ds(BACK * h + 10 + i, 16, stride=2 * BACK), :] for h in range(2)]
        bins.append(both[0] + both[1])
    first = bins[0] + roll(bins[2], 1, 0)
    for c, part in enumerate((first, roll(bins[0], 64, 1), bins[1], roll(bins[1], 64, 1))):
        totals[pl.ds(c, 16, stride=4), :] = part
    histogram[...] = totals[:, :64].T * scale


def shards(
    density,
    momentum,
    energy,
    eddy_normal_cell,
    eddy_spanwise_cell,
    eddy_signs,
    eddy_strengths,
    filter_matrices,
    shock_switch,
    dilatation_bin,
    vorticity_bin,
):
    slabs, cores = lax.axis_size("gx"), lax.axis_size("gy")
    shapes = (density.shape, eddy_strengths.shape, filter_matrices.shape, slabs, cores)
    if shapes != ((8, 32, 32), (64,), (1, 128, 128), 16, 2):
        return general_shards(
            density,
            momentum,
            energy,
            eddy_normal_cell,
            eddy_spanwise_cell,
            eddy_signs,
            eddy_strengths,
            filter_matrices,
            shock_switch,
            dilatation_bin,
            vorticity_bin,
        )
    cells_x, span, cells_y = density.shape
    total_y = cells_y * cores
    total_eddies = eddy_strengths.shape[0] * slabs
    amplitude = math.sqrt(total_y * span / (total_eddies * SIGMA_Y * SIGMA_Z))
    plane = jax.ShapeDtypeStruct((5, 8, LANES), jnp.float32)
    cells = (8, 8, LANES)
    f32 = lambda *shape: jax.ShapeDtypeStruct(shape, jnp.float32)
    vmem = lambda *shape: pltpu.VMEM(shape, jnp.float32)
    near = lambda a: pltpu.with_memory_space_constraint(a, pltpu.VMEM)
    send, far, pair, edge = pl.pallas_call(
        lambda *refs: slab_kernel(amplitude, *refs),
        out_shape=[vmem(32 * SENT, LANES), vmem(5, 8, LANES), vmem(5, 8, LANES), vmem(*cells)],
        name="slab",
    )(
        density,
        momentum,
        energy,
        eddy_normal_cell.reshape(1, -1),
        eddy_spanwise_cell.reshape(1, -1),
        eddy_signs.T,
        eddy_strengths.reshape(1, -1),
    )
    received = lax.all_to_all(send.reshape(32, SENT, 1, LANES), ("gx", "gy"), 0, 0, tiled=True)
    both = lambda first: [p for i in range(first, slabs - 1, 2) for p in ((i, i + 1), (i + 1, i))]
    far = lax.ppermute(far, "gx", both(1))
    pair = lax.ppermute(pair, "gx", both(0))
    other_edge = lax.ppermute(edge, "gy", [(0, 1), (1, 0)])
    updated, updated_energy, weight, ends, counts, bins, matrix, mask = pl.pallas_call(
        interior_kernel,
        out_shape=[
            vmem(4, *cells),
            vmem(2, 4, 2, 8, LANES),
            vmem(4, *cells),
            vmem(9, 2, 8, LANES),
            vmem(8, 64),
            pltpu.VMEM((2, 2, 8, LANES), jnp.int32),
            pltpu.VMEM((2, *filter_matrices.shape[1:]), jnp.bfloat16),
            vmem(8, LANES),
        ],
        cost_estimate=pl.CostEstimate(flops=10_000_000, bytes_accessed=2_000_000, transcendentals=0),
        name="interior",
    )(
        density,
        momentum,
        energy,
        near(other_edge),
        dilatation_bin,
        vorticity_bin,
        shock_switch,
        filter_matrices[0],
    )
    send, *end_rows = pl.pallas_call(
        pencil_kernel,
        out_shape=[vmem(32 * BACK, LANES)] + [vmem(2, 4, 8, LANES)] * 3,
        scratch_shapes=[pltpu.VMEM((5, 8, LANES), jnp.float32)],
        name="pencil",
    )(
        near(received.reshape(32 * SENT, LANES)),
        *map(near, (matrix, ends, counts, bins, mask, far, pair)),
    )
    received = lax.all_to_all(send.reshape(32, BACK, 1, LANES), ("gx", "gy"), 0, 0, tiled=True)
    scale = HISTOGRAM_BINS * HISTOGRAM_BINS / (cells_x * slabs * span * total_y)
    conserved_next, histogram = pl.pallas_call(
        lambda *refs: final_kernel(scale, *refs),
        out_shape=[f32(5, cells_x, span, cells_y), f32(HISTOGRAM_BINS, HISTOGRAM_BINS)],
        scratch_shapes=[vmem(HISTOGRAM_BINS, LANES)],
        name="final",
    )(
        near(received.reshape(32 * BACK, LANES)),
        *map(near, (updated, updated_energy, weight, *end_rows)),
    )
    return (conserved_next, histogram)


def solution(mesh):
    in_specs = (
        P("gx", None, "gy"),
        P(None, "gx", None, "gy"),
        P("gx", None, "gy"),
        P("gx"),
        P("gx"),
        P("gx", None),
        P("gx"),
        P(),
        P(None, "gy"),
        P("gx", None, "gy"),
        P("gx", None, "gy"),
    )
    out_specs = (P(None, "gx", None, "gy"), P())
    return jax.shard_map(shards, mesh=mesh, in_specs=in_specs, out_specs=out_specs, check_vma=False)
```

```python
import math

import jax
import jax.numpy as jnp
from jax import lax
from jax.experimental import pallas as pl
from jax.experimental.pallas import tpu as pltpu
from jax.sharding import PartitionSpec as P

HISTOGRAM_BINS = 64
SIGMA_Y = 32
SIGMA_Z = 8


TIME_STEP = 0.1
GAMMA_GAS = 1.4
SENSOR_EPS = 0.1
HAT_PEAK = math.sqrt(1.5)


def extended(x, sides, width):
    for axis, dim in sides:
        size, length = (lax.axis_size(axis), x.shape[dim])
        up = [(i, (i + 1) % size) for i in range(size - 1)]
        down = [(j, i) for i, j in up]
        last = lax.slice_in_dim(x, length - width, length, axis=dim)
        first = lax.slice_in_dim(x, 0, width, axis=dim)
        before = lax.ppermute(last, axis, up)
        after = lax.ppermute(first, axis, down)
        x = jnp.concatenate([before, x, after], axis=dim)
    return x


def hat_shape(centres, coords, spread, period):
    offset = coords[None, :] - centres[:, None]
    if period > 0:
        offset = jnp.mod(offset + period / 2, period) - period / 2
    return HAT_PEAK * jnp.maximum(0.0, 1.0 - jnp.abs(offset) / spread)


def inflow_from(centre_y, centre_z, eddy_weight, coords_y, coords_z, span):
    shape_y = hat_shape(centre_y, coords_y, float(SIGMA_Y), 0)
    shape_z = hat_shape(centre_z, coords_z, float(SIGMA_Z), span)
    weighted = (eddy_weight[:, :, None] * shape_z[:, None, :]).reshape(eddy_weight.shape[0], -1)
    inflow = jnp.dot(weighted.T, shape_y, precision=lax.Precision.HIGHEST)
    return inflow.reshape(3, coords_z.shape[0], coords_y.shape[0])


def ghost_state(inflow):
    mom_x = 1.0 + inflow[0]
    kinetic = mom_x * mom_x + inflow[1] * inflow[1] + inflow[2] * inflow[2]
    return jnp.stack([jnp.ones_like(mom_x), mom_x, inflow[1], inflow[2], 3.0 + 0.5 * kinetic])


def flux_of(fields, velocity, pressure, direction):
    result = fields * velocity[direction][None]
    result = result.at[1 + direction].add(pressure)
    return result.at[4].add(pressure * velocity[direction])


def central_x(values):
    return (values[..., 2:, :, 1:-1] - values[..., :-2, :, 1:-1]) * 0.5


def central_y(values):
    return (values[..., 1:-1, :, 2:] - values[..., 1:-1, :, :-2]) * 0.5


def central_z(values):
    centre = values[..., 1:-1, :, 1:-1]
    return (jnp.roll(centre, -1, axis=-2) - jnp.roll(centre, 1, axis=-2)) * 0.5


def section_rhs(padded):
    velocity = padded[1:4] / padded[0][None]
    pressure = (GAMMA_GAS - 1.0) * (padded[4] - 0.5 * jnp.sum(padded[1:4] * velocity, axis=0))
    change = central_x(flux_of(padded, velocity, pressure, 0))
    change = change + central_y(flux_of(padded, velocity, pressure, 1))
    change = change + central_z(flux_of(padded, velocity, pressure, 2))
    updated = padded[:, 1:-1, :, 1:-1] - TIME_STEP * change
    dilatation = central_x(velocity[0]) + central_y(velocity[1]) + central_z(velocity[2])
    vort_x = central_y(velocity[2]) - central_z(velocity[1])
    vort_y = central_z(velocity[0]) - central_x(velocity[2])
    vort_z = central_x(velocity[1]) - central_y(velocity[0])
    squared = dilatation * dilatation
    shock_sensor = squared / (
        squared + vort_x * vort_x + vort_y * vort_y + vort_z * vort_z + SENSOR_EPS
    )
    return (updated, shock_sensor)


def filter_lines(pencil, filter_matrices):
    block_count, block_len = (filter_matrices.shape[0], filter_matrices.shape[1])
    lanes = pencil.shape[2]
    blocks = pencil.reshape(5, block_count, block_len, lanes)
    smooth = jnp.einsum("bij,fbjp->fbip", filter_matrices, blocks, precision=lax.Precision.HIGHEST)
    return smooth.reshape(5, block_count * block_len, lanes)


def plane_histogram(shock_sensor, dilatation_bin, vorticity_bin):
    bin_levels = jnp.arange(HISTOGRAM_BINS, dtype=jnp.int32)

    def accumulate_plane(histogram_totals, histogram_parts):
        sensor_plane, plane_dilatation, plane_vorticity = histogram_parts
        flat_sensor = sensor_plane.reshape(-1)
        dilatation_table = (plane_dilatation.reshape(-1)[None, :] == bin_levels[:, None]).astype(
            jnp.float32
        )
        vorticity_table = jnp.where(
            plane_vorticity.reshape(-1)[:, None] == bin_levels[None, :], flat_sensor[:, None], 0.0
        )
        return (
            histogram_totals
            + jnp.dot(dilatation_table, vorticity_table, precision=lax.Precision.HIGHEST),
            None,
        )

    histogram_totals, _ = lax.scan(
        accumulate_plane,
        jnp.zeros((HISTOGRAM_BINS, HISTOGRAM_BINS), jnp.float32),
        (shock_sensor, dilatation_bin, vorticity_bin),
    )
    return histogram_totals


def general_shards(
    density,
    momentum,
    energy,
    eddy_normal_cell,
    eddy_spanwise_cell,
    eddy_signs,
    eddy_strengths,
    filter_matrices,
    shock_switch,
    dilatation_bin,
    vorticity_bin,
):
    cells_x, span, cells_y = density.shape
    slab_index = lax.axis_index("gx")
    block_index = lax.axis_index("gy")
    slab_count = lax.axis_size("gx")
    fields = jnp.concatenate([density[None], momentum, energy[None]], axis=0)
    total_y = cells_y * lax.axis_size("gy")
    total_eddies = eddy_normal_cell.shape[0] * slab_count
    amplitude = math.sqrt(total_y * span / (total_eddies * SIGMA_Y * SIGMA_Z))
    eddy_weight = (2 * eddy_signs - 1).astype(jnp.float32) * eddy_strengths[:, None] * amplitude
    coords_y = (block_index * cells_y + jnp.arange(cells_y, dtype=jnp.int32)).astype(jnp.float32)
    coords_z = jnp.arange(span, dtype=jnp.int32).astype(jnp.float32)
    partial_sum = inflow_from(
        eddy_normal_cell.astype(jnp.float32),
        eddy_spanwise_cell.astype(jnp.float32),
        eddy_weight,
        coords_y,
        coords_z,
        span,
    )
    inflow = lax.psum(partial_sum, "gx")
    ghost_cells = ghost_state(inflow)
    padded = extended(fields, (("gx", 1), ("gy", 3)), 1)
    padded = padded.at[:, 0, :, 1:-1].set(
        jnp.where(slab_index == 0, ghost_cells, padded[:, 0, :, 1:-1])
    )
    padded = padded.at[:, -1, :, 1:-1].set(
        jnp.where(slab_index == slab_count - 1, fields[:, -1], padded[:, -1, :, 1:-1])
    )
    padded = padded.at[:, 1:-1, :, 0].set(
        jnp.where(block_index == 0, fields[:, :, :, 0], padded[:, 1:-1, :, 0])
    )
    padded = padded.at[:, 1:-1, :, -1].set(
        jnp.where(
            block_index == lax.axis_size("gy") - 1, fields[:, :, :, -1], padded[:, 1:-1, :, -1]
        )
    )
    updated, shock_sensor = section_rhs(padded)
    block_len = filter_matrices.shape[1]
    filter_row = slab_index * cells_x // block_len
    mask_row = lax.dynamic_slice_in_dim(shock_switch, filter_row, 1, 0).astype(jnp.float32)
    weight = mask_row[None] * shock_sensor
    columns = span * cells_y
    stacked = updated.reshape(5, cells_x, columns)
    weight_flat = weight.reshape(1, cells_x, columns)
    pencil, pencil_weight = (
        lax.all_to_all(stacked, "gx", split_axis=2, concat_axis=1, tiled=True),
        lax.all_to_all(weight_flat, "gx", split_axis=2, concat_axis=1, tiled=True),
    )
    smooth = filter_lines(pencil, filter_matrices)
    returned = pencil + pencil_weight * (smooth - pencil)
    back_lines = lax.all_to_all(returned, "gx", split_axis=1, concat_axis=2, tiled=True)
    conserved_next = back_lines.reshape(5, cells_x, span, cells_y)
    partial_histogram = plane_histogram(shock_sensor, dilatation_bin, vorticity_bin)
    summed = lax.psum(partial_histogram, ("gx", "gy"))
    all_cells = cells_x * slab_count * span * total_y
    histogram = summed * (HISTOGRAM_BINS * HISTOGRAM_BINS / all_cells)
    return (conserved_next, histogram)


LANES = 128
SENT = 14
BACK = 13
HALF_STEP = 0.5 * TIME_STEP


def iota(shape, dim):
    return lax.broadcasted_iota(jnp.int32, shape, dim)


def roll(x, shift, axis):
    shift %= x.shape[axis]
    return x if shift == 0 else pltpu.roll(x, shift, axis)


def packed(ref, *lead):
    lead = lead if len(lead) == len(ref.shape) - 2 else (*lead, slice(None))
    parts = [ref[(*lead, pl.ds(8 * k, 8), slice(None))] for k in range(4)]
    return jnp.concatenate(parts, axis=-1)


def regrouped(parts):
    axis = len(parts[0].shape) - 1
    group = iota(parts[0].shape, axis) // 32
    turned = [roll(part, 32 * i, axis) for i, part in enumerate(parts)]
    out = []
    for k in range(4):
        mixed = turned[0]
        for i in range(1, 4):
            mixed = jnp.where(group == (k + i) % 4, turned[i], mixed)
        out.append(roll(mixed, -32 * k, axis))
    return out


def repeated(part):
    return regrouped([part] * 4)


def velocity_pressure(q):
    inverse = 1.0 / q[0]
    vel = [q[1] * inverse, q[2] * inverse, q[3] * inverse]
    kinetic = q[1] * vel[0] + q[2] * vel[1] + q[3] * vel[2]
    return vel, (GAMMA_GAS - 1.0) * (q[4] - 0.5 * kinetic)


def euler_flux(q, vel, pressure, k):
    flux = [q[1 + k], q[1] * vel[k], q[2] * vel[k], q[3] * vel[k], (q[4] + pressure) * vel[k]]
    flux[1 + k] = flux[1 + k] + pressure
    return flux


def z_difference(a):
    row = iota(a.shape, 1)
    up = roll(a, -1, 1)
    up = jnp.where(row == 7, roll(up, -32, 2), up)
    down = roll(a, 1, 1)
    down = jnp.where(row == 0, roll(down, 32, 2), down)
    return up - down


def y_difference(a, first_core):
    lane = iota(a.shape, 2) % 32
    up = jnp.where(lane == 31, jnp.where(first_core, 0.0, a), roll(a, -1, 2))
    down = jnp.where(lane == 0, jnp.where(first_core, a, 0.0), roll(a, 1, 2))
    return up - down


def x_difference(a, before, after):
    up = jnp.concatenate([a[1:], after], axis=0)
    down = jnp.concatenate([before, a[:-1]], axis=0)
    return up - down


def slab_kernel(
    amplitude,
    density,
    momentum,
    energy,
    normal_cell,
    spanwise_cell,
    signs,
    strengths,
    send,
    far_out,
    pair_out,
    edge_out,
):
    slab = lax.axis_index("gx")
    first_core = lax.axis_index("gy") == 0
    odd = slab % 2 == 1
    last_slab = slab == lax.axis_size("gx") - 1
    q = [packed(density)] + [packed(momentum, c) for c in range(3)] + [packed(energy)]
    vel, pressure = velocity_pressure(q)
    flux_x = euler_flux(q, vel, pressure, 0)
    flux_y = euler_flux(q, vel, pressure, 1)
    flux_z = euler_flux(q, vel, pressure, 2)
    zero = jnp.zeros((1, 8, LANES), jnp.float32)
    partial = []
    for f in range(5):
        after = jnp.where(last_slab, flux_x[f][7:], 0.0)
        change = x_difference(flux_x[f], zero, after)
        change = change + y_difference(flux_y[f], first_core)
        change = change + z_difference(flux_z[f])
        partial.append(q[f] - HALF_STEP * change)
        far_out[f] = jnp.where(odd, q[f][7], q[f][0])
        pair_out[f] = jnp.where(odd, q[f][0], q[f][7])

    lane2 = iota((8, LANES), 1)
    shift = jnp.where(first_core, LANES - 31, 0)
    sides = []
    for i, value in enumerate(flux_y + vel):
        side = jnp.zeros((8, LANES), jnp.float32)
        for x in range(8):
            side = jnp.where(lane2 % 32 == x, pltpu.roll(value[x], shift + x, 1), side)
        edge_out[i] = side
        sides.append(side)
    across = jnp.zeros((8, LANES), jnp.float32)
    for f in range(5):
        mine = (lane2 % 32 >= 6 * f) & (lane2 % 32 < 6 * f + 6)
        across = jnp.where(mine, roll(sides[f], 6 * f - 1, 1), across)
    corner = lane2 % 32 == jnp.where(first_core, 31, 0)
    end_rows = [[jnp.where(corner, q[f][x], flux_x[f][x]) for f in range(5)] for x in (7, 0)]

    pick = lambda a: jnp.where(first_core, a[:, :32], a[:, 32:])
    strength = strengths[...] * amplitude
    eddies = [pick(normal_cell[...]).astype(jnp.float32), pick(spanwise_cell[...]).astype(jnp.float32)]
    for c in range(3):
        sign = (2 * signs[c : c + 1, :] - 1).astype(jnp.float32)
        eddies.append(pick(sign * strength))
    eddy_row = jnp.broadcast_to(jnp.concatenate(eddies[:4], axis=1), (8, LANES))
    eddy_rest = jnp.broadcast_to(jnp.concatenate([eddies[4]] * 4, axis=1), (8, LANES))
    cells = regrouped(partial[:4])
    energies = [regrouped([partial[4][4 * a + b] for b in range(4)]) for a in range(2)]
    faces = [regrouped(a[:4]) for a in end_rows]
    blank = jnp.zeros_like(eddy_rest)
    ends = regrouped([blank, end_rows[0][4], end_rows[1][4], across])
    for k in range(4):
        rows = [cells[k][x] for x in range(8)] + [e[k] for e in energies] + [a[k] for a in faces]
        rows += [eddy_row, jnp.where(lane2 < 32, eddy_rest, ends[k])]
        for r, value in enumerate(rows):
            send[pl.ds(8 * SENT * k + r, 8, stride=SENT), :] = value


def dot_nt(a, b):
    return lax.dot_general(
        a, b, (((1,), (1,)), ((), ())), preferred_element_type=jnp.float32
    )


def halves(a):
    high = a.astype(jnp.bfloat16)
    return high, (a - high.astype(jnp.float32)).astype(jnp.bfloat16)


def span_hat(z, centre, span):
    offset = z - centre + span / 2
    offset = jnp.where(offset < 0, offset + span, jnp.where(offset >= span, offset - span, offset))
    return jnp.maximum(0.0, 1.0 - jnp.abs(offset - span / 2) * (1.0 / SIGMA_Z))


def normal_hat(y, centre):
    return jnp.maximum(0.0, 1.0 - jnp.abs(y - centre) * (1.0 / SIGMA_Y)).astype(jnp.bfloat16)


def ghost_state_rows(a, b, c):
    mom = 1.0 + a
    kinetic = mom * mom + b * b + c * c
    return [jnp.ones_like(mom), mom, b, c, 3.0 + 0.5 * kinetic]


def sensor_of(d, vort_x, vort_y, vort_z):
    squared = d * d
    total = squared + vort_x * vort_x + vort_y * vort_y + vort_z * vort_z
    return squared / (total + 4.0 * SENSOR_EPS)


def counted(sensor, dil, vort):
    row = iota((8, LANES), 0)
    levels = iota((HISTOGRAM_BINS, LANES), 0)
    values, ones = [], []
    for x in range(len(sensor)):
        for z in range(8):
            values.append(jnp.where(vort[x][z : z + 1] == row, sensor[x][z : z + 1], 0.0))
            ones.append(jnp.where(dil[x][z : z + 1] == levels, 1.0, 0.0).astype(jnp.bfloat16))
    high, low = halves(jnp.concatenate(values, axis=1))
    counts = dot_nt(jnp.concatenate([high, low], axis=0), jnp.concatenate(ones, axis=1))
    return counts[:8] + counts[8:]


def slab_bins(bins):
    base = lax.axis_index("gx") * HISTOGRAM_BINS // lax.axis_size("gx")
    return (bins - base) & (HISTOGRAM_BINS - 1)


def interior_kernel(
    density,
    momentum,
    energy,
    edge,
    dilatation_bin,
    vorticity_bin,
    switch,
    matrix,
    updated_out,
    energy_out,
    weight_out,
    ends_out,
    counts_out,
    bins_out,
    matrix_out,
    mask_out,
):
    first_core = lax.axis_index("gy") == 0
    last_slab = lax.axis_index("gx") == lax.axis_size("gx") - 1
    q = [packed(density)] + [packed(momentum, c) for c in range(3)] + [packed(energy)]
    vel, pressure = velocity_pressure(q)
    flux_x = euler_flux(q, vel, pressure, 0)
    flux_y = euler_flux(q, vel, pressure, 1)
    flux_z = euler_flux(q, vel, pressure, 2)
    zero = jnp.zeros((1, 8, LANES), jnp.float32)
    lane = iota((8, 8, LANES), 2) % 32
    halo = edge[...]

    shift = jnp.where(first_core, 31, LANES)
    sign = jnp.where(first_core, 1.0, -1.0)

    def y_whole(a, i):
        near = jnp.stack([pltpu.roll(halo[i], shift - x, 1) for x in range(8)]) * sign
        near = jnp.where(lane == jnp.where(first_core, 31, 0), near, 0.0)
        return y_difference(a, first_core) + near

    updated = []
    for f in range(5):
        after = jnp.where(last_slab, flux_x[f][7:], 0.0)
        change = x_difference(flux_x[f], zero, after)
        change = change + y_whole(flux_y[f], f) + z_difference(flux_z[f])
        updated.append(q[f] - HALF_STEP * change)
    dx = [x_difference(a, zero, jnp.where(last_slab, a[7:], 0.0)) for a in vel]
    dy = [y_whole(vel[c], 5 + c) for c in range(3)]
    dz = [z_difference(a) for a in vel]
    rates = [dx[0] + dy[1] + dz[2], dy[2] - dz[1], dz[0] - dx[2], dx[1] - dy[0]]
    sensor = sensor_of(*rates)
    mask = jnp.concatenate([switch[...].astype(jnp.float32)] * 4, axis=1)
    weight = sensor * mask[None]
    cells, weights = regrouped(updated[:4]), repeated(weight)
    for k in range(4):
        updated_out[k] = cells[k]
        weight_out[k] = weights[k]
    for a in range(2):
        energies = regrouped([updated[4][x] for x in range(4 * a, 4 * a + 4)])
        weights = regrouped([weight[x] for x in range(4 * a, 4 * a + 4)])
        for k in range(4):
            energy_out[0, k, a] = energies[k]
            energy_out[1, k, a] = weights[k]
    for i, a in enumerate(updated + rates):
        ends_out[i, 0] = a[0]
        ends_out[i, 1] = a[7]
    dil = packed(dilatation_bin)
    vort = slab_bins(packed(vorticity_bin))
    inner = range(1, 7)
    counts_out[...] = counted(
        [sensor[x] for x in inner], [dil[x] for x in inner], [vort[x] for x in inner]
    )
    for end in range(2):
        bins_out[0, end] = dil[7 * end]
        bins_out[1, end] = vort[7 * end]
    rows = jnp.concatenate([matrix[pl.ds(r, 16, stride=8), :] for r in range(8)], axis=0)
    source, target = iota((LANES, LANES), 0), iota((LANES, LANES), 1)
    order = jnp.where(source == 8 * (target % 16) + target // 16, 1.0, 0.0).astype(jnp.bfloat16)
    for i, part in enumerate(halves(rows)):
        ordered = jnp.dot(part, order, preferred_element_type=jnp.float32)
        matrix_out[i] = ordered.astype(jnp.bfloat16)
    mask_out[...] = jnp.broadcast_to(mask, (8, LANES))


def pencil_kernel(
    received,
    matrix,
    ends,
    counts_in,
    bins,
    mask,
    far,
    pair,
    send,
    updated_out,
    energy_out,
    weight_out,
    before,
):
    slab = lax.axis_index("gx")
    core = lax.axis_index("gy")
    last_slab = slab == lax.axis_size("gx") - 1
    odd = slab % 2 == 1
    plane = (slab * 2 + core).astype(jnp.float32)
    row = iota((8, LANES), 0)
    lane = iota((8, LANES), 1)
    peak = HAT_PEAK * HAT_PEAK

    def side_by_side(r, group):
        out = None
        for j in range(4):
            moved = received[pl.ds(SENT * j + r, 8, stride=4 * SENT), :]
            moved = roll(moved, 32 * (j - group), 1)
            out = moved if out is None else jnp.where(lane // 32 == j, moved, out)
        return out

    centre_y, centre_z = side_by_side(12, 0), side_by_side(12, 1)
    strength = [side_by_side(12, 2), side_by_side(12, 3), side_by_side(13, 0)]
    strength = [a * peak for a in strength]
    @pl.when(slab == 0)
    def _():
        z_all = iota((32, LANES), 0).astype(jnp.float32)
        y_own = (iota((32, LANES), 0) + core * 32).astype(jnp.float32)
        lhs, rhs = [], []
        for c in range(8):
            hat = span_hat(z_all, centre_z[c : c + 1], 32.0)
            lhs.append(jnp.concatenate([hat * a[c : c + 1] for a in strength], axis=0))
            rhs.append(normal_hat(y_own, centre_y[c : c + 1]))
        high, low = halves(jnp.concatenate(lhs, axis=1))
        own = dot_nt(jnp.concatenate([high, low], axis=0), jnp.concatenate(rhs, axis=1))
        own = own[:96] + own[96:]
        parts = [
            jnp.concatenate([own[c * 32 + 8 * k : c * 32 + 8 * k + 8] for k in range(4)], axis=1)
            for c in range(3)
        ]
        q = ghost_state_rows(*parts)
        for f in range(5):
            before[f] = q[f]

    @pl.when(slab != 0)
    def _():
        before[...] = jnp.where(odd, pair[...], far[...])

    hat = span_hat(plane, centre_z, 32.0)
    y_all = iota((64, LANES), 0).astype(jnp.float32)
    lhs, rhs = [], []
    for c in range(8):
        weighted = jnp.where(row == 1, strength[1][c : c + 1], strength[2][c : c + 1])
        weighted = jnp.where(row == 0, strength[0][c : c + 1], weighted)
        lhs.append(jnp.where(row < 3, weighted * hat[c : c + 1], 0.0))
        rhs.append(normal_hat(y_all, centre_y[c : c + 1]))
    high, low = halves(jnp.concatenate(lhs, axis=1))
    inflow = dot_nt(jnp.concatenate([high, low], axis=0), jnp.concatenate(rhs, axis=1))
    inflow = inflow[:8] + inflow[8:]
    ghost = ghost_state_rows(inflow[0:1], inflow[1:2], inflow[2:3])
    ghost_vel, ghost_pressure = velocity_pressure(ghost)
    ghost_x = euler_flux(ghost, ghost_vel, ghost_pressure, 0)

    row16 = iota((16, LANES), 0)
    lane16 = iota((16, LANES), 1)
    chunk_row = lambda r, h: received[pl.ds(SENT * h + r, 16, stride=2 * SENT), :]
    edges = (31, 0)
    ends_a, ends_e, corners = [], [], []
    for h in range(2):
        rest = chunk_row(13, h)
        for end in range(2):
            a, e = chunk_row(10 + end, h), roll(rest, -32 * (1 + end), 1)
            q = [roll(a, -32 * f, 1) for f in range(4)] + [e]
            vel, pressure = velocity_pressure(q)
            flux = euler_flux(q, vel, pressure, 0)
            for f in range(4):
                a = jnp.where(lane16 == 32 * f + edges[h], roll(flux[f], 32 * f, 1), a)
            ends_a.append(a)
            ends_e.append(jnp.where(lane16 == edges[h], flux[4], e))
            flux = euler_flux(q, vel, pressure, 1)
            four = flux[0]
            for f in range(1, 4):
                four = jnp.where(lane16 // 32 == f, roll(flux[f], 32 * f, 1), four)
            corners.append((four, flux[4]))
    columns, energy_columns = [], []
    for h in range(2):
        target, other = edges[h], edges[1 - h]
        side = -HALF_STEP if h == 0 else HALF_STEP
        across = chunk_row(13, 1 - h)
        across_a = roll(across, -96, 1)
        for f in range(1, 4):
            across_a = jnp.where(lane16 // 32 == f, roll(across, 26 * f - 96, 1), across_a)
        before_a = jnp.where(row16 == 0, 0.0, roll(ends_a[2 * h], 1, 0))
        before_e = jnp.where(row16 == 0, 0.0, roll(ends_e[2 * h], 1, 0))
        after_a = jnp.where(row16 == 15, 0.0, roll(ends_a[2 * h + 1], -1, 0))
        after_e = jnp.where(row16 == 15, 0.0, roll(ends_e[2 * h + 1], -1, 0))
        for r in range(8):
            a = chunk_row(r, h)
            e = roll(chunk_row(8 + r // 4, h), -32 * (r % 4), 1)
            if r == 0:
                a, e = a + HALF_STEP * before_a, e + HALF_STEP * before_e
            if r == 7:
                a, e = a - HALF_STEP * after_a, e - HALF_STEP * after_e
            if r in (0, 7):
                moved_a, moved_e = corners[2 * (1 - h) + (1 if r == 0 else 0)]
                shift_a, shift_e = target - other, target - other
            else:
                moved_a, moved_e = across_a, across
                shift_a, shift_e = target - (r - 1), target - (120 + r - 1)
            a = jnp.where(lane16 % 32 == target, a + side * roll(moved_a, shift_a, 1), a)
            e = jnp.where(lane16 == target, e + side * roll(moved_e, shift_e, 1), e)
            columns.append(a)
            energy_columns.append(roll(e, 32 * h, 1))
    joined = [jnp.where(lane16 < 32, energy_columns[r], energy_columns[8 + r]) for r in range(8)]
    columns = jnp.concatenate(
        [jnp.concatenate(part, axis=0) for part in (columns[:8], columns[8:], joined)], axis=1
    )
    m_high, m_low = matrix[0], matrix[1]
    c_high, c_low = halves(columns)
    smooth = (
        jnp.dot(m_high, c_high, preferred_element_type=jnp.float32)
        + jnp.dot(m_high, c_low, preferred_element_type=jnp.float32)
        + jnp.dot(m_low, c_high, preferred_element_type=jnp.float32)
    )

    first_column = (m_high[:, :1].astype(jnp.float32) + m_low[:, :1].astype(jnp.float32)) * HALF_STEP
    inflow_flux = [ghost_x[f][:, 32 * h : 32 * h + 32] for h in range(2) for f in range(4)]
    inflow_flux += [ghost_x[4], jnp.zeros((1, 64), jnp.float32)]
    smooth = smooth + first_column * jnp.concatenate(inflow_flux, axis=1)

    sensors, dils, vorts = [], [], []
    for end in range(2):
        q = [jnp.where(odd, far[f], pair[f]) if end else before[f] for f in range(5)]
        vel, pressure = velocity_pressure(q)
        flux = euler_flux(q, vel, pressure, 0)
        sign = -1.0 if end == 0 else 1.0
        add = [sign * a for a in flux + vel]
        if end == 1:
            add = [jnp.where(last_slab, 0.0, a) for a in add]
        updated = [ends[f, end] - HALF_STEP * add[f] for f in range(5)]
        rates = [ends[5 + i, end] for i in range(4)]
        rates = [rates[0] + add[5], rates[1], rates[2] - add[7], rates[3] + add[6]]
        sensor = sensor_of(*rates)
        weight = sensor * mask[...]
        cells, weights = regrouped(updated[:4]), repeated(weight)
        for k in range(4):
            updated_out[end, k] = cells[k]
            energy_out[end, k] = roll(updated[4], 32 * (3 * end - k), 1)
            weight_out[end, k] = weights[k]
        sensors.append(sensor)
        dils.append(bins[0, end])
        vorts.append(bins[1, end])
    counts = counts_in[...] + counted(sensors, dils, vorts)

    for h in range(2):
        back_row = lambda r: (pl.ds(BACK * h + r, 16, stride=2 * BACK), slice(None))
        for r in range(8):
            send[back_row(r)] = smooth[16 * r : 16 * r + 16, 128 * h : 128 * h + 128]
        for a in range(2):
            out = None
            for b in range(4):
                r = 4 * a + b
                moved = roll(smooth[16 * r : 16 * r + 16, 256:], 32 * (b - h), 1)
                out = moved if out is None else jnp.where(lane16 // 32 == b, moved, out)
            send[back_row(8 + a)] = out
        for i in range(3):
            pair_of_bins = jnp.concatenate([counts[2 * i : 2 * i + 1], counts[2 * i + 1 : 2 * i + 2]], axis=1)
            send[back_row(10 + i)] = jnp.broadcast_to(pair_of_bins, (16, LANES))


def final_kernel(
    scale,
    received,
    updated,
    energy,
    weight,
    end_updated,
    end_energy,
    end_weight,
    conserved,
    histogram,
    totals,
):
    group = iota((8, LANES), 1) // 32
    for k in range(4):
        planes = pl.ds(8 * k, 8)
        chunk_row = lambda r: received[pl.ds(8 * BACK * k + r, 8, stride=BACK), :]
        for x in range(8):
            if x in (0, 7):
                u, w = end_updated[x // 7, k], end_weight[x // 7, k]
            else:
                u, w = updated[k, x], weight[k, x]
            result = u + w * (chunk_row(x) - u)
            for f in range(4):
                conserved[f, x, planes, :] = result[:, 32 * f : 32 * f + 32]
        for a in range(2):
            ours = group == 3 * a
            u = jnp.where(ours, end_energy[a, k], energy[0, k, a])
            w = jnp.where(ours, end_weight[a, k], energy[1, k, a])
            result = u + w * (chunk_row(8 + a) - u)
            for b in range(4):
                conserved[4, 4 * a + b, planes, :] = result[:, 32 * b : 32 * b + 32]

    bins = []
    for i in range(3):
        both = [received[pl.ds(BACK * h + 10 + i, 16, stride=2 * BACK), :] for h in range(2)]
        bins.append(both[0] + both[1])
    first = bins[0] + roll(bins[2], 1, 0)
    for c, part in enumerate((first, roll(bins[0], 64, 1), bins[1], roll(bins[1], 64, 1))):
        totals[pl.ds(c, 16, stride=4), :] = part
    histogram[...] = totals[:, :64].T * scale


def shards(
    density,
    momentum,
    energy,
    eddy_normal_cell,
    eddy_spanwise_cell,
    eddy_signs,
    eddy_strengths,
    filter_matrices,
    shock_switch,
    dilatation_bin,
    vorticity_bin,
):
    slabs, cores = lax.axis_size("gx"), lax.axis_size("gy")
    shapes = (density.shape, eddy_strengths.shape, filter_matrices.shape, slabs, cores)
    if shapes != ((8, 32, 32), (64,), (1, 128, 128), 16, 2):
        return general_shards(
            density,
            momentum,
            energy,
            eddy_normal_cell,
            eddy_spanwise_cell,
            eddy_signs,
            eddy_strengths,
            filter_matrices,
            shock_switch,
            dilatation_bin,
            vorticity_bin,
        )
    cells_x, span, cells_y = density.shape
    total_y = cells_y * cores
    total_eddies = eddy_strengths.shape[0] * slabs
    amplitude = math.sqrt(total_y * span / (total_eddies * SIGMA_Y * SIGMA_Z))
    plane = jax.ShapeDtypeStruct((5, 8, LANES), jnp.float32)
    cells = (8, 8, LANES)
    f32 = lambda *shape: jax.ShapeDtypeStruct(shape, jnp.float32)
    vmem = lambda *shape: pltpu.VMEM(shape, jnp.float32)
    near = lambda a: pltpu.with_memory_space_constraint(a, pltpu.VMEM)
    send, far, pair, edge = pl.pallas_call(
        lambda *refs: slab_kernel(amplitude, *refs),
        out_shape=[vmem(32 * SENT, LANES), vmem(5, 8, LANES), vmem(5, 8, LANES), vmem(*cells)],
        name="slab",
    )(
        density,
        momentum,
        energy,
        eddy_normal_cell.reshape(1, -1),
        eddy_spanwise_cell.reshape(1, -1),
        eddy_signs.T,
        eddy_strengths.reshape(1, -1),
    )
    received = lax.all_to_all(send.reshape(32, SENT, 1, LANES), ("gx", "gy"), 0, 0, tiled=True)
    both = lambda first: [p for i in range(first, slabs - 1, 2) for p in ((i, i + 1), (i + 1, i))]
    far = lax.ppermute(far, "gx", both(1))
    pair = lax.ppermute(pair, "gx", both(0))
    other_edge = lax.ppermute(edge, "gy", [(0, 1), (1, 0)])
    updated, updated_energy, weight, ends, counts, bins, matrix, mask = pl.pallas_call(
        interior_kernel,
        out_shape=[
            vmem(4, *cells),
            vmem(2, 4, 2, 8, LANES),
            vmem(4, *cells),
            vmem(9, 2, 8, LANES),
            vmem(8, 64),
            pltpu.VMEM((2, 2, 8, LANES), jnp.int32),
            pltpu.VMEM((2, *filter_matrices.shape[1:]), jnp.bfloat16),
            vmem(8, LANES),
        ],
        cost_estimate=pl.CostEstimate(flops=10_000_000, bytes_accessed=2_000_000, transcendentals=0),
        name="interior",
    )(
        density,
        momentum,
        energy,
        near(other_edge),
        dilatation_bin,
        vorticity_bin,
        shock_switch,
        filter_matrices[0],
    )
    send, *end_rows = pl.pallas_call(
        pencil_kernel,
        out_shape=[vmem(32 * BACK, LANES)] + [vmem(2, 4, 8, LANES)] * 3,
        scratch_shapes=[pltpu.VMEM((5, 8, LANES), jnp.float32)],
        name="pencil",
    )(
        near(received.reshape(32 * SENT, LANES)),
        *map(near, (matrix, ends, counts, bins, mask, far, pair)),
    )
    received = lax.all_to_all(send.reshape(32, BACK, 1, LANES), ("gx", "gy"), 0, 0, tiled=True)
    scale = HISTOGRAM_BINS * HISTOGRAM_BINS / (cells_x * slabs * span * total_y)
    conserved_next, histogram = pl.pallas_call(
        lambda *refs: final_kernel(scale, *refs),
        out_shape=[f32(5, cells_x, span, cells_y), f32(HISTOGRAM_BINS, HISTOGRAM_BINS)],
        scratch_shapes=[vmem(HISTOGRAM_BINS, LANES)],
        name="final",
    )(
        near(received.reshape(32 * BACK, LANES)),
        *map(near, (updated, updated_energy, weight, *end_rows)),
    )
    return (conserved_next, histogram)


def solution(mesh):
    in_specs = (
        P("gx", None, "gy"),
        P(None, "gx", None, "gy"),
        P("gx", None, "gy"),
        P("gx"),
        P("gx"),
        P("gx", None),
        P("gx"),
        P(),
        P(None, "gy"),
        P("gx", None, "gy"),
        P("gx", None, "gy"),
    )
    out_specs = (P(None, "gx", None, "gy"), P())
    return jax.shard_map(shards, mesh=mesh, in_specs=in_specs, out_specs=out_specs, check_vma=False)
```
